32 devices in a mesh: space: 16 (over z, y, x), rhs: 2 (over core).
Axes of the slice: x: 2, y: 2, z: 4, core: 2. Of those that a mesh axis runs over, the one named last changes fastest.
Arguments:
- positions: float32 [4096, 3, 128], P('space'), may hold values from -0.5 to 0.5
- point_counts: int32 [4096], P('space'), may hold values from 1 to 128
- charges: bfloat16 [4096, 8, 128], P('space', 'rhs'), may hold values from -1.1953125 to 1.1953125
- frequencies: float32 [3, 128], replicated, may hold values from -8 to 8
- octants: int32 [4096], P('space'), may hold values from 0 to 7, as said below
- child_shift: bfloat16 [8, 256, 256], replicated, may hold values from -0.125 to 0.125
- to_wave: bfloat16 [256, 256], replicated, may hold values from -0.375 to 0.375
- to_local: bfloat16 [256, 256], replicated, may hold values from -0.375 to 0.375
- translation: float32 [316, 256], replicated, may hold values from -0.3086067 to 0.3086067
- send_leaf: int32 [16, 8, 48], P('space'), may hold values from 0 to 255
- send_parent: int32 [16, 8, 16], P('space'), may hold values from 0 to 31
- leaf_pairs: int32 [4096, 2, 189], P('space'), may hold values from 0 to 799, as said below
- parent_pairs: int32 [512, 2, 189], P('space'), may hold values from 0 to 799, as said below
Outputs:
- leaf_locals: float32 [4096, 8, 256], P('space', 'rhs')
- parent_locals: float32 [512, 8, 256], P('space', 'rhs')
The draws below stay inside these ranges and needn't reach their ends.
Inputs may be any that keep to these rules, and one draw needn't show every extreme that they name: `octants`: each aligned group of 8 leaves holds every octant 0 to 7 once. `leaf_pairs`: entries [., 0, .] are rows of the device's source table, entries [., 1, .] offset classes below 316. `parent_pairs`: entries [., 0, .] are rows of the device's source table, entries [., 1, .] offset classes below 316.
All inputs are finite; a program needn't handle non-finite values.
Results may differ from the reference program's by a relative error of at most 0.0056.
Values may be sent and summed in bfloat16 or wider, within the bound.
No kernel may reach another device: no remote copies, remote signals or barrier semaphores. Data moves between devices by JAX's collectives and lax.ppermute only.
A program may use at most 128 MiB of HBM per device.

```python
import jax
import jax.numpy as jnp
from jax import lax

K = 256
KH = 128
RHS = 8
SLOTS = 128
LIST = 189
OFFSETS = 316
NEAR = 4
LEAF_DEV = 256
CAP_L = 48
CAP_P = 16
PAR_DEV = 32
LEAVES = 4096
PARENTS = 512
TABLE = 800
N_SPACE = 16


def draw_point_counts(key, part):
    drawn = jax.random.randint(key, (LEAVES,), 1, SLOTS + 1)
    position = jnp.arange(LEAVES) % LEAF_DEV
    drawn = jnp.where(position == 0, SLOTS, drawn)
    drawn = jnp.where(position == 1, 1, drawn)
    return drawn.astype(jnp.int32)


def draw_octants(key, part):
    scores = jax.random.randint(key, (LEAVES,), 0, 1 << 20) * 8 + jnp.arange(LEAVES) % 8
    ordering = jnp.argsort(scores.reshape(-1, 8), axis=1)
    return ordering.reshape(LEAVES).astype(jnp.int32)


def pair_table(key, row_count):
    own_rows = LEAF_DEV + PAR_DEV
    local_rows = jax.random.randint(jax.random.fold_in(key, 11), (row_count, LIST), 0, own_rows)
    remote_rows = jax.random.randint(jax.random.fold_in(key, 13), (row_count, LIST), own_rows, TABLE)
    remote_pick = jax.random.randint(jax.random.fold_in(key, 14), (row_count, LIST), 0, 4) == 0
    source_rows = jnp.where(remote_pick, remote_rows, local_rows)
    offset_rows = jax.random.randint(jax.random.fold_in(key, 12), (row_count, LIST), 0, OFFSETS)
    source_rows = source_rows.at[0, 0].set(TABLE - 1)
    source_rows = source_rows.at[0, 1].set(0)
    offset_rows = offset_rows.at[0, 0].set(OFFSETS - 1)
    offset_rows = offset_rows.at[0, 1].set(0)
    return jnp.stack([source_rows, offset_rows], axis=1).astype(jnp.int32)


def draw_leaf_pairs(key, part):
    return pair_table(jax.random.fold_in(key, 21), LEAVES)


def draw_parent_pairs(key, part):
    return pair_table(jax.random.fold_in(key, 22), PARENTS)


def with_ends(values, own_key, smallest, top_value):
    place = [jax.random.randint(jax.random.fold_in(own_key, axis), (), 0, length) for axis, length in enumerate(values.shape)]
    longest = values.shape.index(max(values.shape))
    beside = place[:longest] + [(place[longest] + 1) % values.shape[longest]] + place[longest + 1:]
    return values.at[tuple(place)].set(smallest).at[tuple(beside)].set(top_value)


def level_of(own_key, extent, pieces, low, high):
    level = 1.0
    for axis_at, parts in pieces:
        draws = jax.random.uniform(jax.random.fold_in(jax.random.fold_in(own_key, 6), axis_at), (parts,), jnp.float32, low / len(pieces), high / len(pieces))
        level = level * jnp.repeat(jnp.exp(draws), extent[axis_at] // parts).reshape((-1,) + (1,) * (len(extent) - 1 - axis_at))
    return level


def centred(rng, dims, deviation, most, shards=(), held_as=jnp.bfloat16):
    values = deviation * jax.random.normal(rng, dims, jnp.float32)
    if shards:
        values = values * level_of(rng, dims, shards, -0.22, 0.18)
    return jnp.clip(values, -most, most).astype(held_as)


def setup_inputs(seed: int = 0) -> dict:
    streams_of = jax.random.split(jax.random.key(seed), 14)
    positions = jnp.clip(jax.random.uniform(streams_of[0], (LEAVES, 3, SLOTS), jnp.float32, -0.5, 0.5) * level_of(streams_of[0], (LEAVES, 3, SLOTS), ((0, 16),), -0.4, 0.0), -0.5, 0.5)
    point_counts = draw_point_counts(jax.random.fold_in(streams_of[13], 71), 0)
    charges = centred(streams_of[2], (LEAVES, RHS, SLOTS), 0.2, 1.1953125, ((0, 16), (1, 2)))
    frequencies = centred(streams_of[3], (3, KH), 2.0, 8.0, (), jnp.float32)
    octants = draw_octants(jax.random.fold_in(streams_of[13], 71), 0)
    child_shift = centred(streams_of[5], (8, K, K), (8 * K) ** -0.5, 0.125)
    to_wave = centred(streams_of[6], (K, K), K ** -0.5, 0.375)
    to_local = centred(streams_of[7], (K, K), K ** -0.5, 0.375)
    translation = centred(streams_of[8], (OFFSETS, K), (1.0 / (2 * LIST) ** 0.5), 0.3086067, (), jnp.float32)
    send_leaf = with_ends(jax.random.randint(streams_of[9], (N_SPACE, 2 * NEAR, CAP_L), 0, LEAF_DEV), jax.random.fold_in(streams_of[9], 1), 0, LEAF_DEV - 1).astype(jnp.int32)
    send_parent = with_ends(jax.random.randint(streams_of[10], (N_SPACE, 2 * NEAR, CAP_P), 0, PAR_DEV), jax.random.fold_in(streams_of[10], 1), 0, PAR_DEV - 1).astype(jnp.int32)
    leaf_pairs = draw_leaf_pairs(jax.random.fold_in(streams_of[13], 71), 0)
    parent_pairs = draw_parent_pairs(jax.random.fold_in(streams_of[13], 71), 0)
    return {"positions": positions, "point_counts": point_counts, "charges": charges, "frequencies": frequencies, "octants": octants, "child_shift": child_shift, "to_wave": to_wave, "to_local": to_local, "translation": translation, "send_leaf": send_leaf, "send_parent": send_parent, "leaf_pairs": leaf_pairs, "parent_pairs": parent_pairs}


def plane_basis(positions, frequencies):
    phase = positions[:, 0, :, None] * frequencies[0] + positions[:, 1, :, None] * frequencies[1] + positions[:, 2, :, None] * frequencies[2]
    return jnp.concatenate([jnp.cos(phase), jnp.sin(phase)], axis=-1).astype(jnp.bfloat16)


def expand(positions, point_counts, charges, frequencies):
    basis = plane_basis(positions, frequencies)
    slot_ids = jnp.arange(charges.shape[2], dtype=jnp.int32)[None, None, :]
    masked = jnp.where(slot_ids < point_counts[:, None, None], charges, jnp.zeros_like(charges))
    product = jnp.einsum("brs,bsk->brk", masked.astype(jnp.float32), basis.astype(jnp.float32))
    return product.astype(jnp.bfloat16)


def upward(multipole, octants, child_shift):
    leaf_count, width_r, width_k = multipole.shape
    children = multipole.reshape(leaf_count // 8, 8, width_r, width_k)
    octant_rows = octants.reshape(leaf_count // 8, 8)
    summed = jnp.zeros((leaf_count // 8 * width_r, child_shift.shape[2]), jnp.float32)
    for octant_id in range(8):
        chosen = jnp.where((octant_rows == octant_id)[:, :, None, None], children, jnp.zeros_like(children))
        chosen = jnp.sum(chosen, axis=1)
        summed = summed + jnp.dot(chosen.reshape(-1, width_k), child_shift[octant_id], preferred_element_type=jnp.float32)
    return summed.reshape(leaf_count // 8, width_r, -1).astype(jnp.bfloat16)


def apply_matrix(values, matrix):
    in_shape = values.shape
    flattened = jnp.dot(values.reshape(-1, in_shape[-1]), matrix, preferred_element_type=jnp.float32)
    return flattened.reshape(in_shape[:-1] + (matrix.shape[1],))


def interact(source_table, pairs, translation, block_size):
    half_width = source_table.shape[-1] // 2

    def one_block(block_pairs):
        picked = source_table[block_pairs[:, 0]].astype(jnp.float32)
        factor = translation[block_pairs[:, 1]][:, :, None, :]
        wave_re = picked[..., :half_width]
        wave_im = picked[..., half_width:]
        factor_re = factor[..., :half_width]
        factor_im = factor[..., half_width:]
        real_part = jnp.sum(factor_re * wave_re - factor_im * wave_im, axis=1)
        imag_part = jnp.sum(factor_re * wave_im + factor_im * wave_re, axis=1)
        return jnp.concatenate([real_part, imag_part], axis=-1).astype(jnp.bfloat16)

    grouped = pairs.reshape((-1, block_size) + pairs.shape[1:])
    result = lax.map(one_block, grouped)
    return result.reshape((pairs.shape[0],) + result.shape[2:])


def reference(positions, point_counts, charges, frequencies, octants, child_shift, to_wave, to_local, translation, send_leaf, send_parent, leaf_pairs, parent_pairs):
    def device_waves(inputs):
        positions_dev, counts_dev, charges_dev, octants_dev = inputs
        multipole = expand(positions_dev, counts_dev, charges_dev, frequencies)
        parent = upward(multipole, octants_dev, child_shift)
        leaf_wave = apply_matrix(multipole, to_wave).astype(jnp.bfloat16)
        parent_wave = apply_matrix(parent, to_wave).astype(jnp.bfloat16)
        return leaf_wave, parent_wave

    leaf_waves, parent_waves = lax.map(device_waves, (
        positions.reshape(N_SPACE, LEAF_DEV, 3, SLOTS),
        point_counts.reshape(N_SPACE, LEAF_DEV),
        charges.reshape(N_SPACE, LEAF_DEV, RHS, SLOTS),
        octants.reshape(N_SPACE, LEAF_DEV)))
    device_ids = jnp.arange(N_SPACE, dtype=jnp.int32)
    offsets = jnp.concatenate([jnp.arange(-NEAR, 0, dtype=jnp.int32), jnp.arange(1, NEAR + 1, dtype=jnp.int32)])
    slot_ids = jnp.arange(2 * NEAR, dtype=jnp.int32)
    all_pairs = jnp.concatenate([leaf_pairs.reshape(N_SPACE, LEAF_DEV, 2, LIST), parent_pairs.reshape(N_SPACE, PAR_DEV, 2, LIST)], axis=1)

    def device_locals(inputs):
        own_index, pairs_dev = inputs
        senders = own_index - offsets
        valid = (senders >= 0) & (senders < N_SPACE)
        safe = jnp.clip(senders, 0, N_SPACE - 1).astype(jnp.int32)
        leaf_ids = send_leaf[safe, slot_ids]
        parent_ids = send_parent[safe, slot_ids]
        received_leaf = leaf_waves[safe[:, None], leaf_ids]
        received_parent = parent_waves[safe[:, None], parent_ids]
        received_leaf = jnp.where(valid[:, None, None, None], received_leaf, jnp.zeros_like(received_leaf)).reshape(-1, RHS, K)
        received_parent = jnp.where(valid[:, None, None, None], received_parent, jnp.zeros_like(received_parent)).reshape(-1, RHS, K)
        source_table = jnp.concatenate([leaf_waves[own_index], parent_waves[own_index], received_leaf, received_parent], axis=0)
        incoming = interact(source_table, pairs_dev, translation, PAR_DEV)
        return apply_matrix(incoming, to_local)

    local_all = lax.map(device_locals, (device_ids, all_pairs))
    leaf_locals = local_all[:, :LEAF_DEV].reshape(LEAVES, RHS, K)
    parent_locals = local_all[:, LEAF_DEV:].reshape(PARENTS, RHS, K)
    return (leaf_locals, parent_locals)
```

```python
import functools
import math

import jax
import jax.numpy as jnp
from jax import lax
from jax.experimental import pallas as pl
from jax.experimental.pallas import tpu as pltpu
from jax.sharding import PartitionSpec as P

F32 = jnp.float32
BF16 = jnp.bfloat16
CHUNK = 63
GROUP = 9
SIN_POLY = (4.44286790342698, -7.307443431653506, 3.594788153158899, -0.7843741906863176)
COS_POLY = (
    1.4142134967586113,
    -6.978850998632011,
    5.7394613208713325,
    -1.883563790130787,
    0.31069962133630835,
)

VMEM = pl.BlockSpec(memory_space=pltpu.VMEM)
SMEM = pl.BlockSpec(memory_space=pltpu.SMEM)


def swap_cores(value):
    return lax.ppermute(value, "rhs", [(0, 1), (1, 0)])


def horner(coefficients, x):
    total = coefficients[-1] * x + coefficients[-2]
    for coefficient in coefficients[-3::-1]:
        total = total * x + coefficient
    return total


def tree(values):
    values = list(values)
    while len(values) > 1:
        paired = [values[i] + values[i + 1] for i in range(0, len(values) - 1, 2)]
        values = paired + values[2 * len(paired) :]
    return values[0]


def sin_cos_turns(turns):
    r = turns - jnp.round(turns)
    r2 = r * r
    s = r * horner(SIN_POLY, r2)
    c = horner(COS_POLY, r2)
    return s * c, 1.0 - s * s


def upward_kernel(
    core_ref, counts_ref, octants_ref, freq_ref, pos_ref, own_ref, recv_ref, shift_ref, wave_mat_ref,
    out_ref, freq_scr, mult_scr, child_scr,
):
    core = core_ref[0]
    leaves, slots = pos_ref.shape[0], pos_ref.shape[2]
    nodes = freq_ref.shape[1]
    for d in range(3):
        row = freq_ref[d : d + 1, :] * (1.0 / (2.0 * math.pi))
        freq_scr[d] = jnp.broadcast_to(row, (slots, nodes)).T
    lane = lax.broadcasted_iota(jnp.int32, (2 * own_ref.shape[1], slots), 1)

    def one_leaf(b, carry):
        lo = jnp.where(core == 0, own_ref[b].astype(F32), recv_ref[b].astype(F32))
        hi = jnp.where(core == 0, recv_ref[b].astype(F32), own_ref[b].astype(F32))
        charge = jnp.concatenate([lo, hi], axis=0)
        charge = jnp.where(lane < counts_ref[b], charge, 0.0).astype(BF16)
        xs = [jnp.broadcast_to(pos_ref[b, d : d + 1, :], (nodes, slots)) for d in range(3)]
        turns = freq_scr[0] * xs[0] + freq_scr[1] * xs[1] + freq_scr[2] * xs[2]
        sin, cos = sin_cos_turns(turns)
        basis = jnp.concatenate([cos.astype(BF16), sin.astype(BF16)], axis=0)
        multipole = lax.dot_general(
            charge, basis, (((1,), (1,)), ((), ())), preferred_element_type=F32
        ).astype(BF16)
        mult_scr[b] = multipole
        child_scr[octants_ref[b], b // 8] = multipole
        return carry

    lax.fori_loop(0, leaves, one_leaf, 0)
    parents = leaves // 8
    rhs, width = mult_scr.shape[1:]
    wave_mat = wave_mat_ref[...]
    multipoles = mult_scr[...].reshape(leaves * rhs, width)
    waves = jnp.dot(multipoles, wave_mat, preferred_element_type=F32).astype(BF16)
    out_ref[:leaves] = waves.reshape(leaves, rhs, width)
    summed = None
    for octant in range(8):
        part = jnp.dot(
            child_scr[octant].reshape(parents * rhs, width),
            shift_ref[octant],
            preferred_element_type=F32,
        )
        summed = part if summed is None else summed + part
    parent_waves = jnp.dot(summed.astype(BF16), wave_mat, preferred_element_type=F32)
    out_ref[leaves:] = parent_waves.astype(BF16).reshape(parents, rhs, width)


def pack_kernel(leaf_ids_ref, parent_ids_ref, own_ref, recv_ref, *refs):
    outs, scr = refs[:-1], refs[-1]
    held = own_ref.shape[0]
    scr[:held] = own_ref[...]
    scr[held:] = recv_ref[...]
    cap_l, cap_p = leaf_ids_ref.shape[1], parent_ids_ref.shape[1]
    for j, out in enumerate(outs):
        for k in range(cap_l):
            out[k] = scr[leaf_ids_ref[j, k]]
        for k in range(cap_p):
            out[cap_l + k] = scr[parent_ids_ref[j, k]]


def interact_kernel(dims, info_ref, source_ref, class_ref, *refs):
    leaves, parents, slots, cap_l, cap_p, list_len, stride = dims
    own_ref, recv_ref = refs[:2]
    near_own = refs[2 : 2 + slots]
    near_recv = refs[2 + slots : 2 + 2 * slots]
    trans_ref, keep_ref, send_ref, table, factor = refs[2 + 2 * slots :]
    core = info_ref[0]
    other = 1 - core
    half = keep_ref.shape[2] // 2
    rows = 16

    def put(source, at, count, base, valid=None):
        def body(k, carry):
            value = source[at + k].astype(F32)
            if valid is not None:
                value = jnp.where(valid > 0, value, 0.0)
            row = pl.multiple_of((base + k) * rows, rows)
            table[pl.ds(row, 8), :] = value[:, :half]
            table[pl.ds(pl.multiple_of(row + 8, 8), 8), :] = value[:, half:]
            return carry

        lax.fori_loop(0, count, body, 0, unroll=8)

    for values, which in ((own_ref, core), (recv_ref, other)):
        put(values, 0, leaves, which * leaves)
        put(values, leaves, parents, 2 * leaves + which * parents)
    base = 2 * (leaves + parents)
    for j in range(slots):
        for values, which in ((near_own[j], core), (near_recv[j], other)):
            valid = info_ref[1 + j]
            put(values, 0, cap_l, base + (2 * j + which) * cap_l, valid)
            put(values, cap_l, cap_p, base + 2 * slots * cap_l + (2 * j + which) * cap_p, valid)

    def put_factors(first, values):
        for k in range(values.shape[0]):
            row = pl.multiple_of((first + k) * rows, rows)
            factor[pl.ds(row, 8), :] = jnp.broadcast_to(values[k : k + 1, :half], (8, half))
            factor[pl.ds(pl.multiple_of(row + 8, 8), 8), :] = jnp.broadcast_to(
                values[k : k + 1, half:], (8, half)
            )

    def factor_block(g, carry):
        first = pl.multiple_of(g * 8, 8)
        put_factors(first, trans_ref[pl.ds(first, 8), :])
        return carry

    classes_full = trans_ref.shape[0] // 8 * 8
    lax.fori_loop(0, classes_full // 8, factor_block, 0)
    if classes_full < trans_ref.shape[0]:
        put_factors(classes_full, trans_ref[classes_full:, :])

    def accumulate(first, count, total):
        total_re, total_im = total
        reals, imags = [], []
        for k in range(count):
            if k % GROUP == 0:
                span = min(GROUP, count - k)
                sources = source_ref.at[pl.ds(first + k, span)]
                classes = class_ref.at[pl.ds(first + k, span)]
            s = pl.multiple_of(sources[k % GROUP], 8)
            o = pl.multiple_of(classes[k % GROUP], 8)
            wave = table.at[pl.ds(s, rows)]
            shift = factor.at[pl.ds(o, rows)]
            wave_re, wave_im, shift_re, shift_im = wave[:8], wave[8:], shift[:8], shift[8:]
            reals.append(shift_re * wave_re - shift_im * wave_im)
            imags.append(shift_re * wave_im + shift_im * wave_re)
            if len(reals) == 3 or k == count - 1:
                total_re, total_im = total_re + tree(reals), total_im + tree(imags)
                reals, imags = [], []
        return total_re, total_im

    def one_target(b, carry):
        zero = jnp.zeros((8, half), F32)
        start = b * stride
        total = lax.fori_loop(
            0,
            list_len // CHUNK,
            lambda c, t: accumulate(start + c * CHUNK, CHUNK, t),
            (zero, zero),
        )
        if list_len % CHUNK:
            total = accumulate(start + list_len - list_len % CHUNK, list_len % CHUNK, total)
        incoming = jnp.concatenate(total, axis=1)
        lower, upper = incoming[:4], incoming[4:]
        keep_ref[b] = jnp.where(core == 0, lower, upper).astype(BF16)
        send_ref[b] = jnp.where(core == 0, upper, lower).astype(BF16)
        return carry

    lax.fori_loop(0, keep_ref.shape[0], one_target, 0)


def local_kernel(leaves, core_ref, keep_ref, recv_ref, mat_ref, leaf_ref, parent_ref):
    core = core_ref[0]
    parents = keep_ref.shape[0] - leaves
    rhs, width = keep_ref.shape[1:]
    for values, which in ((keep_ref, core), (recv_ref, 1 - core)):
        flat = values[...].reshape((leaves + parents) * rhs, width)
        local = jnp.dot(flat, mat_ref[...], preferred_element_type=F32)
        local = local.reshape(leaves + parents, rhs, width)
        leaf_ref[pl.ds(which * leaves, leaves)] = local[:leaves]
        parent_ref[pl.ds(which * parents, parents)] = local[leaves:]


def shards(
    positions, point_counts, charges, frequencies, octants, child_shift, to_wave, to_local,
    translation, send_leaf, send_parent, leaf_pairs, parent_pairs,
):
    core = lax.axis_index("rhs")
    other = 1 - core
    device = lax.axis_index("space")
    count = lax.axis_size("space")
    leaves = positions.shape[0] // 2
    parents = leaves // 8
    rhs = charges.shape[1]
    width = to_wave.shape[0]
    slots = send_leaf.shape[1]
    near = slots // 2
    held = leaves + parents
    core_arr = core.reshape(1)

    def half_of(value, which):
        size = value.shape[0] // 2
        return lax.dynamic_slice_in_dim(value, which * size, size, 0)

    arrived_charges = swap_cores(half_of(charges, other))
    waves = pl.pallas_call(
        upward_kernel,
        out_shape=jax.ShapeDtypeStruct((held, 2 * rhs, width), BF16),
        in_specs=[SMEM] * 3 + [VMEM] * 6,
        out_specs=VMEM,
        scratch_shapes=[
            pltpu.VMEM((3, width // 2, positions.shape[2]), F32),
            pltpu.VMEM((leaves, 2 * rhs, width), BF16),
            pltpu.VMEM((8, parents, 2 * rhs, width), BF16),
        ],
        name="upward",
    )(
        core_arr,
        half_of(point_counts, core),
        half_of(octants, core),
        frequencies,
        half_of(positions, core),
        half_of(charges, core),
        arrived_charges,
        child_shift,
        to_wave,
    )
    arrived_waves = swap_cores(waves)

    cap_l, cap_p = send_leaf.shape[2] // 2, send_parent.shape[2] // 2
    leaf_ids = lax.dynamic_slice_in_dim(send_leaf[0], core * cap_l, cap_l, 1)
    parent_ids = lax.dynamic_slice_in_dim(send_parent[0], core * cap_p, cap_p, 1)
    leaf_rows = jnp.where(leaf_ids // leaves == core, 0, held) + leaf_ids % leaves
    parent_rows = jnp.where(parent_ids // parents == core, 0, held) + leaves + parent_ids % parents
    sent = pl.pallas_call(
        pack_kernel,
        out_shape=[jax.ShapeDtypeStruct((cap_l + cap_p, 2 * rhs, width), BF16)] * slots,
        in_specs=[SMEM] * 2 + [VMEM] * 2,
        out_specs=[VMEM] * slots,
        scratch_shapes=[pltpu.VMEM((2 * held, 2 * rhs, width), BF16)],
        name="pack",
    )(leaf_rows, parent_rows, waves, arrived_waves)
    offsets = [j - near if j < near else j - near + 1 for j in range(slots)]
    near_own = [
        lax.ppermute(part, "space", [(e, (e + o) % count) for e in range(count)])
        for part, o in zip(sent, offsets)
    ]
    near_recv = [swap_cores(part) for part in near_own]

    list_len = leaf_pairs.shape[2]
    stride = -(-list_len // 64) * 64
    targets = jnp.concatenate([half_of(leaf_pairs, core), half_of(parent_pairs, core)], axis=0)
    targets = jnp.pad(targets * 16, ((0, 0), (0, 0), (0, stride - list_len)))
    source_rows = targets[:, 0].reshape(-1)
    class_rows = targets[:, 1].reshape(-1)
    senders = device - jnp.array(offsets, jnp.int32)
    valid = ((senders >= 0) & (senders < count)).astype(jnp.int32)
    info = jnp.concatenate([core_arr, valid])
    dims = (leaves, parents, slots, cap_l, cap_p, list_len, stride)
    table_rows = 2 * held + 2 * slots * (cap_l + cap_p)
    keep, send = pl.pallas_call(
        functools.partial(interact_kernel, dims),
        out_shape=[jax.ShapeDtypeStruct((held, rhs, width), BF16)] * 2,
        in_specs=[SMEM] * 3 + [VMEM] * (3 + 2 * slots),
        out_specs=[VMEM] * 2,
        scratch_shapes=[
            pltpu.VMEM((table_rows * 16, width // 2), F32),
            pltpu.VMEM((translation.shape[0] * 16, width // 2), F32),
        ],
        name="interact",
    )(info, source_rows, class_rows, waves, arrived_waves, *near_own, *near_recv, translation)
    arrived = swap_cores(send)
    return tuple(
        pl.pallas_call(
            functools.partial(local_kernel, leaves),
            out_shape=[
                jax.ShapeDtypeStruct((2 * leaves, rhs, width), F32),
                jax.ShapeDtypeStruct((2 * parents, rhs, width), F32),
            ],
            in_specs=[SMEM] + [VMEM] * 3,
            out_specs=[VMEM] * 2,
            name="local",
        )(core_arr, keep, arrived, to_local)
    )


def solution(mesh):
    in_specs = (
        P("space", None, None), P("space"), P("space", "rhs", None), P(), P("space"), P(), P(), P(),
        P(), P("space", None, None), P("space", None, None), P("space", None, None),
        P("space", None, None),
    )
    out_specs = (P("space", "rhs", None), P("space", "rhs", None))
    return jax.shard_map(shards, mesh=mesh, in_specs=in_specs, out_specs=out_specs, check_vma=False)
```

```python
import functools
import math

import jax
import jax.numpy as jnp
from jax import lax
from jax.experimental import pallas as pl
from jax.experimental.pallas import tpu as pltpu
from jax.sharding import PartitionSpec as P

F32 = jnp.float32
BF16 = jnp.bfloat16
CHUNKS = 3
GROUP = 9
LEAF_UNROLL = 8
SIN_POLY = (4.44286790342698, -7.307443431653506, 3.594788153158899, -0.7843741906863176)
COS_POLY = (
    1.4142134967586113,
    -6.978850998632011,
    5.7394613208713325,
    -1.883563790130787,
    0.31069962133630835,
)

VMEM = pl.BlockSpec(memory_space=pltpu.VMEM)
SMEM = pl.BlockSpec(memory_space=pltpu.SMEM)


def swap_cores(value):
    return lax.ppermute(value, "rhs", [(0, 1), (1, 0)])


def horner(coefficients, x):
    total = coefficients[-1] * x + coefficients[-2]
    for coefficient in coefficients[-3::-1]:
        total = total * x + coefficient
    return total


def tree(values):
    values = list(values)
    while len(values) > 1:
        paired = [values[i] + values[i + 1] for i in range(0, len(values) - 1, 2)]
        values = paired + values[2 * len(paired) :]
    return values[0]


def sin_cos_turns(turns):
    r = turns - jnp.round(turns)
    r2 = r * r
    s = r * horner(SIN_POLY, r2)
    c = horner(COS_POLY, r2)
    return s * c, 1.0 - s * s


def upward_kernel(
    counts_ref, octants_ref, freq_ref, pos_ref, own_ref, recv_ref, shift_ref, wave_mat_ref,
    out_ref, freq_scr, mult_scr, child_scr,
):
    core = lax.axis_index("rhs")
    leaves, rhs_half, slots = recv_ref.shape
    nodes = freq_ref.shape[1]
    base = core * leaves
    for d in range(3):
        row = freq_ref[d : d + 1, :] * (1.0 / (2.0 * math.pi))
        freq_scr[d] = jnp.broadcast_to(row, (slots, nodes)).T
    lane = lax.broadcasted_iota(jnp.int32, (2 * rhs_half, slots), 1)

    def one_leaf(b):
        own, recv = own_ref[base + b].astype(F32), recv_ref[b].astype(F32)
        lower = jnp.where(core == 0, own, recv)
        upper = jnp.where(core == 0, recv, own)
        charge = jnp.concatenate([lower, upper], axis=0)
        charge = jnp.where(lane < counts_ref[base + b], charge, 0.0).astype(BF16)
        xs = [jnp.broadcast_to(pos_ref[d, pl.ds(base + b, 1), :], (nodes, slots)) for d in range(3)]
        turns = freq_scr[0] * xs[0] + freq_scr[1] * xs[1] + freq_scr[2] * xs[2]
        sin, cos = sin_cos_turns(turns)
        basis = jnp.concatenate([cos.astype(BF16), sin.astype(BF16)], axis=0)
        multipole = lax.dot_general(
            charge, basis, (((1,), (1,)), ((), ())), preferred_element_type=F32
        ).astype(BF16)
        mult_scr[b] = multipole
        child_scr[octants_ref[base + b], b // 8] = multipole

    def step(g, carry):
        for k in range(LEAF_UNROLL):
            one_leaf(g * LEAF_UNROLL + k)
        return carry

    lax.fori_loop(0, leaves // LEAF_UNROLL, step, 0)
    parents = leaves // 8
    rhs, width = mult_scr.shape[1:]
    wave_mat = wave_mat_ref[...]
    multipoles = mult_scr[...].reshape(leaves * rhs, width)
    waves = jnp.dot(multipoles, wave_mat, preferred_element_type=F32).astype(BF16)
    out_ref[:leaves] = waves.reshape(leaves, rhs, width)
    summed = None
    for octant in range(8):
        part = jnp.dot(
            child_scr[octant].reshape(parents * rhs, width),
            shift_ref[octant],
            preferred_element_type=F32,
        )
        summed = part if summed is None else summed + part
    parent_waves = jnp.dot(summed.astype(BF16), wave_mat, preferred_element_type=F32)
    out_ref[leaves:] = parent_waves.astype(BF16).reshape(parents, rhs, width)


def plan_kernel(local_rows, chunk, leaf_ref, parent_ref, source_out, class_out, chunks_out):
    core = lax.axis_index("rhs")
    list_len = leaf_ref.shape[0]
    targets = source_out.shape[0] // 2
    parents = parent_ref.shape[0] // 2
    leaves = targets - parents
    depth = -(-list_len // 8) * 8

    def packed(source, shift):
        return source + shift * (1 << 10)

    lanes = pl.ds(pl.multiple_of(core * leaves, leaves), leaves)
    leaf_words = packed(leaf_ref[:, 0, lanes], leaf_ref[:, 1, lanes])
    rows = pl.ds(core * parents, parents)
    parent_words = packed(parent_ref[rows, 0, :], parent_ref[rows, 1, :])
    parent_words = jnp.concatenate(
        [parent_words, jnp.zeros((parents, 256 - list_len), jnp.int32)], axis=1
    )
    parent_words = jnp.concatenate(
        [parent_words, jnp.zeros((128 - parents, 256), jnp.int32)], axis=0
    ).T[:depth]
    leaf_words = jnp.concatenate(
        [leaf_words, jnp.zeros((depth - list_len, leaves), jnp.int32)], axis=0
    )
    words = jnp.concatenate([leaf_words, parent_words], axis=1)
    row = lax.broadcasted_iota(jnp.int32, words.shape, 0)
    local = ((words & 1023) < local_rows) & (row < list_len)
    below = lax.broadcasted_iota(jnp.int32, (depth, depth), 0) >= lax.broadcasted_iota(
        jnp.int32, (depth, depth), 1
    )
    running = jnp.dot(
        jnp.where(below, 1.0, 0.0).astype(BF16),
        jnp.where(local, 1.0, 0.0).astype(BF16),
        preferred_element_type=F32,
    ).astype(jnp.int32)
    total = running[depth - 1 :]
    front = jnp.where(local, words + (row + 1 - running) * (1 << 20), 0)
    back = jnp.where(local, 0, words + (total - running) * (1 << 20))
    for k in range(8):
        bit = 1 << (20 + k)
        step = 1 << k
        moved = pltpu.roll(front, depth - step, 0)
        front = jnp.where((moved & bit) != 0, moved, jnp.where((front & bit) != 0, 0, front))
        moved = pltpu.roll(back, step, 0)
        back = jnp.where((moved & bit) != 0, moved, jnp.where((back & bit) != 0, 0, back))
    words = front + back
    for out, values in (
        (source_out, (words & 1023) * 16),
        (class_out, (lax.shift_right_logical(words, 10) & 1023) * 16),
    ):
        out[:targets] = values[:128].T[:targets]
        out[targets:] = pltpu.roll(values, depth - 2 * chunk, 0)[:128].T[:targets]
    full = [(total >= n * chunk).astype(jnp.int32) for n in range(1, list_len // chunk + 1)]
    chunks_out[...] = tree(full)


def pack_kernel(leaf_ids_ref, parent_ids_ref, own_ref, recv_ref, *refs):
    core = lax.axis_index("rhs")
    rows_ref, outs = refs[0], refs[1:]
    cap_l, cap_p = leaf_ids_ref.shape[1] // 2, parent_ids_ref.shape[1] // 2
    parents = rows_ref.shape[0] // 18
    leaves = 8 * parents
    for values, which in ((own_ref, core), (recv_ref, 1 - core)):
        rows_ref[pl.ds(which * leaves, leaves)] = values[:leaves]
        rows_ref[pl.ds(2 * leaves + which * parents, parents)] = values[leaves:]
    for j, out in enumerate(outs):
        for k in range(cap_l):
            out[k] = rows_ref[leaf_ids_ref[j, core * cap_l + k]]
        for k in range(cap_p):
            out[cap_l + k] = rows_ref[2 * leaves + parent_ids_ref[j, core * cap_p + k]]


def put_rows(table, source, at, count, base, valid=None):
    half = table.shape[1]

    def body(k, carry):
        value = source[at + k].astype(F32)
        if valid is not None:
            value = jnp.where(valid, value, 0.0)
        row = pl.multiple_of((base + k) * 16, 16)
        table[pl.ds(row, 8), :] = value[:, :half]
        table[pl.ds(pl.multiple_of(row + 8, 8), 8), :] = value[:, half:]
        return carry

    lax.fori_loop(0, count, body, 0, unroll=8)


def put_all_factors(factor, trans_ref):
    half = factor.shape[1]

    def put_factors(first, values):
        for k in range(values.shape[0]):
            row = pl.multiple_of((first + k) * 16, 16)
            factor[pl.ds(row, 8), :] = jnp.broadcast_to(values[k : k + 1, :half], (8, half))
            factor[pl.ds(pl.multiple_of(row + 8, 8), 8), :] = jnp.broadcast_to(
                values[k : k + 1, half:], (8, half)
            )

    def factor_block(g, carry):
        first = pl.multiple_of(g * 8, 8)
        put_factors(first, trans_ref[pl.ds(first, 8), :])
        return carry

    full = trans_ref.shape[0] // 8 * 8
    lax.fori_loop(0, full // 8, factor_block, 0)
    if full < trans_ref.shape[0]:
        put_factors(full, trans_ref[full:, :])


def pair_sums(source_ref, class_ref, table, factor, chunk, targets):
    def accumulate(b, c, total):
        total_re, total_im = total
        first = b * 128 + jnp.where(c == 2, targets * 128, c * chunk)
        reals, imags = [], []
        for k in range(chunk):
            if k % GROUP == 0:
                span = min(GROUP, chunk - k)
                sources = source_ref.at[pl.ds(first + k, span)]
                classes = class_ref.at[pl.ds(first + k, span)]
            s = pl.multiple_of(sources[k % GROUP], 8)
            o = pl.multiple_of(classes[k % GROUP], 8)
            wave, shift = table.at[pl.ds(s, 16)], factor.at[pl.ds(o, 16)]
            wave_re, wave_im, shift_re, shift_im = wave[:8], wave[8:], shift[:8], shift[8:]
            reals.append(shift_re * wave_re - shift_im * wave_im)
            imags.append(shift_re * wave_im + shift_im * wave_re)
            if len(reals) == 3 or k == chunk - 1:
                total_re, total_im = total_re + tree(reals), total_im + tree(imags)
                reals, imags = [], []
        return total_re, total_im

    return accumulate


def near_kernel(chunk, chunks_ref, source_ref, class_ref, rows_ref, trans_ref, acc_ref, table, factor):
    put_rows(table, rows_ref, 0, rows_ref.shape[0], 0)
    put_all_factors(factor, trans_ref)
    targets = acc_ref.shape[0]
    accumulate = pair_sums(source_ref, class_ref, table, factor, chunk, targets)

    def one_target(b, carry):
        zero = jnp.zeros((8, table.shape[1]), F32)
        total = lax.fori_loop(
            0, chunks_ref[0, b], lambda c, t: accumulate(b, c, t), (zero, zero)
        )
        acc_ref[b, :8] = total[0]
        acc_ref[b, 8:] = total[1]
        return carry

    lax.fori_loop(0, targets, one_target, 0)


def rest_kernel(dims, chunks_ref, source_ref, class_ref, rows_ref, *refs):
    slots, cap_l, cap_p, chunk, chunk_count, count = dims
    near_own, near_recv = refs[:slots], refs[slots : 2 * slots]
    trans_ref, acc_ref, keep_ref, send_ref, table, factor = refs[2 * slots :]
    core = lax.axis_index("rhs")
    device = lax.axis_index("space")
    put_rows(table, rows_ref, 0, rows_ref.shape[0], 0)
    base = rows_ref.shape[0]
    for j in range(slots):
        sender = device - (j - slots // 2 if j < slots // 2 else j - slots // 2 + 1)
        valid = (sender >= 0) & (sender < count)
        for values, which in ((near_own[j], core), (near_recv[j], 1 - core)):
            put_rows(table, values, 0, cap_l, base + (2 * j + which) * cap_l, valid)
            parent_base = base + 2 * slots * cap_l + (2 * j + which) * cap_p
            put_rows(table, values, cap_l, cap_p, parent_base, valid)
    put_all_factors(factor, trans_ref)
    targets = acc_ref.shape[0]
    accumulate = pair_sums(source_ref, class_ref, table, factor, chunk, targets)

    def one_target(b, carry):
        total = lax.fori_loop(
            chunks_ref[0, b],
            chunk_count,
            lambda c, t: accumulate(b, c, t),
            (acc_ref[b, :8], acc_ref[b, 8:]),
        )
        incoming = jnp.concatenate(total, axis=1)
        lower, upper = incoming[:4], incoming[4:]
        keep_ref[b] = jnp.where(core == 0, lower, upper).astype(BF16)
        send_ref[b] = jnp.where(core == 0, upper, lower).astype(BF16)
        return carry

    lax.fori_loop(0, targets, one_target, 0)


def local_kernel(leaves, keep_ref, recv_ref, mat_ref, leaf_ref, parent_ref):
    core = lax.axis_index("rhs")
    parents = keep_ref.shape[0] - leaves
    rhs, width = keep_ref.shape[1:]
    for values, which in ((keep_ref, core), (recv_ref, 1 - core)):
        flat = values[...].reshape((leaves + parents) * rhs, width)
        local = jnp.dot(flat, mat_ref[...], preferred_element_type=F32)
        local = local.reshape(leaves + parents, rhs, width)
        leaf_ref[pl.ds(which * leaves, leaves)] = local[:leaves]
        parent_ref[pl.ds(which * parents, parents)] = local[leaves:]


def shards(
    positions, point_counts, charges, frequencies, octants, child_shift, to_wave, to_local,
    translation, send_leaf, send_parent, leaf_pairs, parent_pairs,
):
    other = 1 - lax.axis_index("rhs")
    count = lax.axis_size("space")
    leaves = positions.shape[0] // 2
    parents = leaves // 8
    rhs = charges.shape[1]
    width = to_wave.shape[0]
    slots = send_leaf.shape[1]
    near = slots // 2
    held = leaves + parents
    list_len = leaf_pairs.shape[2]
    chunk = list_len // CHUNKS
    cap_l, cap_p = send_leaf.shape[2] // 2, send_parent.shape[2] // 2
    table_rows = 2 * held + 2 * slots * (cap_l + cap_p)

    arrived_charges = swap_cores(lax.dynamic_slice_in_dim(charges, other * leaves, leaves, 0))
    index_shape = jax.ShapeDtypeStruct((2 * held, 128), jnp.int32)
    source_rows, class_rows, chunks = pl.pallas_call(
        functools.partial(plan_kernel, 2 * held, chunk),
        out_shape=[index_shape, index_shape, jax.ShapeDtypeStruct((1, 256), jnp.int32)],
        in_specs=[VMEM] * 2,
        out_specs=[VMEM] * 3,
        name="plan",
    )(jnp.transpose(leaf_pairs, (2, 1, 0)), parent_pairs)
    arrived_charges, source_rows, class_rows, chunks = lax.optimization_barrier(
        (arrived_charges, source_rows, class_rows, chunks)
    )
    source_rows, class_rows = source_rows.reshape(-1), class_rows.reshape(-1)
    waves = pl.pallas_call(
        upward_kernel,
        out_shape=jax.ShapeDtypeStruct((held, 2 * rhs, width), BF16),
        in_specs=[SMEM] * 2 + [VMEM] * 6,
        out_specs=VMEM,
        scratch_shapes=[
            pltpu.VMEM((3, width // 2, positions.shape[2]), F32),
            pltpu.VMEM((leaves, 2 * rhs, width), BF16),
            pltpu.VMEM((8, parents, 2 * rhs, width), BF16),
        ],
        name="upward",
    )(
        point_counts, octants, frequencies, jnp.transpose(positions, (1, 0, 2)), charges,
        arrived_charges, child_shift, to_wave,
    )
    arrived_waves = swap_cores(waves)
    rows, *sent = pl.pallas_call(
        pack_kernel,
        out_shape=[jax.ShapeDtypeStruct((2 * held, 2 * rhs, width), BF16)]
        + [jax.ShapeDtypeStruct((cap_l + cap_p, 2 * rhs, width), BF16)] * slots,
        in_specs=[SMEM] * 2 + [VMEM] * 2,
        out_specs=[VMEM] * (1 + slots),
        name="pack",
    )(send_leaf[0], send_parent[0], waves, arrived_waves)
    offsets = [j - near if j < near else j - near + 1 for j in range(slots)]
    near_own = [
        lax.ppermute(part, "space", [(e, (e + o) % count) for e in range(count)])
        for part, o in zip(sent, offsets)
    ]
    factor_scr = pltpu.VMEM((translation.shape[0] * 16, width // 2), F32)
    acc_shape = jax.ShapeDtypeStruct((held, 16, width // 2), F32)
    acc = pl.pallas_call(
        functools.partial(near_kernel, chunk),
        out_shape=acc_shape,
        in_specs=[SMEM] * 3 + [VMEM] * 2,
        out_specs=VMEM,
        scratch_shapes=[pltpu.VMEM((2 * held * 16, width // 2), F32), factor_scr],
        cost_estimate=pl.CostEstimate(flops=25_000_000_000, bytes_accessed=80_000_000, transcendentals=0),
        name="near",
    )(chunks, source_rows, class_rows, rows, translation)
    near_recv = [swap_cores(part) for part in near_own]
    keep, send = pl.pallas_call(
        functools.partial(rest_kernel, (slots, cap_l, cap_p, chunk, CHUNKS, count)),
        out_shape=[jax.ShapeDtypeStruct((held, rhs, width), BF16)] * 2,
        in_specs=[SMEM] * 3 + [VMEM] * (3 + 2 * slots),
        out_specs=[VMEM] * 2,
        scratch_shapes=[pltpu.VMEM((table_rows * 16, width // 2), F32), factor_scr],
        name="rest",
    )(chunks, source_rows, class_rows, rows, *near_own, *near_recv, translation, acc)
    arrived = swap_cores(send)
    return tuple(
        pl.pallas_call(
            functools.partial(local_kernel, leaves),
            out_shape=[
                jax.ShapeDtypeStruct((2 * leaves, rhs, width), F32),
                jax.ShapeDtypeStruct((2 * parents, rhs, width), F32),
            ],
            in_specs=[VMEM] * 3,
            out_specs=[VMEM] * 2,
            name="local",
        )(keep, arrived, to_local)
    )


def solution(mesh):
    in_specs = (
        P("space", None, None), P("space"), P("space", "rhs", None), P(), P("space"), P(), P(), P(),
        P(), P("space", None, None), P("space", None, None), P("space", None, None),
        P("space", None, None),
    )
    out_specs = (P("space", "rhs", None), P("space", "rhs", None))
    return jax.shard_map(shards, mesh=mesh, in_specs=in_specs, out_specs=out_specs, check_vma=False)
```

```python
import functools
import math

import jax
import jax.numpy as jnp
from jax import lax
from jax.experimental import pallas as pl
from jax.experimental.pallas import tpu as pltpu
from jax.sharding import PartitionSpec as P

F32 = jnp.float32
BF16 = jnp.bfloat16
CHUNKS = 3
GROUP = 9
LEAF_UNROLL = 8
TARGET_GROUP = 16
SIN_POLY = (4.44286790342698, -7.307443431653506, 3.594788153158899, -0.7843741906863176)
COS_POLY = (
    1.4142134967586113,
    -6.978850998632011,
    5.7394613208713325,
    -1.883563790130787,
    0.31069962133630835,
)

VMEM = pl.BlockSpec(memory_space=pltpu.VMEM)
SMEM = pl.BlockSpec(memory_space=pltpu.SMEM)
ANY = pl.BlockSpec(memory_space=pl.ANY)


def swap_cores(value):
    return lax.ppermute(value, "rhs", [(0, 1), (1, 0)])


def horner(coefficients, x):
    total = coefficients[-1] * x + coefficients[-2]
    for coefficient in coefficients[-3::-1]:
        total = total * x + coefficient
    return total


def tree(values):
    values = list(values)
    while len(values) > 1:
        paired = [values[i] + values[i + 1] for i in range(0, len(values) - 1, 2)]
        values = paired + values[2 * len(paired) :]
    return values[0]


def sin_cos_turns(turns):
    r = turns - jnp.round(turns)
    r2 = r * r
    s = r * horner(SIN_POLY, r2)
    c = horner(COS_POLY, r2)
    return s * c, 1.0 - s * s


def upward_kernel(
    counts_ref, octants_ref, freq_ref, pos_ref, own_ref, recv_ref, shift_ref, wave_mat_ref,
    out_ref, freq_scr, mult_scr, child_scr,
):
    core = lax.axis_index("rhs")
    leaves, rhs_half, slots = recv_ref.shape
    nodes = freq_ref.shape[1]
    base = core * leaves
    for d in range(3):
        row = freq_ref[d : d + 1, :] * (1.0 / (2.0 * math.pi))
        freq_scr[d] = jnp.broadcast_to(row, (slots, nodes)).T
    lane = lax.broadcasted_iota(jnp.int32, (2 * rhs_half, slots), 1)

    def one_leaf(b):
        own, recv = own_ref[base + b].astype(F32), recv_ref[b].astype(F32)
        lower = jnp.where(core == 0, own, recv)
        upper = jnp.where(core == 0, recv, own)
        charge = jnp.concatenate([lower, upper], axis=0)
        charge = jnp.where(lane < counts_ref[base + b], charge, 0.0).astype(BF16)
        xs = [jnp.broadcast_to(pos_ref[d, pl.ds(base + b, 1), :], (nodes, slots)) for d in range(3)]
        turns = freq_scr[0] * xs[0] + freq_scr[1] * xs[1] + freq_scr[2] * xs[2]
        sin, cos = sin_cos_turns(turns)
        basis = jnp.concatenate([cos.astype(BF16), sin.astype(BF16)], axis=0)
        multipole = lax.dot_general(
            charge, basis, (((1,), (1,)), ((), ())), preferred_element_type=F32
        ).astype(BF16)
        mult_scr[b] = multipole
        child_scr[octants_ref[base + b], b // 8] = multipole

    def step(g, carry):
        for k in range(LEAF_UNROLL):
            one_leaf(g * LEAF_UNROLL + k)
        return carry

    lax.fori_loop(0, leaves // LEAF_UNROLL, step, 0)
    parents = leaves // 8
    rhs, width = mult_scr.shape[1:]
    wave_mat = wave_mat_ref[...]
    multipoles = mult_scr[...].reshape(leaves * rhs, width)
    waves = jnp.dot(multipoles, wave_mat, preferred_element_type=F32).astype(BF16)
    out_ref[:leaves] = waves.reshape(leaves, rhs, width)
    summed = None
    for octant in range(8):
        part = jnp.dot(
            child_scr[octant].reshape(parents * rhs, width),
            shift_ref[octant],
            preferred_element_type=F32,
        )
        summed = part if summed is None else summed + part
    parent_waves = jnp.dot(summed.astype(BF16), wave_mat, preferred_element_type=F32)
    out_ref[leaves:] = parent_waves.astype(BF16).reshape(parents, rhs, width)


def plan_kernel(local_rows, chunk, leaf_ref, parent_ref, source_out, class_out, chunks_out):
    core = lax.axis_index("rhs")
    list_len = leaf_ref.shape[0]
    targets = source_out.shape[0] // 2
    parents = parent_ref.shape[0] // 2
    leaves = targets - parents
    depth = -(-list_len // 8) * 8

    def packed(source, shift):
        return source + shift * (1 << 10)

    lanes = pl.ds(pl.multiple_of(core * leaves, leaves), leaves)
    leaf_words = packed(leaf_ref[:, 0, lanes], leaf_ref[:, 1, lanes])
    rows = pl.ds(core * parents, parents)
    parent_words = packed(parent_ref[rows, 0, :], parent_ref[rows, 1, :])
    parent_words = jnp.concatenate(
        [parent_words, jnp.zeros((parents, 256 - list_len), jnp.int32)], axis=1
    )
    parent_words = jnp.concatenate(
        [parent_words, jnp.zeros((128 - parents, 256), jnp.int32)], axis=0
    ).T[:depth]
    leaf_words = jnp.concatenate(
        [leaf_words, jnp.zeros((depth - list_len, leaves), jnp.int32)], axis=0
    )
    words = jnp.concatenate([leaf_words, parent_words], axis=1)
    row = lax.broadcasted_iota(jnp.int32, words.shape, 0)
    local = ((words & 1023) < local_rows) & (row < list_len)
    below = lax.broadcasted_iota(jnp.int32, (depth, depth), 0) >= lax.broadcasted_iota(
        jnp.int32, (depth, depth), 1
    )
    running = jnp.dot(
        jnp.where(below, 1.0, 0.0).astype(BF16),
        jnp.where(local, 1.0, 0.0).astype(BF16),
        preferred_element_type=F32,
    ).astype(jnp.int32)
    total = running[depth - 1 :]
    front = jnp.where(local, words + (row + 1 - running) * (1 << 20), 0)
    back = jnp.where(local, 0, words + (total - running) * (1 << 20))
    for k in range(8):
        bit = 1 << (20 + k)
        step = 1 << k
        moved = pltpu.roll(front, depth - step, 0)
        front = jnp.where((moved & bit) != 0, moved, jnp.where((front & bit) != 0, 0, front))
        moved = pltpu.roll(back, step, 0)
        back = jnp.where((moved & bit) != 0, moved, jnp.where((back & bit) != 0, 0, back))
    words = front + back
    for out, values in (
        (source_out, (words & 1023) * 16),
        (class_out, (lax.shift_right_logical(words, 10) & 1023) * 16),
    ):
        out[:targets] = values[:128].T[:targets]
        out[targets:] = pltpu.roll(values, depth - 2 * chunk, 0)[:128].T[:targets]
    full = [(total >= n * chunk).astype(jnp.int32) for n in range(1, list_len // chunk + 1)]
    chunks_out[...] = tree(full)


def pack_kernel(leaf_ids_ref, parent_ids_ref, own_ref, recv_ref, *refs):
    core = lax.axis_index("rhs")
    rows_ref, outs = refs[0], refs[1:]
    cap_l, cap_p = leaf_ids_ref.shape[1], parent_ids_ref.shape[1]
    parents = rows_ref.shape[0] // 18
    leaves = 8 * parents
    for values, which in ((own_ref, core), (recv_ref, 1 - core)):
        rows_ref[pl.ds(which * leaves, leaves)] = values[:leaves]
        rows_ref[pl.ds(2 * leaves + which * parents, parents)] = values[leaves:]
    for j, out in enumerate(outs):
        slot = core * len(outs) + j
        for k in range(cap_l):
            out[k] = rows_ref[leaf_ids_ref[slot, k]]
        for k in range(cap_p):
            out[cap_l + k] = rows_ref[2 * leaves + parent_ids_ref[slot, k]]


def put_rows(table, source, at, count, base, valid=None):
    half = table.shape[1]

    def body(k, carry):
        value = source[at + k].astype(F32)
        if valid is not None:
            value = jnp.where(valid, value, 0.0)
        row = pl.multiple_of((base + k) * 16, 16)
        table[pl.ds(row, 8), :] = value[:, :half]
        table[pl.ds(pl.multiple_of(row + 8, 8), 8), :] = value[:, half:]
        return carry

    lax.fori_loop(0, count, body, 0, unroll=8)


def put_all_factors(factor, trans_ref):
    half = factor.shape[1]

    def put_factors(first, values):
        for k in range(values.shape[0]):
            row = pl.multiple_of((first + k) * 16, 16)
            factor[pl.ds(row, 8), :] = jnp.broadcast_to(values[k : k + 1, :half], (8, half))
            factor[pl.ds(pl.multiple_of(row + 8, 8), 8), :] = jnp.broadcast_to(
                values[k : k + 1, half:], (8, half)
            )

    def factor_block(g, carry):
        first = pl.multiple_of(g * 8, 8)
        put_factors(first, trans_ref[pl.ds(first, 8), :])
        return carry

    full = trans_ref.shape[0] // 8 * 8
    lax.fori_loop(0, full // 8, factor_block, 0)
    if full < trans_ref.shape[0]:
        put_factors(full, trans_ref[full:, :])


def pair_sums(source_ref, class_ref, table, factor, chunk, targets):
    def accumulate(b, c, total):
        total_re, total_im = total
        first = b * 128 + jnp.where(c == 2, targets * 128, c * chunk)
        reals, imags = [], []
        for k in range(chunk):
            if k % GROUP == 0:
                span = min(GROUP, chunk - k)
                sources = source_ref.at[pl.ds(first + k, span)]
                classes = class_ref.at[pl.ds(first + k, span)]
            s = pl.multiple_of(sources[k % GROUP], 8)
            o = pl.multiple_of(classes[k % GROUP], 8)
            wave, shift = table.at[pl.ds(s, 16)], factor.at[pl.ds(o, 16)]
            wave_re, wave_im, shift_re, shift_im = wave[:8], wave[8:], shift[:8], shift[8:]
            reals.append(shift_re * wave_re - shift_im * wave_im)
            imags.append(shift_re * wave_im + shift_im * wave_re)
            if len(reals) == 3 or k == chunk - 1:
                total_re, total_im = total_re + tree(reals), total_im + tree(imags)
                reals, imags = [], []
        return total_re, total_im

    return accumulate


def index_copies(hbm_refs, smem_refs, sems, group, parts):
    words = TARGET_GROUP * 128
    part_words = hbm_refs[0].shape[0] // 2
    copies = []
    for hbm, smem in zip(hbm_refs, smem_refs):
        for part in range(parts):
            span = pl.ds(pl.multiple_of(part * part_words + group * words, 1024), words)
            sem = sems.at[group, len(copies)]
            copies.append(pltpu.make_async_copy(hbm.at[span], smem.at[span], sem))
    return copies


def over_targets(hbm_refs, smem_refs, sems, parts, targets, one_target):
    def one_group(g, carry):
        for copy in index_copies(hbm_refs, smem_refs, sems, g, parts):
            copy.wait()
        return lax.fori_loop(
            0, TARGET_GROUP, lambda t, c: one_target(g * TARGET_GROUP + t, c), carry
        )

    lax.fori_loop(0, targets // TARGET_GROUP, one_group, 0)


def start_indices(hbm_refs, smem_refs, sems, parts, targets):
    for group in range(targets // TARGET_GROUP):
        for copy in index_copies(hbm_refs, smem_refs, sems, group, parts):
            copy.start()


def near_kernel(
    chunk, chunks_ref, source_ref, class_ref, rows_ref, trans_ref, acc_ref,
    table, factor, source_scr, class_scr, sems,
):
    targets = acc_ref.shape[0]
    index = ((source_ref, class_ref), (source_scr, class_scr), sems)
    start_indices(*index, 1, targets)
    put_rows(table, rows_ref, 0, rows_ref.shape[0], 0)
    put_all_factors(factor, trans_ref)
    accumulate = pair_sums(source_scr, class_scr, table, factor, chunk, targets)

    def one_target(b, carry):
        zero = jnp.zeros((8, table.shape[1]), F32)
        total = lax.fori_loop(
            0, jnp.minimum(chunks_ref[0, b], 2), lambda c, t: accumulate(b, c, t), (zero, zero)
        )
        acc_ref[b, :8] = total[0]
        acc_ref[b, 8:] = total[1]
        return carry

    over_targets(*index, 1, targets, one_target)


def rest_kernel(dims, chunks_ref, source_ref, class_ref, rows_ref, *refs):
    slots, cap_l, cap_p, chunk, chunk_count, count = dims
    near = slots // 2
    near_own, near_recv = refs[:near], refs[near:slots]
    trans_ref, acc_ref, keep_ref, send_ref = refs[slots : slots + 4]
    table, factor, source_scr, class_scr, sems = refs[slots + 4 :]
    core = lax.axis_index("rhs")
    device = lax.axis_index("space")
    targets = acc_ref.shape[0]
    index = ((source_ref, class_ref), (source_scr, class_scr), sems)
    start_indices(*index, 2, targets)
    put_rows(table, rows_ref, 0, rows_ref.shape[0], 0)
    base = rows_ref.shape[0]
    for k in range(near):
        for values, which in ((near_own[k], core), (near_recv[k], 1 - core)):
            slot = which * near + k
            sender = device - jnp.where(which == 0, k - near, k + 1)
            valid = (sender >= 0) & (sender < count)
            put_rows(table, values, 0, cap_l, base + slot * cap_l, valid)
            put_rows(table, values, cap_l, cap_p, base + slots * cap_l + slot * cap_p, valid)
    put_all_factors(factor, trans_ref)
    accumulate = pair_sums(source_scr, class_scr, table, factor, chunk, targets)

    def one_target(b, carry):
        total = lax.fori_loop(
            jnp.minimum(chunks_ref[0, b], 2),
            chunk_count,
            lambda c, t: accumulate(b, c, t),
            (acc_ref[b, :8], acc_ref[b, 8:]),
        )
        incoming = jnp.concatenate(total, axis=1)
        lower, upper = incoming[:4], incoming[4:]
        keep_ref[b] = jnp.where(core == 0, lower, upper).astype(BF16)
        send_ref[b] = jnp.where(core == 0, upper, lower).astype(BF16)
        return carry

    over_targets(*index, 2, targets, one_target)


def local_kernel(leaves, keep_ref, recv_ref, mat_ref, leaf_ref, parent_ref):
    core = lax.axis_index("rhs")
    parents = keep_ref.shape[0] - leaves
    rhs, width = keep_ref.shape[1:]
    for values, which in ((keep_ref, core), (recv_ref, 1 - core)):
        flat = values[...].reshape((leaves + parents) * rhs, width)
        local = jnp.dot(flat, mat_ref[...], preferred_element_type=F32)
        local = local.reshape(leaves + parents, rhs, width)
        leaf_ref[pl.ds(which * leaves, leaves)] = local[:leaves]
        parent_ref[pl.ds(which * parents, parents)] = local[leaves:]


def shards(
    positions, point_counts, charges, frequencies, octants, child_shift, to_wave, to_local,
    translation, send_leaf, send_parent, leaf_pairs, parent_pairs,
):
    other = 1 - lax.axis_index("rhs")
    count = lax.axis_size("space")
    leaves = positions.shape[0] // 2
    parents = leaves // 8
    rhs = charges.shape[1]
    width = to_wave.shape[0]
    slots = send_leaf.shape[1]
    near = slots // 2
    held = leaves + parents
    list_len = leaf_pairs.shape[2]
    chunk = list_len // CHUNKS
    cap_l, cap_p = send_leaf.shape[2], send_parent.shape[2]
    table_rows = 2 * held + slots * (cap_l + cap_p)

    arrived_charges = swap_cores(lax.dynamic_slice_in_dim(charges, other * leaves, leaves, 0))
    index_shape = jax.ShapeDtypeStruct((2 * held, 128), jnp.int32)
    source_rows, class_rows, chunks = pl.pallas_call(
        functools.partial(plan_kernel, 2 * held, chunk),
        out_shape=[index_shape, index_shape, jax.ShapeDtypeStruct((1, 256), jnp.int32)],
        in_specs=[VMEM] * 2,
        out_specs=[VMEM] * 3,
        compiler_params=pltpu.CompilerParams(vmem_limit_bytes=12 << 20),
        name="plan",
    )(jnp.transpose(leaf_pairs, (2, 1, 0)), parent_pairs)
    arrived_charges, source_rows, class_rows, chunks = lax.optimization_barrier(
        (arrived_charges, source_rows, class_rows, chunks)
    )
    source_rows, class_rows = source_rows.reshape(-1), class_rows.reshape(-1)
    waves = pl.pallas_call(
        upward_kernel,
        out_shape=jax.ShapeDtypeStruct((held, 2 * rhs, width), BF16),
        in_specs=[SMEM] * 2 + [VMEM] * 6,
        out_specs=VMEM,
        scratch_shapes=[
            pltpu.VMEM((3, width // 2, positions.shape[2]), F32),
            pltpu.VMEM((leaves, 2 * rhs, width), BF16),
            pltpu.VMEM((8, parents, 2 * rhs, width), BF16),
        ],
        compiler_params=pltpu.CompilerParams(vmem_limit_bytes=12 << 20),
        name="upward",
    )(
        point_counts, octants, frequencies, jnp.transpose(positions, (1, 0, 2)), charges,
        arrived_charges, child_shift, to_wave,
    )
    arrived_waves = swap_cores(waves)
    rows, *sent = pl.pallas_call(
        pack_kernel,
        out_shape=[jax.ShapeDtypeStruct((2 * held, 2 * rhs, width), BF16)]
        + [jax.ShapeDtypeStruct((cap_l + cap_p, 2 * rhs, width), BF16)] * near,
        in_specs=[SMEM] * 2 + [VMEM] * 2,
        out_specs=[VMEM] * (1 + near),
        compiler_params=pltpu.CompilerParams(vmem_limit_bytes=12 << 20),
        name="pack",
    )(send_leaf[0], send_parent[0], waves, arrived_waves)
    def slot_permutation(k):
        pairs = []
        for core, offset in ((0, k - near), (1, k + 1)):
            pairs += [(2 * e + core, 2 * ((e + offset) % count) + core) for e in range(count)]
        return pairs

    near_own = [
        lax.ppermute(part, ("space", "rhs"), slot_permutation(k)) for k, part in enumerate(sent)
    ]
    index_scratch = [
        pltpu.VMEM((translation.shape[0] * 16, width // 2), F32),
        pltpu.SMEM((4 * held * 64,), jnp.int32),
        pltpu.SMEM((4 * held * 64,), jnp.int32),
        pltpu.SemaphoreType.DMA((held // TARGET_GROUP, 4)),
    ]
    acc = pl.pallas_call(
        functools.partial(near_kernel, chunk),
        out_shape=jax.ShapeDtypeStruct((held, 16, width // 2), F32),
        in_specs=[SMEM] + [ANY] * 2 + [VMEM] * 2,
        out_specs=VMEM,
        scratch_shapes=[pltpu.VMEM((2 * held * 16, width // 2), F32)] + index_scratch,
        cost_estimate=pl.CostEstimate(flops=25_000_000_000, bytes_accessed=80_000_000, transcendentals=0),
        compiler_params=pltpu.CompilerParams(vmem_limit_bytes=16 << 20),
        name="near",
    )(chunks, source_rows, class_rows, rows, translation)
    *near_own, acc = lax.optimization_barrier((*near_own, acc))
    near_recv = [swap_cores(part) for part in near_own]
    keep, send = pl.pallas_call(
        functools.partial(rest_kernel, (slots, cap_l, cap_p, chunk, CHUNKS, count)),
        out_shape=[jax.ShapeDtypeStruct((held, rhs, width), BF16)] * 2,
        in_specs=[SMEM] + [ANY] * 2 + [VMEM] * (3 + slots),
        out_specs=[VMEM] * 2,
        scratch_shapes=[pltpu.VMEM((table_rows * 16, width // 2), F32)] + index_scratch,
        compiler_params=pltpu.CompilerParams(vmem_limit_bytes=24 << 20),
        name="rest",
    )(chunks, source_rows, class_rows, rows, *near_own, *near_recv, translation, acc)
    arrived = swap_cores(send)
    return tuple(
        pl.pallas_call(
            functools.partial(local_kernel, leaves),
            out_shape=[
                jax.ShapeDtypeStruct((2 * leaves, rhs, width), F32),
                jax.ShapeDtypeStruct((2 * parents, rhs, width), F32),
            ],
            in_specs=[VMEM] * 3,
            out_specs=[VMEM] * 2,
            compiler_params=pltpu.CompilerParams(vmem_limit_bytes=12 << 20),
        name="local",
        )(keep, arrived, to_local)
    )


def solution(mesh):
    in_specs = (
        P("space", None, None), P("space"), P("space", "rhs", None), P(), P("space"), P(), P(), P(),
        P(), P("space", None, None), P("space", None, None), P("space", None, None),
        P("space", None, None),
    )
    out_specs = (P("space", "rhs", None), P("space", "rhs", None))
    return jax.shard_map(shards, mesh=mesh, in_specs=in_specs, out_specs=out_specs, check_vma=False)
```

```python
import functools
import math

import jax
import jax.numpy as jnp
from jax import lax
from jax.experimental import pallas as pl
from jax.experimental.pallas import tpu as pltpu
from jax.sharding import PartitionSpec as P

F32 = jnp.float32
BF16 = jnp.bfloat16
CHUNKS = 3
GROUP = 9
LEAF_UNROLL = 8
TARGET_GROUP = 16
FIRST_TARGETS = 112
SIN_POLY = (4.44286790342698, -7.307443431653506, 3.594788153158899, -0.7843741906863176)
COS_POLY = (
    1.4142134967586113,
    -6.978850998632011,
    5.7394613208713325,
    -1.883563790130787,
    0.31069962133630835,
)

VMEM = pl.BlockSpec(memory_space=pltpu.VMEM)
SMEM = pl.BlockSpec(memory_space=pltpu.SMEM)
ANY = pl.BlockSpec(memory_space=pl.ANY)
HBM = pl.BlockSpec(memory_space=pltpu.HBM)


def in_hbm(*values):
    return [pltpu.with_memory_space_constraint(value, pltpu.HBM) for value in values]


def swap_cores(value):
    return lax.ppermute(value, "rhs", [(0, 1), (1, 0)])


def horner(coefficients, x):
    total = coefficients[-1] * x + coefficients[-2]
    for coefficient in coefficients[-3::-1]:
        total = total * x + coefficient
    return total


def tree(values):
    values = list(values)
    while len(values) > 1:
        paired = [values[i] + values[i + 1] for i in range(0, len(values) - 1, 2)]
        values = paired + values[2 * len(paired) :]
    return values[0]


def sin_cos_turns(turns):
    r = turns - jnp.round(turns)
    r2 = r * r
    s = r * horner(SIN_POLY, r2)
    c = horner(COS_POLY, r2)
    return s * c, 1.0 - s * s


def upward_kernel(
    counts_hbm, octants_hbm, freq_hbm, pos_hbm, own_hbm, shift_hbm, wave_mat_hbm, recv_ref,
    out_ref, freq_scr, mult_scr, child_scr,
    counts_ref, octants_ref, freq_ref, pos_ref, own_ref, shift_ref, wave_mat_ref, sems,
):
    core = lax.axis_index("rhs")
    leaves, rhs_half, slots = own_ref.shape
    nodes = freq_ref.shape[1]
    base = core * leaves
    half = pl.ds(pl.multiple_of(base, leaves), leaves)
    moves = (
        (counts_hbm, counts_ref),
        (octants_hbm, octants_ref),
        (freq_hbm, freq_ref),
        (pos_hbm.at[:, half, :], pos_ref),
        (own_hbm.at[half], own_ref),
        (wave_mat_hbm, wave_mat_ref),
        (shift_hbm, shift_ref),
    )
    copies = [pltpu.make_async_copy(a, b, sems.at[i]) for i, (a, b) in enumerate(moves)]
    for copy in copies:
        copy.start()
    for copy in copies[:5]:
        copy.wait()
    for d in range(3):
        row = freq_ref[d : d + 1, :] * (1.0 / (2.0 * math.pi))
        freq_scr[d] = jnp.broadcast_to(row, (slots, nodes)).T
    lane = lax.broadcasted_iota(jnp.int32, (2 * rhs_half, slots), 1)

    def one_leaf(b):
        own, recv = own_ref[b].astype(F32), recv_ref[base + b].astype(F32)
        lower = jnp.where(core == 0, own, recv)
        upper = jnp.where(core == 0, recv, own)
        charge = jnp.concatenate([lower, upper], axis=0)
        charge = jnp.where(lane < counts_ref[base + b], charge, 0.0).astype(BF16)
        xs = [jnp.broadcast_to(pos_ref[d, pl.ds(b, 1), :], (nodes, slots)) for d in range(3)]
        turns = freq_scr[0] * xs[0] + freq_scr[1] * xs[1] + freq_scr[2] * xs[2]
        sin, cos = sin_cos_turns(turns)
        basis = jnp.concatenate([cos.astype(BF16), sin.astype(BF16)], axis=0)
        multipole = lax.dot_general(
            charge, basis, (((1,), (1,)), ((), ())), preferred_element_type=F32
        ).astype(BF16)
        mult_scr[b] = multipole
        child_scr[octants_ref[base + b], b // 8] = multipole

    def step(g, carry):
        for k in range(LEAF_UNROLL):
            one_leaf(g * LEAF_UNROLL + k)
        return carry

    lax.fori_loop(0, leaves // LEAF_UNROLL, step, 0)
    for copy in copies[5:]:
        copy.wait()
    parents = leaves // 8
    rhs, width = mult_scr.shape[1:]
    wave_mat = wave_mat_ref[...]
    multipoles = mult_scr[...].reshape(leaves * rhs, width)
    waves = jnp.dot(multipoles, wave_mat, preferred_element_type=F32).astype(BF16)
    out_ref[:leaves] = waves.reshape(leaves, rhs, width)
    summed = None
    for octant in range(8):
        part = jnp.dot(
            child_scr[octant].reshape(parents * rhs, width),
            shift_ref[octant],
            preferred_element_type=F32,
        )
        summed = part if summed is None else summed + part
    parent_waves = jnp.dot(summed.astype(BF16), wave_mat, preferred_element_type=F32)
    out_ref[leaves:] = parent_waves.astype(BF16).reshape(parents, rhs, width)


def plan_kernel(
    local_rows, chunk, leaf_hbm, parent_hbm, send_leaf_hbm, send_parent_hbm, trans_hbm,
    index_out, chunks_out, send_leaf_out, send_parent_out, trans_out, leaf_ref, parent_ref, sems,
):
    core = lax.axis_index("rhs")
    list_len, _, leaves = leaf_ref.shape
    parents = parent_ref.shape[0]
    targets = leaves + parents
    lanes = pl.ds(pl.multiple_of(core * leaves, leaves), leaves)
    copies = [
        pltpu.make_async_copy(leaf_hbm.at[:, :, lanes], leaf_ref, sems.at[0]),
        pltpu.make_async_copy(parent_hbm.at[pl.ds(core * parents, parents)], parent_ref, sems.at[1]),
        pltpu.make_async_copy(send_leaf_hbm, send_leaf_out, sems.at[2]),
        pltpu.make_async_copy(send_parent_hbm, send_parent_out, sems.at[3]),
        pltpu.make_async_copy(trans_hbm, trans_out, sems.at[4]),
    ]
    for copy in copies:
        copy.start()
    for copy in copies[:2]:
        copy.wait()
    depth = -(-list_len // 8) * 8

    def packed(source, shift):
        return source + shift * (1 << 10)

    leaf_words = packed(leaf_ref[:, 0, :], leaf_ref[:, 1, :])
    parent_words = packed(parent_ref[:, 0, :], parent_ref[:, 1, :])
    parent_words = jnp.concatenate(
        [parent_words, jnp.zeros((parents, 256 - list_len), jnp.int32)], axis=1
    )
    parent_words = jnp.concatenate(
        [parent_words, jnp.zeros((128 - parents, 256), jnp.int32)], axis=0
    ).T[:depth]
    leaf_words = jnp.concatenate(
        [leaf_words, jnp.zeros((depth - list_len, leaves), jnp.int32)], axis=0
    )
    words = jnp.concatenate([leaf_words, parent_words], axis=1)
    row = lax.broadcasted_iota(jnp.int32, words.shape, 0)
    local = ((words & 1023) < local_rows) & (row < list_len)
    below = lax.broadcasted_iota(jnp.int32, (depth, depth), 0) >= lax.broadcasted_iota(
        jnp.int32, (depth, depth), 1
    )
    running = jnp.dot(
        jnp.where(below, 1.0, 0.0).astype(BF16),
        jnp.where(local, 1.0, 0.0).astype(BF16),
        preferred_element_type=F32,
    ).astype(jnp.int32)
    total = running[depth - 1 :]
    front = jnp.where(local, words + (row + 1 - running) * (1 << 20), 0)
    back = jnp.where(local, 0, words + (total - running) * (1 << 20))
    for k in range(8):
        bit = 1 << (20 + k)
        step = 1 << k
        moved = pltpu.roll(front, depth - step, 0)
        front = jnp.where((moved & bit) != 0, moved, jnp.where((front & bit) != 0, 0, front))
        moved = pltpu.roll(back, step, 0)
        back = jnp.where((moved & bit) != 0, moved, jnp.where((back & bit) != 0, 0, back))
    words = front + back
    sources = (words & 1023) * 16
    classes = (lax.shift_right_logical(words, 10) & 1023) * 16
    for h, values in enumerate((sources, classes)):
        index_out[pl.ds(h, targets, stride=4), :] = values[:128].T[:targets]
        tail = pltpu.roll(values, depth - 2 * chunk, 0)[:128].T[:targets]
        index_out[pl.ds(2 + h, targets, stride=4), :] = tail
    full = [(total >= n * chunk).astype(jnp.int32) for n in range(1, list_len // chunk + 1)]
    chunks_out[...] = tree(full)
    for copy in copies[2:]:
        copy.wait()


def pack_kernel(leaf_ids_ref, parent_ids_ref, own_ref, recv_ref, *refs):
    core = lax.axis_index("rhs")
    rows_ref, outs = refs[0], refs[1:]
    cap_l, cap_p = leaf_ids_ref.shape[1], parent_ids_ref.shape[1]
    parents = rows_ref.shape[0] // 18
    leaves = 8 * parents
    for values, which in ((own_ref, core), (recv_ref, 1 - core)):
        rows_ref[pl.ds(which * leaves, leaves)] = values[:leaves]
        rows_ref[pl.ds(2 * leaves + which * parents, parents)] = values[leaves:]
    for j, out in enumerate(outs):
        slot = core * len(outs) + j
        for k in range(cap_l):
            out[k] = rows_ref[leaf_ids_ref[slot, k]]
        for k in range(cap_p):
            out[cap_l + k] = rows_ref[2 * leaves + parent_ids_ref[slot, k]]


def put_rows(table, source, at, count, base, valid=None):
    half = table.shape[1]

    def body(k, carry):
        value = source[at + k].astype(F32)
        if valid is not None:
            value = jnp.where(valid, value, 0.0)
        row = pl.multiple_of((base + k) * 16, 16)
        table[pl.ds(row, 8), :] = value[:, :half]
        table[pl.ds(pl.multiple_of(row + 8, 8), 8), :] = value[:, half:]
        return carry

    lax.fori_loop(0, count, body, 0, unroll=8)


def put_all_factors(factor, trans_ref):
    half = factor.shape[1]

    def put_factors(first, values):
        for k in range(values.shape[0]):
            row = pl.multiple_of((first + k) * 16, 16)
            factor[pl.ds(row, 8), :] = jnp.broadcast_to(values[k : k + 1, :half], (8, half))
            factor[pl.ds(pl.multiple_of(row + 8, 8), 8), :] = jnp.broadcast_to(
                values[k : k + 1, half:], (8, half)
            )

    def factor_block(g, carry):
        first = pl.multiple_of(g * 8, 8)
        put_factors(first, trans_ref[pl.ds(first, 8), :])
        return carry

    full = trans_ref.shape[0] // 8 * 8
    lax.fori_loop(0, full // 8, factor_block, 0)
    if full < trans_ref.shape[0]:
        put_factors(full, trans_ref[full:, :])


def pair_sums(index_ref, table, factor, chunk):
    def accumulate(b, c, total):
        total_re, total_im = total
        first = b * 512 + jnp.where(c == 2, 256, c * chunk)
        reals, imags = [], []
        for k in range(chunk):
            if k % GROUP == 0:
                span = min(GROUP, chunk - k)
                sources = index_ref.at[pl.ds(first + k, span)]
                classes = index_ref.at[pl.ds(first + 128 + k, span)]
            s = pl.multiple_of(sources[k % GROUP], 8)
            o = pl.multiple_of(classes[k % GROUP], 8)
            wave, shift = table.at[pl.ds(s, 16)], factor.at[pl.ds(o, 16)]
            wave_re, wave_im, shift_re, shift_im = wave[:8], wave[8:], shift[:8], shift[8:]
            reals.append(shift_re * wave_re - shift_im * wave_im)
            imags.append(shift_re * wave_im + shift_im * wave_re)
            if len(reals) == 3 or k == chunk - 1:
                total_re, total_im = total_re + tree(reals), total_im + tree(imags)
                reals, imags = [], []
        return total_re, total_im

    return accumulate


def index_copy(index_hbm, index_scr, sems, group):
    words = TARGET_GROUP * 512
    span = pl.ds(pl.multiple_of(group * words, 1024), words)
    return pltpu.make_async_copy(index_hbm.at[span], index_scr.at[span], sems.at[group])


def over_targets(index, first, last, one_target):
    def one_group(g, carry):
        @pl.when(g + 2 < last // TARGET_GROUP)
        def _():
            index_copy(*index, g + 2).start()

        index_copy(*index, g).wait()
        return lax.fori_loop(
            0, TARGET_GROUP, lambda t, c: one_target(g * TARGET_GROUP + t, c), carry
        )

    lax.fori_loop(first // TARGET_GROUP, last // TARGET_GROUP, one_group, 0)


def start_indices(index, first, last):
    for group in range(first // TARGET_GROUP, min(first // TARGET_GROUP + 2, last // TARGET_GROUP)):
        index_copy(*index, group).start()


def near_targets(index, first, last, chunks_ref, table, factor, chunk, acc_ref):
    accumulate = pair_sums(index[1], table, factor, chunk)

    def one_target(b, carry):
        zero = jnp.zeros((8, table.shape[1]), F32)
        total = lax.fori_loop(
            0, jnp.minimum(chunks_ref[0, b], 2), lambda c, t: accumulate(b, c, t), (zero, zero)
        )
        acc_ref[b - first, :8] = total[0]
        acc_ref[b - first, 8:] = total[1]
        return carry

    over_targets(index, first, last, one_target)


def near_kernel(
    chunk, last, chunks_ref, index_hbm, rows_ref, trans_ref, table, factor, acc_ref, index_scr, sems
):
    index = (index_hbm, index_scr, sems)
    start_indices(index, 0, last)
    put_rows(table, rows_ref, 0, rows_ref.shape[0], 0)
    put_all_factors(factor, trans_ref)
    near_targets(index, 0, last, chunks_ref, table, factor, chunk, acc_ref)


def more_kernel(
    chunk, first, last, chunks_ref, index_hbm, table, factor, acc_ref, index_scr, sems
):
    index = (index_hbm, index_scr, sems)
    start_indices(index, first, last)
    near_targets(index, first, last, chunks_ref, table, factor, chunk, acc_ref)


def rest_kernel(dims, chunks_ref, index_hbm, table_in, factor, *refs):
    slots, cap_l, cap_p, base, chunk, chunk_count, count = dims
    near = slots // 2
    near_own, near_recv = refs[:near], refs[near:slots]
    acc_refs = refs[slots : slots + 2]
    keep_ref, send_ref, table, index_scr, sems = refs[slots + 2 :]
    core = lax.axis_index("rhs")
    device = lax.axis_index("space")
    targets = keep_ref.shape[0]
    index = (index_hbm, index_scr, sems)
    start_indices(index, 0, targets)
    for k in range(near):
        for values, which in ((near_own[k], core), (near_recv[k], 1 - core)):
            slot = which * near + k
            sender = device - jnp.where(which == 0, k - near, k + 1)
            valid = (sender >= 0) & (sender < count)
            put_rows(table, values, 0, cap_l, base + slot * cap_l, valid)
            put_rows(table, values, cap_l, cap_p, base + slots * cap_l + slot * cap_p, valid)
    accumulate = pair_sums(index_scr, table, factor, chunk)
    first = 0
    for acc_ref in acc_refs:

        def one_target(b, carry, acc_ref=acc_ref, first=first):
            total = lax.fori_loop(
                jnp.minimum(chunks_ref[0, b], 2),
                chunk_count,
                lambda c, t: accumulate(b, c, t),
                (acc_ref[b - first, :8], acc_ref[b - first, 8:]),
            )
            incoming = jnp.concatenate(total, axis=1)
            lower, upper = incoming[:4], incoming[4:]
            keep_ref[b] = jnp.where(core == 0, lower, upper).astype(BF16)
            send_ref[b] = jnp.where(core == 0, upper, lower).astype(BF16)
            return carry

        last = first + acc_ref.shape[0]
        if first:
            start_indices(index, first, last)
        over_targets(index, first, last, one_target)
        first = last


def local_kernel(leaves, keep_ref, recv_ref, mat_ref, leaf_ref, parent_ref):
    core = lax.axis_index("rhs")
    parents = keep_ref.shape[0] - leaves
    rhs, width = keep_ref.shape[1:]
    for values, which in ((keep_ref, core), (recv_ref, 1 - core)):
        flat = values[...].reshape((leaves + parents) * rhs, width)
        local = jnp.dot(flat, mat_ref[...], preferred_element_type=F32)
        local = local.reshape(leaves + parents, rhs, width)
        leaf_ref[pl.ds(which * leaves, leaves)] = local[:leaves]
        parent_ref[pl.ds(which * parents, parents)] = local[leaves:]


def shards(
    positions, point_counts, charges, frequencies, octants, child_shift, to_wave, to_local,
    translation, send_leaf, send_parent, leaf_pairs, parent_pairs,
):
    other = 1 - lax.axis_index("rhs")
    count = lax.axis_size("space")
    leaves = positions.shape[0] // 2
    parents = leaves // 8
    rhs = charges.shape[1]
    width = to_wave.shape[0]
    slots = send_leaf.shape[1]
    near = slots // 2
    held = leaves + parents
    list_len = leaf_pairs.shape[2]
    chunk = list_len // CHUNKS
    cap_l, cap_p = send_leaf.shape[2], send_parent.shape[2]
    table_rows = 2 * held + slots * (cap_l + cap_p)

    arrived_charges = swap_cores(charges)
    indices, chunks, leaf_ids, parent_ids, factors = pl.pallas_call(
        functools.partial(plan_kernel, 2 * held, chunk),
        out_shape=[
            jax.ShapeDtypeStruct((4 * held, 128), jnp.int32),
            jax.ShapeDtypeStruct((1, 256), jnp.int32),
            jax.ShapeDtypeStruct(send_leaf.shape[1:], jnp.int32),
            jax.ShapeDtypeStruct(send_parent.shape[1:], jnp.int32),
            jax.ShapeDtypeStruct(translation.shape, F32),
        ],
        in_specs=[HBM] * 5,
        out_specs=[VMEM] * 5,
        scratch_shapes=[
            pltpu.VMEM((list_len, 2, leaves), jnp.int32),
            pltpu.VMEM((parents, 2, list_len), jnp.int32),
            pltpu.SemaphoreType.DMA((5,)),
        ],
        compiler_params=pltpu.CompilerParams(vmem_limit_bytes=12 << 20),
        name="plan",
    )(
        *in_hbm(
            jnp.transpose(leaf_pairs, (2, 1, 0)), parent_pairs, send_leaf[0], send_parent[0],
            translation,
        )
    )
    arrived_charges, indices, chunks, leaf_ids, parent_ids, factors = lax.optimization_barrier(
        (arrived_charges, indices, chunks, leaf_ids, parent_ids, factors)
    )
    indices = indices.reshape(-1)
    waves = pl.pallas_call(
        upward_kernel,
        out_shape=jax.ShapeDtypeStruct((held, 2 * rhs, width), BF16),
        in_specs=[HBM] * 7 + [VMEM],
        out_specs=VMEM,
        scratch_shapes=[
            pltpu.VMEM((3, width // 2, positions.shape[2]), F32),
            pltpu.VMEM((leaves, 2 * rhs, width), BF16),
            pltpu.VMEM((8, parents, 2 * rhs, width), BF16),
            pltpu.SMEM(point_counts.shape, jnp.int32),
            pltpu.SMEM(octants.shape, jnp.int32),
            pltpu.VMEM(frequencies.shape, F32),
            pltpu.VMEM((3, leaves, positions.shape[2]), F32),
            pltpu.VMEM((leaves,) + charges.shape[1:], BF16),
            pltpu.VMEM(child_shift.shape, BF16),
            pltpu.VMEM(to_wave.shape, BF16),
            pltpu.SemaphoreType.DMA((7,)),
        ],
        compiler_params=pltpu.CompilerParams(vmem_limit_bytes=12 << 20),
        name="upward",
    )(
        *in_hbm(
            point_counts, octants, frequencies, jnp.transpose(positions, (1, 0, 2)), charges,
            child_shift, to_wave,
        ),
        arrived_charges,
    )
    arrived_waves = swap_cores(waves)
    rows, *sent = pl.pallas_call(
        pack_kernel,
        out_shape=[jax.ShapeDtypeStruct((2 * held, 2 * rhs, width), BF16)]
        + [jax.ShapeDtypeStruct((cap_l + cap_p, 2 * rhs, width), BF16)] * near,
        in_specs=[SMEM] * 2 + [VMEM] * 2,
        out_specs=[VMEM] * (1 + near),
        compiler_params=pltpu.CompilerParams(vmem_limit_bytes=12 << 20),
        name="pack",
    )(leaf_ids, parent_ids, waves, arrived_waves)
    def slot_permutation(k):
        pairs = []
        for core, offset in ((0, k - near), (1, k + 1)):
            pairs += [(2 * e + core, 2 * ((e + offset) % count) + core) for e in range(count)]
        return pairs

    near_own = [
        lax.ppermute(part, ("space", "rhs"), slot_permutation(k)) for k, part in enumerate(sent)
    ]
    index_scratch = [
        pltpu.SMEM((held * 512,), jnp.int32),
        pltpu.SemaphoreType.DMA((held // TARGET_GROUP,)),
    ]
    table_shape = jax.ShapeDtypeStruct((table_rows * 16, width // 2), F32)
    factor_shape = jax.ShapeDtypeStruct((translation.shape[0] * 16, width // 2), F32)

    def acc_shape(targets):
        return jax.ShapeDtypeStruct((targets, 16, width // 2), F32)

    def cost(targets):
        return pl.CostEstimate(
            flops=targets * 170_000_000, bytes_accessed=targets * 500_000, transcendentals=0
        )

    table, factor, acc_first = pl.pallas_call(
        functools.partial(near_kernel, chunk, FIRST_TARGETS),
        out_shape=[table_shape, factor_shape, acc_shape(FIRST_TARGETS)],
        in_specs=[SMEM, ANY, VMEM, VMEM],
        out_specs=[VMEM] * 3,
        scratch_shapes=index_scratch,
        cost_estimate=cost(FIRST_TARGETS),
        compiler_params=pltpu.CompilerParams(vmem_limit_bytes=20 << 20),
        name="near",
    )(chunks, indices, rows, factors)
    *near_own, acc_first = lax.optimization_barrier((*near_own, acc_first))
    near_recv = [swap_cores(part) for part in near_own]
    acc_last = pl.pallas_call(
        functools.partial(more_kernel, chunk, FIRST_TARGETS, held),
        out_shape=acc_shape(held - FIRST_TARGETS),
        in_specs=[SMEM, ANY, VMEM, VMEM],
        out_specs=VMEM,
        scratch_shapes=index_scratch,
        cost_estimate=cost(held - FIRST_TARGETS),
        compiler_params=pltpu.CompilerParams(vmem_limit_bytes=20 << 20),
        name="more",
    )(chunks, indices, table, factor)
    keep, send, _ = pl.pallas_call(
        functools.partial(
            rest_kernel, (slots, cap_l, cap_p, 2 * held, chunk, CHUNKS, count)
        ),
        out_shape=[jax.ShapeDtypeStruct((held, rhs, width), BF16)] * 2 + [table_shape],
        in_specs=[SMEM, ANY] + [VMEM] * (4 + slots),
        out_specs=[VMEM] * 3,
        scratch_shapes=index_scratch,
        input_output_aliases={2: 2},
        compiler_params=pltpu.CompilerParams(vmem_limit_bytes=20 << 20),
        name="rest",
    )(chunks, indices, table, factor, *near_own, *near_recv, acc_first, acc_last)
    arrived = swap_cores(send)
    return tuple(
        pl.pallas_call(
            functools.partial(local_kernel, leaves),
            out_shape=[
                jax.ShapeDtypeStruct((2 * leaves, rhs, width), F32),
                jax.ShapeDtypeStruct((2 * parents, rhs, width), F32),
            ],
            in_specs=[VMEM] * 3,
            out_specs=[VMEM] * 2,
            compiler_params=pltpu.CompilerParams(vmem_limit_bytes=12 << 20),
        name="local",
        )(keep, arrived, to_local)
    )


def solution(mesh):
    in_specs = (
        P("space", None, None), P("space"), P("space", "rhs", None), P(), P("space"), P(), P(), P(),
        P(), P("space", None, None), P("space", None, None), P("space", None, None),
        P("space", None, None),
    )
    out_specs = (P("space", "rhs", None), P("space", "rhs", None))
    return jax.shard_map(shards, mesh=mesh, in_specs=in_specs, out_specs=out_specs, check_vma=False)
```

```python
import functools
import math

import jax
import jax.numpy as jnp
from jax import lax
from jax.experimental import pallas as pl
from jax.experimental.pallas import tpu as pltpu
from jax.sharding import PartitionSpec as P

F32 = jnp.float32
BF16 = jnp.bfloat16
GROUP = 9
LEAF_UNROLL = 2
TARGET_GROUP = 16
SIN_POLY = (4.44286790342698, -7.307443431653506, 3.594788153158899, -0.7843741906863176)
COS_POLY = (
    1.4142134967586113,
    -6.978850998632011,
    5.7394613208713325,
    -1.883563790130787,
    0.31069962133630835,
)

VMEM = pl.BlockSpec(memory_space=pltpu.VMEM)
SMEM = pl.BlockSpec(memory_space=pltpu.SMEM)
ANY = pl.BlockSpec(memory_space=pl.ANY)
HBM = pl.BlockSpec(memory_space=pltpu.HBM)


def in_hbm(*values):
    return [pltpu.with_memory_space_constraint(value, pltpu.HBM) for value in values]


def swap_cores(value):
    return lax.ppermute(value, "rhs", [(0, 1), (1, 0)])


def horner(coefficients, x):
    total = coefficients[-1] * x + coefficients[-2]
    for coefficient in coefficients[-3::-1]:
        total = total * x + coefficient
    return total


def tree(values):
    values = list(values)
    while len(values) > 1:
        paired = [values[i] + values[i + 1] for i in range(0, len(values) - 1, 2)]
        values = paired + values[2 * len(paired) :]
    return values[0]


def sin_cos_turns(turns):
    r = turns - jnp.round(turns)
    r2 = r * r
    s = r * horner(SIN_POLY, r2)
    c = horner(COS_POLY, r2)
    return s * c, 1.0 - s * s


def upward_kernel(
    counts_hbm, octants_hbm, freq_hbm, pos_hbm, own_hbm, shift_hbm, wave_mat_hbm, recv_ref,
    out_ref, freq_scr, mult_scr, child_scr, basis_scr,
    counts_ref, octants_ref, freq_ref, pos_ref, own_ref, shift_ref, wave_mat_ref, sems,
):
    core = lax.axis_index("rhs")
    leaves, rhs_half, slots = own_ref.shape
    nodes = freq_ref.shape[1]
    base = core * leaves
    half = pl.ds(pl.multiple_of(base, leaves), leaves)
    moves = (
        (counts_hbm, counts_ref),
        (octants_hbm, octants_ref),
        (freq_hbm, freq_ref),
        (pos_hbm.at[:, half, :], pos_ref),
        (own_hbm.at[half], own_ref),
        (wave_mat_hbm, wave_mat_ref),
        (shift_hbm, shift_ref),
    )
    copies = [pltpu.make_async_copy(a, b, sems.at[i]) for i, (a, b) in enumerate(moves)]
    for copy in copies:
        copy.start()
    for copy in copies[:5]:
        copy.wait()
    for d in range(3):
        row = freq_ref[d : d + 1, :] * (1.0 / (2.0 * math.pi))
        freq_scr[d] = jnp.broadcast_to(row, (slots, nodes)).T
    lane = lax.broadcasted_iota(jnp.int32, (2 * rhs_half, slots), 1)

    def put_basis(b):
        xs = [jnp.broadcast_to(pos_ref[d, pl.ds(b, 1), :], (nodes, slots)) for d in range(3)]
        turns = freq_scr[0] * xs[0] + freq_scr[1] * xs[1] + freq_scr[2] * xs[2]
        sin, cos = sin_cos_turns(turns)
        basis_scr[b % (2 * LEAF_UNROLL), :nodes] = cos.astype(BF16)
        basis_scr[b % (2 * LEAF_UNROLL), nodes:] = sin.astype(BF16)

    def put_multipole(b):
        own, recv = own_ref[b].astype(F32), recv_ref[base + b].astype(F32)
        lower = jnp.where(core == 0, own, recv)
        upper = jnp.where(core == 0, recv, own)
        charge = jnp.concatenate([lower, upper], axis=0)
        charge = jnp.where(lane < counts_ref[base + b], charge, 0.0).astype(BF16)
        multipole = lax.dot_general(
            charge,
            basis_scr[b % (2 * LEAF_UNROLL)],
            (((1,), (1,)), ((), ())),
            preferred_element_type=F32,
        ).astype(BF16)
        mult_scr[b] = multipole
        child_scr[octants_ref[base + b], b // 8] = multipole

    def step(g, carry):
        for k in range(LEAF_UNROLL):
            put_multipole((g - 1) * LEAF_UNROLL + k)
        for k in range(LEAF_UNROLL):
            put_basis(g * LEAF_UNROLL + k)
        return carry

    for k in range(LEAF_UNROLL):
        put_basis(k)
    lax.fori_loop(1, leaves // LEAF_UNROLL, step, 0)
    for k in range(LEAF_UNROLL):
        put_multipole(leaves - LEAF_UNROLL + k)
    for copy in copies[5:]:
        copy.wait()
    parents = leaves // 8
    rhs, width = mult_scr.shape[1:]
    wave_mat = wave_mat_ref[...]
    multipoles = mult_scr[...].reshape(leaves * rhs, width)
    waves = jnp.dot(multipoles, wave_mat, preferred_element_type=F32).astype(BF16)
    out_ref[:leaves] = waves.reshape(leaves, rhs, width)
    summed = None
    for octant in range(8):
        part = jnp.dot(
            child_scr[octant].reshape(parents * rhs, width),
            shift_ref[octant],
            preferred_element_type=F32,
        )
        summed = part if summed is None else summed + part
    parent_waves = jnp.dot(summed.astype(BF16), wave_mat, preferred_element_type=F32)
    out_ref[leaves:] = parent_waves.astype(BF16).reshape(parents, rhs, width)


def plan_kernel(
    local_rows, split, leaf_hbm, parent_hbm, send_leaf_hbm, send_parent_hbm, trans_hbm,
    first_out, second_out, send_leaf_out, send_parent_out, trans_out, leaf_ref, parent_ref, sems,
):
    core = lax.axis_index("rhs")
    list_len, _, leaves = leaf_ref.shape
    parents = parent_ref.shape[0]
    targets = leaves + parents
    lanes = pl.ds(pl.multiple_of(core * leaves, leaves), leaves)
    copies = [
        pltpu.make_async_copy(leaf_hbm.at[:, :, lanes], leaf_ref, sems.at[0]),
        pltpu.make_async_copy(parent_hbm.at[pl.ds(core * parents, parents)], parent_ref, sems.at[1]),
        pltpu.make_async_copy(send_leaf_hbm, send_leaf_out, sems.at[2]),
        pltpu.make_async_copy(send_parent_hbm, send_parent_out, sems.at[3]),
        pltpu.make_async_copy(trans_hbm, trans_out, sems.at[4]),
    ]
    for copy in copies:
        copy.start()
    for copy in copies[:2]:
        copy.wait()
    depth = -(-list_len // 8) * 8

    def packed(source, shift):
        return source + shift * (1 << 10)

    leaf_words = packed(leaf_ref[:, 0, :], leaf_ref[:, 1, :])
    parent_words = packed(parent_ref[:, 0, :], parent_ref[:, 1, :])
    parent_words = jnp.concatenate(
        [parent_words, jnp.zeros((parents, 256 - list_len), jnp.int32)], axis=1
    )
    parent_words = jnp.concatenate(
        [parent_words, jnp.zeros((128 - parents, 256), jnp.int32)], axis=0
    ).T[:depth]
    leaf_words = jnp.concatenate(
        [leaf_words, jnp.zeros((depth - list_len, leaves), jnp.int32)], axis=0
    )
    words = jnp.concatenate([leaf_words, parent_words], axis=1)
    row = lax.broadcasted_iota(jnp.int32, words.shape, 0)
    local = ((words & 1023) < local_rows) & (row < list_len)
    below = lax.broadcasted_iota(jnp.int32, (depth, depth), 0) >= lax.broadcasted_iota(
        jnp.int32, (depth, depth), 1
    )
    running = jnp.dot(
        jnp.where(below, 1.0, 0.0).astype(BF16),
        jnp.where(local, 1.0, 0.0).astype(BF16),
        preferred_element_type=F32,
    ).astype(jnp.int32)
    total = running[depth - 1 :]
    front = jnp.where(local, words + (row + 1 - running) * (1 << 20), 0)
    back = jnp.where(local, 0, words + (total - running) * (1 << 20))
    for k in range(8):
        bit = 1 << (20 + k)
        step = 1 << k
        moved = pltpu.roll(front, depth - step, 0)
        front = jnp.where((moved & bit) != 0, moved, jnp.where((front & bit) != 0, 0, front))
        moved = pltpu.roll(back, step, 0)
        back = jnp.where((moved & bit) != 0, moved, jnp.where((back & bit) != 0, 0, back))
    words = front + back
    sources = (words & 1023) * 16
    classes = (lax.shift_right_logical(words, 10) & 1023) * 16
    ready = (total >= split).astype(jnp.int32)
    for h, values in enumerate((sources, classes)):
        head = jnp.where(row[:128] == 127, ready, values[:128])
        tail = jnp.where(row[:128] == 127, ready, pltpu.roll(values, depth - split, 0)[:128])
        first_out[pl.ds(h, targets, stride=2), :] = head.T[:targets]
        second_out[pl.ds(h, targets, stride=2), :] = tail.T[:targets]
    for copy in copies[2:]:
        copy.wait()


def pack_kernel(leaf_ids_ref, parent_ids_ref, own_ref, recv_ref, *refs):
    core = lax.axis_index("rhs")
    rows_ref, outs = refs[0], refs[1:]
    cap_l, cap_p = leaf_ids_ref.shape[1], parent_ids_ref.shape[1]
    parents = rows_ref.shape[0] // 18
    leaves = 8 * parents
    for values, which in ((own_ref, core), (recv_ref, 1 - core)):
        rows_ref[pl.ds(which * leaves, leaves)] = values[:leaves]
        rows_ref[pl.ds(2 * leaves + which * parents, parents)] = values[leaves:]
    for j, out in enumerate(outs):
        slot = core * len(outs) + j
        for k in range(cap_l):
            out[k] = rows_ref[leaf_ids_ref[slot, k]]
        for k in range(cap_p):
            out[cap_l + k] = rows_ref[2 * leaves + parent_ids_ref[slot, k]]


def put_rows(table, source, at, count, base, valid=None):
    half = table.shape[1]

    def body(k, carry):
        value = source[at + k].astype(F32)
        if valid is not None:
            value = jnp.where(valid, value, 0.0)
        row = pl.multiple_of((base + k) * 16, 16)
        table[pl.ds(row, 8), :] = value[:, :half]
        table[pl.ds(pl.multiple_of(row + 8, 8), 8), :] = value[:, half:]
        return carry

    lax.fori_loop(0, count, body, 0, unroll=8)


def put_all_factors(factor, trans_ref):
    half = factor.shape[1]

    def put_factors(first, values):
        for k in range(values.shape[0]):
            row = pl.multiple_of((first + k) * 16, 16)
            factor[pl.ds(row, 8), :] = jnp.broadcast_to(values[k : k + 1, :half], (8, half))
            factor[pl.ds(pl.multiple_of(row + 8, 8), 8), :] = jnp.broadcast_to(
                values[k : k + 1, half:], (8, half)
            )

    def factor_block(g, carry):
        first = pl.multiple_of(g * 8, 8)
        put_factors(first, trans_ref[pl.ds(first, 8), :])
        return carry

    full = trans_ref.shape[0] // 8 * 8
    lax.fori_loop(0, full // 8, factor_block, 0)
    if full < trans_ref.shape[0]:
        put_factors(full, trans_ref[full:, :])


def pair_sums(index_ref, first, count, table, factor, total):
    total_re, total_im = total
    reals, imags = [], []
    for k in range(count):
        if k % GROUP == 0:
            span = min(GROUP, count - k)
            sources = index_ref.at[pl.ds(first + k, span)]
            classes = index_ref.at[pl.ds(first + 128 + k, span)]
        s = pl.multiple_of(sources[k % GROUP], 8)
        o = pl.multiple_of(classes[k % GROUP], 8)
        wave, shift = table.at[pl.ds(s, 16)], factor.at[pl.ds(o, 16)]
        wave_re, wave_im, shift_re, shift_im = wave[:8], wave[8:], shift[:8], shift[8:]
        reals.append(shift_re * wave_re - shift_im * wave_im)
        imags.append(shift_re * wave_im + shift_im * wave_re)
        if len(reals) == 3 or k == count - 1:
            total_re, total_im = total_re + tree(reals), total_im + tree(imags)
            reals, imags = [], []
    return total_re, total_im


def index_copy(index_hbm, index_scr, sems, group):
    words = TARGET_GROUP * 256
    span = pl.ds(pl.multiple_of(group * words, 1024), words)
    return pltpu.make_async_copy(index_hbm.at[span], index_scr.at[span], sems.at[group])


def start_indices(index):
    for group in range(2):
        index_copy(*index, group).start()


def over_targets(index, targets, one_target):
    def one_group(g, carry):
        @pl.when(g + 2 < targets // TARGET_GROUP)
        def _():
            index_copy(*index, g + 2).start()

        index_copy(*index, g).wait()
        return lax.fori_loop(
            0, TARGET_GROUP, lambda t, c: one_target(g * TARGET_GROUP + t, c), carry
        )

    lax.fori_loop(0, targets // TARGET_GROUP, one_group, 0)


def near_kernel(split, index_hbm, rows_ref, trans_ref, table, factor, acc_ref, index_scr, sems):
    index = (index_hbm, index_scr, sems)
    start_indices(index)
    put_rows(table, rows_ref, 0, rows_ref.shape[0], 0)
    put_all_factors(factor, trans_ref)
    zero = jnp.zeros((8, table.shape[1]), F32)

    def one_target(b, carry):
        @pl.when(index_scr[b * 256 + 127] > 0)
        def _():
            total = pair_sums(index_scr, b * 256, split, table, factor, (zero, zero))
            acc_ref[b, :8] = total[0]
            acc_ref[b, 8:] = total[1]

        return carry

    over_targets(index, acc_ref.shape[0], one_target)


def rest_kernel(dims, first_hbm, second_hbm, table_in, factor, *refs):
    slots, cap_l, cap_p, base, split, list_len, count = dims
    near = slots // 2
    near_own, near_recv = refs[:near], refs[near:slots]
    acc_ref, keep_ref, send_ref, table, index_scr, late_scr, sems, late_sem = refs[slots + 1 :]
    core = lax.axis_index("rhs")
    device = lax.axis_index("space")
    index = (second_hbm, index_scr, sems)
    start_indices(index)
    for k in range(near):
        for values, which in ((near_own[k], core), (near_recv[k], 1 - core)):
            slot = which * near + k
            sender = device - jnp.where(which == 0, k - near, k + 1)
            valid = (sender >= 0) & (sender < count)
            put_rows(table, values, 0, cap_l, base + slot * cap_l, valid)
            put_rows(table, values, cap_l, cap_p, base + slots * cap_l + slot * cap_p, valid)
    zero = jnp.zeros((8, table.shape[1]), F32)

    def one_target(b, carry):
        @pl.when(index_scr[b * 256 + 127] == 0)
        def _():
            span = pl.ds(pl.multiple_of(b * 256, 256), 256)
            copy = pltpu.make_async_copy(first_hbm.at[span], late_scr, late_sem)
            copy.start()
            copy.wait()
            total = pair_sums(late_scr, 0, split, table, factor, (zero, zero))
            acc_ref[b, :8] = total[0]
            acc_ref[b, 8:] = total[1]

        total = pair_sums(
            index_scr, b * 256, list_len - split, table, factor, (acc_ref[b, :8], acc_ref[b, 8:])
        )
        incoming = jnp.concatenate(total, axis=1)
        lower, upper = incoming[:4], incoming[4:]
        keep_ref[b] = jnp.where(core == 0, lower, upper).astype(BF16)
        send_ref[b] = jnp.where(core == 0, upper, lower).astype(BF16)
        return carry

    over_targets(index, keep_ref.shape[0], one_target)


def local_kernel(leaves, keep_ref, recv_ref, mat_ref, leaf_ref, parent_ref):
    core = lax.axis_index("rhs")
    parents = keep_ref.shape[0] - leaves
    rhs, width = keep_ref.shape[1:]
    for values, which in ((keep_ref, core), (recv_ref, 1 - core)):
        flat = values[...].reshape((leaves + parents) * rhs, width)
        local = jnp.dot(flat, mat_ref[...], preferred_element_type=F32)
        local = local.reshape(leaves + parents, rhs, width)
        leaf_ref[pl.ds(which * leaves, leaves)] = local[:leaves]
        parent_ref[pl.ds(which * parents, parents)] = local[leaves:]


def shards(
    positions, point_counts, charges, frequencies, octants, child_shift, to_wave, to_local,
    translation, send_leaf, send_parent, leaf_pairs, parent_pairs,
):
    other = 1 - lax.axis_index("rhs")
    count = lax.axis_size("space")
    leaves = positions.shape[0] // 2
    parents = leaves // 8
    rhs = charges.shape[1]
    width = to_wave.shape[0]
    slots = send_leaf.shape[1]
    near = slots // 2
    held = leaves + parents
    list_len = leaf_pairs.shape[2]
    split = list_len // 2
    cap_l, cap_p = send_leaf.shape[2], send_parent.shape[2]
    table_rows = 2 * held + slots * (cap_l + cap_p)

    arrived_charges = swap_cores(charges)
    index_shape = jax.ShapeDtypeStruct((2 * held, 128), jnp.int32)
    first, second, leaf_ids, parent_ids, factors = pl.pallas_call(
        functools.partial(plan_kernel, 2 * held, split),
        out_shape=[
            index_shape,
            index_shape,
            jax.ShapeDtypeStruct(send_leaf.shape[1:], jnp.int32),
            jax.ShapeDtypeStruct(send_parent.shape[1:], jnp.int32),
            jax.ShapeDtypeStruct(translation.shape, F32),
        ],
        in_specs=[HBM] * 5,
        out_specs=[VMEM] * 5,
        scratch_shapes=[
            pltpu.VMEM((list_len, 2, leaves), jnp.int32),
            pltpu.VMEM((parents, 2, list_len), jnp.int32),
            pltpu.SemaphoreType.DMA((5,)),
        ],
        compiler_params=pltpu.CompilerParams(vmem_limit_bytes=12 << 20),
        name="plan",
    )(
        *in_hbm(
            jnp.transpose(leaf_pairs, (2, 1, 0)), parent_pairs, send_leaf[0], send_parent[0],
            translation,
        )
    )
    arrived_charges, first, second, leaf_ids, parent_ids, factors = lax.optimization_barrier(
        (arrived_charges, first, second, leaf_ids, parent_ids, factors)
    )
    first, second = first.reshape(-1), second.reshape(-1)
    waves = pl.pallas_call(
        upward_kernel,
        out_shape=jax.ShapeDtypeStruct((held, 2 * rhs, width), BF16),
        in_specs=[HBM] * 7 + [VMEM],
        out_specs=VMEM,
        scratch_shapes=[
            pltpu.VMEM((3, width // 2, positions.shape[2]), F32),
            pltpu.VMEM((leaves, 2 * rhs, width), BF16),
            pltpu.VMEM((8, parents, 2 * rhs, width), BF16),
            pltpu.VMEM((2 * LEAF_UNROLL, width, positions.shape[2]), BF16),
            pltpu.SMEM(point_counts.shape, jnp.int32),
            pltpu.SMEM(octants.shape, jnp.int32),
            pltpu.VMEM(frequencies.shape, F32),
            pltpu.VMEM((3, leaves, positions.shape[2]), F32),
            pltpu.VMEM((leaves,) + charges.shape[1:], BF16),
            pltpu.VMEM(child_shift.shape, BF16),
            pltpu.VMEM(to_wave.shape, BF16),
            pltpu.SemaphoreType.DMA((7,)),
        ],
        compiler_params=pltpu.CompilerParams(vmem_limit_bytes=12 << 20),
        name="upward",
    )(
        *in_hbm(
            point_counts, octants, frequencies, jnp.transpose(positions, (1, 0, 2)), charges,
            child_shift, to_wave,
        ),
        arrived_charges,
    )
    arrived_waves = swap_cores(waves)
    rows, *sent = pl.pallas_call(
        pack_kernel,
        out_shape=[jax.ShapeDtypeStruct((2 * held, 2 * rhs, width), BF16)]
        + [jax.ShapeDtypeStruct((cap_l + cap_p, 2 * rhs, width), BF16)] * near,
        in_specs=[SMEM] * 2 + [VMEM] * 2,
        out_specs=[VMEM] * (1 + near),
        compiler_params=pltpu.CompilerParams(vmem_limit_bytes=12 << 20),
        name="pack",
    )(leaf_ids, parent_ids, waves, arrived_waves)
    def slot_permutation(k):
        pairs = []
        for core, offset in ((0, k - near), (1, k + 1)):
            pairs += [(2 * e + core, 2 * ((e + offset) % count) + core) for e in range(count)]
        return pairs

    near_own = [
        lax.ppermute(part, ("space", "rhs"), slot_permutation(k)) for k, part in enumerate(sent)
    ]
    index_scr = pltpu.SMEM((held * 256,), jnp.int32)
    index_sems = pltpu.SemaphoreType.DMA((held // TARGET_GROUP,))
    table_shape = jax.ShapeDtypeStruct((table_rows * 16, width // 2), F32)
    factor_shape = jax.ShapeDtypeStruct((translation.shape[0] * 16, width // 2), F32)
    acc_shape = jax.ShapeDtypeStruct((held, 16, width // 2), F32)
    table, factor, acc = pl.pallas_call(
        functools.partial(near_kernel, split),
        out_shape=[table_shape, factor_shape, acc_shape],
        in_specs=[ANY, VMEM, VMEM],
        out_specs=[VMEM] * 3,
        scratch_shapes=[index_scr, index_sems],
        cost_estimate=pl.CostEstimate(
            flops=20_000_000_000, bytes_accessed=60_000_000, transcendentals=0
        ),
        compiler_params=pltpu.CompilerParams(vmem_limit_bytes=20 << 20),
        name="near",
    )(first, rows, factors)
    *near_own, acc = lax.optimization_barrier((*near_own, acc))
    near_recv = [swap_cores(part) for part in near_own]
    _, keep, send, _ = pl.pallas_call(
        functools.partial(
            rest_kernel, (slots, cap_l, cap_p, 2 * held, split, list_len, count)
        ),
        out_shape=[acc_shape]
        + [jax.ShapeDtypeStruct((held, rhs, width), BF16)] * 2
        + [table_shape],
        in_specs=[ANY] * 2 + [VMEM] * (3 + slots),
        out_specs=[VMEM] * 4,
        scratch_shapes=[
            index_scr,
            pltpu.SMEM((256,), jnp.int32),
            index_sems,
            pltpu.SemaphoreType.DMA,
        ],
        input_output_aliases={2: 3, 4 + slots: 0},
        compiler_params=pltpu.CompilerParams(vmem_limit_bytes=20 << 20),
        name="rest",
    )(first, second, table, factor, *near_own, *near_recv, acc)
    arrived = swap_cores(send)
    return tuple(
        pl.pallas_call(
            functools.partial(local_kernel, leaves),
            out_shape=[
                jax.ShapeDtypeStruct((2 * leaves, rhs, width), F32),
                jax.ShapeDtypeStruct((2 * parents, rhs, width), F32),
            ],
            in_specs=[VMEM] * 3,
            out_specs=[VMEM] * 2,
            compiler_params=pltpu.CompilerParams(vmem_limit_bytes=12 << 20),
        name="local",
        )(keep, arrived, to_local)
    )


def solution(mesh):
    in_specs = (
        P("space", None, None), P("space"), P("space", "rhs", None), P(), P("space"), P(), P(), P(),
        P(), P("space", None, None), P("space", None, None), P("space", None, None),
        P("space", None, None),
    )
    out_specs = (P("space", "rhs", None), P("space", "rhs", None))
    return jax.shard_map(shards, mesh=mesh, in_specs=in_specs, out_specs=out_specs, check_vma=False)
```

```python
import functools
import math

import jax
import jax.numpy as jnp
from jax import lax
from jax.experimental import pallas as pl
from jax.experimental.pallas import tpu as pltpu
from jax.sharding import PartitionSpec as P

F32 = jnp.float32
BF16 = jnp.bfloat16
GROUP = 9
LEAF_UNROLL = 16
TARGET_GROUP = 16
SIN_POLY = (4.44286790342698, -7.307443431653506, 3.594788153158899, -0.7843741906863176)
COS_POLY = (
    1.4142134967586113,
    -6.978850998632011,
    5.7394613208713325,
    -1.883563790130787,
    0.31069962133630835,
)

VMEM = pl.BlockSpec(memory_space=pltpu.VMEM)
SMEM = pl.BlockSpec(memory_space=pltpu.SMEM)
ANY = pl.BlockSpec(memory_space=pl.ANY)
HBM = pl.BlockSpec(memory_space=pltpu.HBM)


def in_hbm(*values):
    return [pltpu.with_memory_space_constraint(value, pltpu.HBM) for value in values]


def swap_cores(value):
    return lax.ppermute(value, "rhs", [(0, 1), (1, 0)])


def horner(coefficients, x):
    total = coefficients[-1] * x + coefficients[-2]
    for coefficient in coefficients[-3::-1]:
        total = total * x + coefficient
    return total


def tree(values):
    values = list(values)
    while len(values) > 1:
        paired = [values[i] + values[i + 1] for i in range(0, len(values) - 1, 2)]
        values = paired + values[2 * len(paired) :]
    return values[0]


def sin_cos_turns(turns):
    r = turns - jnp.round(turns)
    r2 = r * r
    s = r * horner(SIN_POLY, r2)
    c = horner(COS_POLY, r2)
    return s * c, 1.0 - s * s


def upward_kernel(
    counts_ref, octants_ref, freq_ref, pos_ref, own_ref, recv_ref, shift_hbm, wave_mat_hbm,
    out_ref, freq_scr, mult_scr, child_scr, shift_ref, wave_mat_ref, sems,
):
    core = lax.axis_index("rhs")
    leaves, rhs_half, slots = own_ref.shape
    nodes = freq_ref.shape[1]
    base = core * leaves
    copies = [
        pltpu.make_async_copy(wave_mat_hbm, wave_mat_ref, sems.at[0]),
        pltpu.make_async_copy(shift_hbm, shift_ref, sems.at[1]),
    ]
    for copy in copies:
        copy.start()
    for d in range(3):
        row = freq_ref[d : d + 1, :] * (1.0 / (2.0 * math.pi))
        freq_scr[d] = jnp.broadcast_to(row, (slots, nodes)).T
    lane = lax.broadcasted_iota(jnp.int32, (2 * rhs_half, slots), 1)

    def one_leaf(b):
        own, recv = own_ref[b].astype(F32), recv_ref[base + b].astype(F32)
        lower = jnp.where(core == 0, own, recv)
        upper = jnp.where(core == 0, recv, own)
        charge = jnp.concatenate([lower, upper], axis=0)
        charge = jnp.where(lane < counts_ref[base + b], charge, 0.0).astype(BF16)
        xs = [jnp.broadcast_to(pos_ref[d, pl.ds(b, 1), :], (nodes, slots)) for d in range(3)]
        turns = freq_scr[0] * xs[0] + freq_scr[1] * xs[1] + freq_scr[2] * xs[2]
        sin, cos = sin_cos_turns(turns)
        basis = jnp.concatenate([cos.astype(BF16), sin.astype(BF16)], axis=0)
        multipole = lax.dot_general(
            charge, basis, (((1,), (1,)), ((), ())), preferred_element_type=F32
        ).astype(BF16)
        mult_scr[b] = multipole
        child_scr[octants_ref[base + b], b // 8] = multipole

    def step(g, carry):
        for k in range(LEAF_UNROLL):
            one_leaf(g * LEAF_UNROLL + k)
        return carry

    lax.fori_loop(0, leaves // LEAF_UNROLL, step, 0)
    for copy in copies:
        copy.wait()
    parents = leaves // 8
    rhs, width = mult_scr.shape[1:]
    wave_mat = wave_mat_ref[...]
    multipoles = mult_scr[...].reshape(leaves * rhs, width)
    waves = jnp.dot(multipoles, wave_mat, preferred_element_type=F32).astype(BF16)
    out_ref[:leaves] = waves.reshape(leaves, rhs, width)
    summed = None
    for octant in range(8):
        part = jnp.dot(
            child_scr[octant].reshape(parents * rhs, width),
            shift_ref[octant],
            preferred_element_type=F32,
        )
        summed = part if summed is None else summed + part
    parent_waves = jnp.dot(summed.astype(BF16), wave_mat, preferred_element_type=F32)
    out_ref[leaves:] = parent_waves.astype(BF16).reshape(parents, rhs, width)


def plan_kernel(
    local_rows, split, leaf_hbm, parent_hbm, send_leaf_hbm, send_parent_hbm, trans_hbm,
    counts_hbm, octants_hbm, freq_hbm, pos_hbm, own_hbm,
    first_out, second_out, send_leaf_out, send_parent_out, trans_out,
    counts_out, octants_out, freq_out, pos_out, own_out, leaf_ref, parent_ref, sems,
):
    core = lax.axis_index("rhs")
    list_len, _, leaves = leaf_ref.shape
    parents = parent_ref.shape[0]
    targets = leaves + parents
    lanes = pl.ds(pl.multiple_of(core * leaves, leaves), leaves)
    copies = [
        pltpu.make_async_copy(leaf_hbm.at[:, :, lanes], leaf_ref, sems.at[0]),
        pltpu.make_async_copy(parent_hbm.at[pl.ds(core * parents, parents)], parent_ref, sems.at[1]),
        pltpu.make_async_copy(send_leaf_hbm, send_leaf_out, sems.at[2]),
        pltpu.make_async_copy(send_parent_hbm, send_parent_out, sems.at[3]),
        pltpu.make_async_copy(trans_hbm, trans_out, sems.at[4]),
        pltpu.make_async_copy(counts_hbm, counts_out, sems.at[5]),
        pltpu.make_async_copy(octants_hbm, octants_out, sems.at[6]),
        pltpu.make_async_copy(freq_hbm, freq_out, sems.at[7]),
        pltpu.make_async_copy(pos_hbm.at[:, lanes, :], pos_out, sems.at[8]),
        pltpu.make_async_copy(own_hbm.at[lanes], own_out, sems.at[9]),
    ]
    for copy in copies:
        copy.start()
    for copy in copies[:2]:
        copy.wait()
    depth = -(-list_len // 8) * 8

    def packed(source, shift):
        return source + shift * (1 << 10)

    leaf_words = packed(leaf_ref[:, 0, :], leaf_ref[:, 1, :])
    parent_words = packed(parent_ref[:, 0, :], parent_ref[:, 1, :])
    parent_words = jnp.concatenate(
        [parent_words, jnp.zeros((parents, 256 - list_len), jnp.int32)], axis=1
    )
    parent_words = jnp.concatenate(
        [parent_words, jnp.zeros((128 - parents, 256), jnp.int32)], axis=0
    ).T[:depth]
    leaf_words = jnp.concatenate(
        [leaf_words, jnp.zeros((depth - list_len, leaves), jnp.int32)], axis=0
    )
    words = jnp.concatenate([leaf_words, parent_words], axis=1)
    row = lax.broadcasted_iota(jnp.int32, words.shape, 0)
    local = ((words & 1023) < local_rows) & (row < list_len)
    below = lax.broadcasted_iota(jnp.int32, (depth, depth), 0) >= lax.broadcasted_iota(
        jnp.int32, (depth, depth), 1
    )
    running = jnp.dot(
        jnp.where(below, 1.0, 0.0).astype(BF16),
        jnp.where(local, 1.0, 0.0).astype(BF16),
        preferred_element_type=F32,
    ).astype(jnp.int32)
    total = running[depth - 1 :]
    front = jnp.where(local, words + (row + 1 - running) * (1 << 20), 0)
    back = jnp.where(local, 0, words + (total - running) * (1 << 20))
    for k in range(8):
        bit = 1 << (20 + k)
        step = 1 << k
        moved = pltpu.roll(front, depth - step, 0)
        front = jnp.where((moved & bit) != 0, moved, jnp.where((front & bit) != 0, 0, front))
        moved = pltpu.roll(back, step, 0)
        back = jnp.where((moved & bit) != 0, moved, jnp.where((back & bit) != 0, 0, back))
    words = front + back
    sources = (words & 1023) * 16
    classes = (lax.shift_right_logical(words, 10) & 1023) * 16
    ready = (total >= split).astype(jnp.int32)
    for h, values in enumerate((sources, classes)):
        head = jnp.where(row[:128] == 127, ready, values[:128])
        tail = jnp.where(row[:128] == 127, ready, pltpu.roll(values, depth - split, 0)[:128])
        first_out[pl.ds(h, targets, stride=2), :] = head.T[:targets]
        second_out[pl.ds(h, targets, stride=2), :] = tail.T[:targets]
    for copy in copies[2:]:
        copy.wait()


def pack_kernel(leaf_ids_ref, parent_ids_ref, own_ref, recv_ref, *refs):
    core = lax.axis_index("rhs")
    rows_ref, outs = refs[0], refs[1:]
    cap_l, cap_p = leaf_ids_ref.shape[1], parent_ids_ref.shape[1]
    parents = rows_ref.shape[0] // 18
    leaves = 8 * parents
    for values, which in ((own_ref, core), (recv_ref, 1 - core)):
        rows_ref[pl.ds(which * leaves, leaves)] = values[:leaves]
        rows_ref[pl.ds(2 * leaves + which * parents, parents)] = values[leaves:]
    for j, out in enumerate(outs):
        slot = core * len(outs) + j
        for k in range(cap_l):
            out[k] = rows_ref[leaf_ids_ref[slot, k]]
        for k in range(cap_p):
            out[cap_l + k] = rows_ref[2 * leaves + parent_ids_ref[slot, k]]


def put_rows(table, source, at, count, base, valid=None):
    half = table.shape[1]

    def body(k, carry):
        value = source[at + k].astype(F32)
        if valid is not None:
            value = jnp.where(valid, value, 0.0)
        row = pl.multiple_of((base + k) * 16, 16)
        table[pl.ds(row, 8), :] = value[:, :half]
        table[pl.ds(pl.multiple_of(row + 8, 8), 8), :] = value[:, half:]
        return carry

    lax.fori_loop(0, count, body, 0, unroll=8)


def put_all_factors(factor, trans_ref):
    half = factor.shape[1]

    def put_factors(first, values):
        for k in range(values.shape[0]):
            row = pl.multiple_of((first + k) * 16, 16)
            factor[pl.ds(row, 8), :] = jnp.broadcast_to(values[k : k + 1, :half], (8, half))
            factor[pl.ds(pl.multiple_of(row + 8, 8), 8), :] = jnp.broadcast_to(
                values[k : k + 1, half:], (8, half)
            )

    def factor_block(g, carry):
        first = pl.multiple_of(g * 8, 8)
        put_factors(first, trans_ref[pl.ds(first, 8), :])
        return carry

    full = trans_ref.shape[0] // 8 * 8
    lax.fori_loop(0, full // 8, factor_block, 0)
    if full < trans_ref.shape[0]:
        put_factors(full, trans_ref[full:, :])


def pair_sums(index_ref, first, count, table, factor, total):
    total_re, total_im = total
    reals, imags = [], []
    for k in range(count):
        if k % GROUP == 0:
            span = min(GROUP, count - k)
            sources = index_ref.at[pl.ds(first + k, span)]
            classes = index_ref.at[pl.ds(first + 128 + k, span)]
        s = pl.multiple_of(sources[k % GROUP], 8)
        o = pl.multiple_of(classes[k % GROUP], 8)
        wave, shift = table.at[pl.ds(s, 16)], factor.at[pl.ds(o, 16)]
        wave_re, wave_im, shift_re, shift_im = wave[:8], wave[8:], shift[:8], shift[8:]
        reals.append(shift_re * wave_re - shift_im * wave_im)
        imags.append(shift_re * wave_im + shift_im * wave_re)
        if len(reals) == 3 or k == count - 1:
            total_re, total_im = total_re + tree(reals), total_im + tree(imags)
            reals, imags = [], []
    return total_re, total_im


def index_copy(index_hbm, index_scr, sems, group):
    words = TARGET_GROUP * 256
    span = pl.ds(pl.multiple_of(group * words, 1024), words)
    return pltpu.make_async_copy(index_hbm.at[span], index_scr.at[span], sems.at[group])


def start_indices(index):
    for group in range(2):
        index_copy(*index, group).start()


def over_targets(index, targets, one_target):
    def one_group(g, carry):
        @pl.when(g + 2 < targets // TARGET_GROUP)
        def _():
            index_copy(*index, g + 2).start()

        index_copy(*index, g).wait()
        return lax.fori_loop(
            0, TARGET_GROUP, lambda t, c: one_target(g * TARGET_GROUP + t, c), carry
        )

    lax.fori_loop(0, targets // TARGET_GROUP, one_group, 0)


def near_kernel(split, index_hbm, rows_ref, trans_ref, table, factor, acc_ref, index_scr, sems):
    index = (index_hbm, index_scr, sems)
    start_indices(index)
    put_rows(table, rows_ref, 0, rows_ref.shape[0], 0)
    put_all_factors(factor, trans_ref)
    zero = jnp.zeros((8, table.shape[1]), F32)

    def one_target(b, carry):
        @pl.when(index_scr[b * 256 + 127] > 0)
        def _():
            total = pair_sums(index_scr, b * 256, split, table, factor, (zero, zero))
            acc_ref[b, :8] = total[0]
            acc_ref[b, 8:] = total[1]

        return carry

    over_targets(index, acc_ref.shape[0], one_target)


def rest_kernel(dims, first_hbm, second_hbm, table_in, factor, *refs):
    slots, cap_l, cap_p, base, split, list_len, count = dims
    near = slots // 2
    near_own, near_recv = refs[:near], refs[near:slots]
    acc_ref, keep_ref, send_ref, table, index_scr, late_scr, sems, late_sem = refs[slots + 1 :]
    core = lax.axis_index("rhs")
    device = lax.axis_index("space")
    index = (second_hbm, index_scr, sems)
    start_indices(index)
    for k in range(near):
        for values, which in ((near_own[k], core), (near_recv[k], 1 - core)):
            slot = which * near + k
            sender = device - jnp.where(which == 0, k - near, k + 1)
            valid = (sender >= 0) & (sender < count)
            put_rows(table, values, 0, cap_l, base + slot * cap_l, valid)
            put_rows(table, values, cap_l, cap_p, base + slots * cap_l + slot * cap_p, valid)
    zero = jnp.zeros((8, table.shape[1]), F32)

    def one_target(b, carry):
        @pl.when(index_scr[b * 256 + 127] == 0)
        def _():
            span = pl.ds(pl.multiple_of(b * 256, 256), 256)
            copy = pltpu.make_async_copy(first_hbm.at[span], late_scr, late_sem)
            copy.start()
            copy.wait()
            total = pair_sums(late_scr, 0, split, table, factor, (zero, zero))
            acc_ref[b, :8] = total[0]
            acc_ref[b, 8:] = total[1]

        total = pair_sums(
            index_scr, b * 256, list_len - split, table, factor, (acc_ref[b, :8], acc_ref[b, 8:])
        )
        incoming = jnp.concatenate(total, axis=1)
        lower, upper = incoming[:4], incoming[4:]
        keep_ref[b] = jnp.where(core == 0, lower, upper).astype(BF16)
        send_ref[b] = jnp.where(core == 0, upper, lower).astype(BF16)
        return carry

    over_targets(index, keep_ref.shape[0], one_target)


def local_kernel(leaves, keep_ref, recv_ref, mat_ref, leaf_ref, parent_ref):
    core = lax.axis_index("rhs")
    parents = keep_ref.shape[0] - leaves
    rhs, width = keep_ref.shape[1:]
    for values, which in ((keep_ref, core), (recv_ref, 1 - core)):
        flat = values[...].reshape((leaves + parents) * rhs, width)
        local = jnp.dot(flat, mat_ref[...], preferred_element_type=F32)
        local = local.reshape(leaves + parents, rhs, width)
        leaf_ref[pl.ds(which * leaves, leaves)] = local[:leaves]
        parent_ref[pl.ds(which * parents, parents)] = local[leaves:]


def shards(
    positions, point_counts, charges, frequencies, octants, child_shift, to_wave, to_local,
    translation, send_leaf, send_parent, leaf_pairs, parent_pairs,
):
    other = 1 - lax.axis_index("rhs")
    count = lax.axis_size("space")
    leaves = positions.shape[0] // 2
    parents = leaves // 8
    rhs = charges.shape[1]
    width = to_wave.shape[0]
    slots = send_leaf.shape[1]
    near = slots // 2
    held = leaves + parents
    list_len = leaf_pairs.shape[2]
    split = list_len // 2
    cap_l, cap_p = send_leaf.shape[2], send_parent.shape[2]
    table_rows = 2 * held + slots * (cap_l + cap_p)

    arrived_charges = swap_cores(charges)
    index_shape = jax.ShapeDtypeStruct((2 * held, 128), jnp.int32)
    first, second, leaf_ids, parent_ids, factors, *early = pl.pallas_call(
        functools.partial(plan_kernel, 2 * held, split),
        out_shape=[
            index_shape,
            index_shape,
            jax.ShapeDtypeStruct(send_leaf.shape[1:], jnp.int32),
            jax.ShapeDtypeStruct(send_parent.shape[1:], jnp.int32),
            jax.ShapeDtypeStruct(translation.shape, F32),
            jax.ShapeDtypeStruct(point_counts.shape, jnp.int32),
            jax.ShapeDtypeStruct(octants.shape, jnp.int32),
            jax.ShapeDtypeStruct(frequencies.shape, F32),
            jax.ShapeDtypeStruct((3, leaves, positions.shape[2]), F32),
            jax.ShapeDtypeStruct((leaves,) + charges.shape[1:], BF16),
        ],
        in_specs=[HBM] * 10,
        out_specs=[VMEM] * 10,
        scratch_shapes=[
            pltpu.VMEM((list_len, 2, leaves), jnp.int32),
            pltpu.VMEM((parents, 2, list_len), jnp.int32),
            pltpu.SemaphoreType.DMA((10,)),
        ],
        compiler_params=pltpu.CompilerParams(vmem_limit_bytes=12 << 20),
        name="plan",
    )(
        *in_hbm(
            jnp.transpose(leaf_pairs, (2, 1, 0)), parent_pairs, send_leaf[0], send_parent[0],
            translation, point_counts, octants, frequencies,
            jnp.transpose(positions, (1, 0, 2)), charges,
        )
    )
    first, second = first.reshape(-1), second.reshape(-1)
    waves = pl.pallas_call(
        upward_kernel,
        out_shape=jax.ShapeDtypeStruct((held, 2 * rhs, width), BF16),
        in_specs=[SMEM] * 2 + [VMEM] * 4 + [HBM] * 2,
        out_specs=VMEM,
        scratch_shapes=[
            pltpu.VMEM((3, width // 2, positions.shape[2]), F32),
            pltpu.VMEM((leaves, 2 * rhs, width), BF16),
            pltpu.VMEM((8, parents, 2 * rhs, width), BF16),
            pltpu.VMEM(child_shift.shape, BF16),
            pltpu.VMEM(to_wave.shape, BF16),
            pltpu.SemaphoreType.DMA((2,)),
        ],
        compiler_params=pltpu.CompilerParams(vmem_limit_bytes=12 << 20),
        name="upward",
    )(
        *early, arrived_charges, *in_hbm(child_shift, to_wave)
    )
    arrived_waves = swap_cores(waves)
    rows, *sent = pl.pallas_call(
        pack_kernel,
        out_shape=[jax.ShapeDtypeStruct((2 * held, 2 * rhs, width), BF16)]
        + [jax.ShapeDtypeStruct((cap_l + cap_p, 2 * rhs, width), BF16)] * near,
        in_specs=[SMEM] * 2 + [VMEM] * 2,
        out_specs=[VMEM] * (1 + near),
        compiler_params=pltpu.CompilerParams(vmem_limit_bytes=12 << 20),
        name="pack",
    )(leaf_ids, parent_ids, waves, arrived_waves)
    def slot_permutation(k):
        pairs = []
        for core, offset in ((0, k - near), (1, k + 1)):
            pairs += [(2 * e + core, 2 * ((e + offset) % count) + core) for e in range(count)]
        return pairs

    near_own = [
        lax.ppermute(part, ("space", "rhs"), slot_permutation(k)) for k, part in enumerate(sent)
    ]
    index_scr = pltpu.SMEM((held * 256,), jnp.int32)
    index_sems = pltpu.SemaphoreType.DMA((held // TARGET_GROUP,))
    table_shape = jax.ShapeDtypeStruct((table_rows * 16, width // 2), F32)
    factor_shape = jax.ShapeDtypeStruct((translation.shape[0] * 16, width // 2), F32)
    acc_shape = jax.ShapeDtypeStruct((held, 16, width // 2), F32)
    table, factor, acc = pl.pallas_call(
        functools.partial(near_kernel, split),
        out_shape=[table_shape, factor_shape, acc_shape],
        in_specs=[ANY, VMEM, VMEM],
        out_specs=[VMEM] * 3,
        scratch_shapes=[index_scr, index_sems],
        cost_estimate=pl.CostEstimate(
            flops=20_000_000_000, bytes_accessed=60_000_000, transcendentals=0
        ),
        compiler_params=pltpu.CompilerParams(vmem_limit_bytes=20 << 20),
        name="near",
    )(first, rows, factors)
    *near_own, acc = lax.optimization_barrier((*near_own, acc))
    near_recv = [swap_cores(part) for part in near_own]
    _, keep, send, _ = pl.pallas_call(
        functools.partial(
            rest_kernel, (slots, cap_l, cap_p, 2 * held, split, list_len, count)
        ),
        out_shape=[acc_shape]
        + [jax.ShapeDtypeStruct((held, rhs, width), BF16)] * 2
        + [table_shape],
        in_specs=[ANY] * 2 + [VMEM] * (3 + slots),
        out_specs=[VMEM] * 4,
        scratch_shapes=[
            index_scr,
            pltpu.SMEM((256,), jnp.int32),
            index_sems,
            pltpu.SemaphoreType.DMA,
        ],
        input_output_aliases={2: 3, 4 + slots: 0},
        compiler_params=pltpu.CompilerParams(vmem_limit_bytes=20 << 20),
        name="rest",
    )(first, second, table, factor, *near_own, *near_recv, acc)
    arrived = swap_cores(send)
    return tuple(
        pl.pallas_call(
            functools.partial(local_kernel, leaves),
            out_shape=[
                jax.ShapeDtypeStruct((2 * leaves, rhs, width), F32),
                jax.ShapeDtypeStruct((2 * parents, rhs, width), F32),
            ],
            in_specs=[VMEM] * 3,
            out_specs=[VMEM] * 2,
            compiler_params=pltpu.CompilerParams(vmem_limit_bytes=12 << 20),
        name="local",
        )(keep, arrived, to_local)
    )


def solution(mesh):
    in_specs = (
        P("space", None, None), P("space"), P("space", "rhs", None), P(), P("space"), P(), P(), P(),
        P(), P("space", None, None), P("space", None, None), P("space", None, None),
        P("space", None, None),
    )
    out_specs = (P("space", "rhs", None), P("space", "rhs", None))
    return jax.shard_map(shards, mesh=mesh, in_specs=in_specs, out_specs=out_specs, check_vma=False)
```

```python
import functools
import math

import jax
import jax.numpy as jnp
from jax import lax
from jax.experimental import pallas as pl
from jax.experimental.pallas import tpu as pltpu
from jax.sharding import PartitionSpec as P

F32 = jnp.float32
BF16 = jnp.bfloat16
GROUP = 9
LEAF_UNROLL = 32
TARGET_GROUP = 16
SIN_POLY = (4.44286790342698, -7.307443431653506, 3.594788153158899, -0.7843741906863176)
COS_POLY = (
    1.4142134967586113,
    -6.978850998632011,
    5.7394613208713325,
    -1.883563790130787,
    0.31069962133630835,
)

VMEM = pl.BlockSpec(memory_space=pltpu.VMEM)
SMEM = pl.BlockSpec(memory_space=pltpu.SMEM)
ANY = pl.BlockSpec(memory_space=pl.ANY)
HBM = pl.BlockSpec(memory_space=pltpu.HBM)


def in_hbm(*values):
    return [pltpu.with_memory_space_constraint(value, pltpu.HBM) for value in values]


def swap_cores(value):
    return lax.ppermute(value, "rhs", [(0, 1), (1, 0)])


def horner(coefficients, x):
    total = coefficients[-1] * x + coefficients[-2]
    for coefficient in coefficients[-3::-1]:
        total = total * x + coefficient
    return total


def tree(values):
    values = list(values)
    while len(values) > 1:
        paired = [values[i] + values[i + 1] for i in range(0, len(values) - 1, 2)]
        values = paired + values[2 * len(paired) :]
    return values[0]


def sin_cos_turns(turns):
    r = turns - jnp.round(turns)
    r2 = r * r
    s = r * horner(SIN_POLY, r2)
    c = horner(COS_POLY, r2)
    return s * c, 1.0 - s * s


def upward_kernel(
    counts_ref, octants_ref, freq_ref, pos_ref, own_ref, recv_ref, shift_hbm, wave_mat_hbm,
    out_ref, freq_scr, mult_scr, child_scr, shift_ref, wave_mat_ref, sems,
):
    core = lax.axis_index("rhs")
    leaves, rhs_half, slots = own_ref.shape
    nodes = freq_ref.shape[1]
    base = core * leaves
    copies = [
        pltpu.make_async_copy(wave_mat_hbm, wave_mat_ref, sems.at[0]),
        pltpu.make_async_copy(shift_hbm, shift_ref, sems.at[1]),
    ]
    for copy in copies:
        copy.start()
    for d in range(3):
        row = freq_ref[d : d + 1, :] * (1.0 / (2.0 * math.pi))
        freq_scr[d] = jnp.broadcast_to(row, (slots, nodes)).T
    lane = lax.broadcasted_iota(jnp.int32, (2 * rhs_half, slots), 1)

    def one_leaf(b):
        own, recv = own_ref[b].astype(F32), recv_ref[base + b].astype(F32)
        lower = jnp.where(core == 0, own, recv)
        upper = jnp.where(core == 0, recv, own)
        charge = jnp.concatenate([lower, upper], axis=0)
        charge = jnp.where(lane < counts_ref[base + b], charge, 0.0).astype(BF16)
        xs = [jnp.broadcast_to(pos_ref[d, pl.ds(b, 1), :], (nodes, slots)) for d in range(3)]
        turns = freq_scr[0] * xs[0] + freq_scr[1] * xs[1] + freq_scr[2] * xs[2]
        sin, cos = sin_cos_turns(turns)
        basis = jnp.concatenate([cos.astype(BF16), sin.astype(BF16)], axis=0)
        multipole = lax.dot_general(
            charge, basis, (((1,), (1,)), ((), ())), preferred_element_type=F32
        ).astype(BF16)
        mult_scr[b] = multipole
        child_scr[octants_ref[base + b], b // 8] = multipole

    def step(g, carry):
        for k in range(LEAF_UNROLL):
            one_leaf(g * LEAF_UNROLL + k)
        return carry

    lax.fori_loop(0, leaves // LEAF_UNROLL, step, 0)
    for copy in copies:
        copy.wait()
    parents = leaves // 8
    rhs, width = mult_scr.shape[1:]
    wave_mat = wave_mat_ref[...]
    multipoles = mult_scr[...].reshape(leaves * rhs, width)
    waves = jnp.dot(multipoles, wave_mat, preferred_element_type=F32).astype(BF16)
    out_ref[:leaves] = waves.reshape(leaves, rhs, width)
    summed = None
    for octant in range(8):
        part = jnp.dot(
            child_scr[octant].reshape(parents * rhs, width),
            shift_ref[octant],
            preferred_element_type=F32,
        )
        summed = part if summed is None else summed + part
    parent_waves = jnp.dot(summed.astype(BF16), wave_mat, preferred_element_type=F32)
    out_ref[leaves:] = parent_waves.astype(BF16).reshape(parents, rhs, width)


def fetch_kernel(*refs):
    count = (len(refs) - 1) // 2
    sources, targets, sems = refs[:count], refs[count:-1], refs[-1]
    core = lax.axis_index("rhs")
    leaves, parents = targets[0].shape[2], targets[1].shape[0]
    half = pl.ds(pl.multiple_of(core * leaves, leaves), leaves)
    views = [
        sources[0].at[:, :, half],
        sources[1].at[pl.ds(core * parents, parents)],
        sources[2].at[:, half, :],
        sources[3].at[half],
        *sources[4:],
    ]
    copies = [
        pltpu.make_async_copy(view, target, sems.at[i])
        for i, (view, target) in enumerate(zip(views, targets))
    ]
    for copy in copies:
        copy.start()
    for copy in copies:
        copy.wait()


def plan_kernel(local_rows, split, leaf_ref, parent_ref, first_out, second_out):
    list_len, _, leaves = leaf_ref.shape
    parents = parent_ref.shape[0]
    targets = leaves + parents
    depth = -(-list_len // 8) * 8

    def packed(source, shift):
        return source + shift * (1 << 10)

    leaf_words = packed(leaf_ref[:, 0, :], leaf_ref[:, 1, :])
    parent_words = packed(parent_ref[:, 0, :], parent_ref[:, 1, :])
    parent_words = jnp.concatenate(
        [parent_words, jnp.zeros((parents, 256 - list_len), jnp.int32)], axis=1
    )
    parent_words = jnp.concatenate(
        [parent_words, jnp.zeros((128 - parents, 256), jnp.int32)], axis=0
    ).T[:depth]
    leaf_words = jnp.concatenate(
        [leaf_words, jnp.zeros((depth - list_len, leaves), jnp.int32)], axis=0
    )
    words = jnp.concatenate([leaf_words, parent_words], axis=1)
    row = lax.broadcasted_iota(jnp.int32, words.shape, 0)
    local = ((words & 1023) < local_rows) & (row < list_len)
    below = lax.broadcasted_iota(jnp.int32, (depth, depth), 0) >= lax.broadcasted_iota(
        jnp.int32, (depth, depth), 1
    )
    running = jnp.dot(
        jnp.where(below, 1.0, 0.0).astype(BF16),
        jnp.where(local, 1.0, 0.0).astype(BF16),
        preferred_element_type=F32,
    ).astype(jnp.int32)
    total = running[depth - 1 :]
    front = jnp.where(local, words + (row + 1 - running) * (1 << 20), 0)
    back = jnp.where(local, 0, words + (total - running) * (1 << 20))
    for k in range(8):
        bit = 1 << (20 + k)
        step = 1 << k
        moved = pltpu.roll(front, depth - step, 0)
        front = jnp.where((moved & bit) != 0, moved, jnp.where((front & bit) != 0, 0, front))
        moved = pltpu.roll(back, step, 0)
        back = jnp.where((moved & bit) != 0, moved, jnp.where((back & bit) != 0, 0, back))
    words = front + back
    sources = (words & 1023) * 16
    classes = (lax.shift_right_logical(words, 10) & 1023) * 16
    ready = (total >= split).astype(jnp.int32)
    for h, values in enumerate((sources, classes)):
        head = jnp.where(row[:128] == 127, ready, values[:128])
        tail = jnp.where(row[:128] == 127, ready, pltpu.roll(values, depth - split, 0)[:128])
        first_out[pl.ds(h, targets, stride=2), :] = head.T[:targets]
        second_out[pl.ds(h, targets, stride=2), :] = tail.T[:targets]


def pack_kernel(leaf_ids_ref, parent_ids_ref, own_ref, recv_ref, *refs):
    core = lax.axis_index("rhs")
    rows_ref, outs = refs[0], refs[1:]
    cap_l, cap_p = leaf_ids_ref.shape[1], parent_ids_ref.shape[1]
    parents = rows_ref.shape[0] // 18
    leaves = 8 * parents
    for values, which in ((own_ref, core), (recv_ref, 1 - core)):
        rows_ref[pl.ds(which * leaves, leaves)] = values[:leaves]
        rows_ref[pl.ds(2 * leaves + which * parents, parents)] = values[leaves:]
    for j, out in enumerate(outs):
        slot = core * len(outs) + j
        for k in range(cap_l):
            out[k] = rows_ref[leaf_ids_ref[slot, k]]
        for k in range(cap_p):
            out[cap_l + k] = rows_ref[2 * leaves + parent_ids_ref[slot, k]]


def put_rows(table, source, at, count, base, valid=None):
    half = table.shape[1]

    def body(k, carry):
        value = source[at + k].astype(F32)
        if valid is not None:
            value = jnp.where(valid, value, 0.0)
        row = pl.multiple_of((base + k) * 16, 16)
        table[pl.ds(row, 8), :] = value[:, :half]
        table[pl.ds(pl.multiple_of(row + 8, 8), 8), :] = value[:, half:]
        return carry

    lax.fori_loop(0, count, body, 0, unroll=8)


def put_all_factors(factor, trans_ref):
    half = factor.shape[1]

    def put_factors(first, values):
        for k in range(values.shape[0]):
            row = pl.multiple_of((first + k) * 16, 16)
            factor[pl.ds(row, 8), :] = jnp.broadcast_to(values[k : k + 1, :half], (8, half))
            factor[pl.ds(pl.multiple_of(row + 8, 8), 8), :] = jnp.broadcast_to(
                values[k : k + 1, half:], (8, half)
            )

    def factor_block(g, carry):
        first = pl.multiple_of(g * 8, 8)
        put_factors(first, trans_ref[pl.ds(first, 8), :])
        return carry

    full = trans_ref.shape[0] // 8 * 8
    lax.fori_loop(0, full // 8, factor_block, 0)
    if full < trans_ref.shape[0]:
        put_factors(full, trans_ref[full:, :])


def pair_sums(index_ref, first, count, table, factor, total):
    total_re, total_im = total
    reals, imags = [], []
    for k in range(count):
        if k % GROUP == 0:
            span = min(GROUP, count - k)
            sources = index_ref.at[pl.ds(first + k, span)]
            classes = index_ref.at[pl.ds(first + 128 + k, span)]
        s = pl.multiple_of(sources[k % GROUP], 8)
        o = pl.multiple_of(classes[k % GROUP], 8)
        wave, shift = table.at[pl.ds(s, 16)], factor.at[pl.ds(o, 16)]
        wave_re, wave_im, shift_re, shift_im = wave[:8], wave[8:], shift[:8], shift[8:]
        reals.append(shift_re * wave_re - shift_im * wave_im)
        imags.append(shift_re * wave_im + shift_im * wave_re)
        if len(reals) == 3 or k == count - 1:
            total_re, total_im = total_re + tree(reals), total_im + tree(imags)
            reals, imags = [], []
    return total_re, total_im


def index_copy(index_hbm, index_scr, sems, group):
    words = TARGET_GROUP * 256
    span = pl.ds(pl.multiple_of(group * words, 1024), words)
    return pltpu.make_async_copy(index_hbm.at[span], index_scr.at[span], sems.at[group])


def start_indices(index):
    for group in range(2):
        index_copy(*index, group).start()


def over_targets(index, targets, one_target):
    def one_group(g, carry):
        @pl.when(g + 2 < targets // TARGET_GROUP)
        def _():
            index_copy(*index, g + 2).start()

        index_copy(*index, g).wait()
        return lax.fori_loop(
            0, TARGET_GROUP, lambda t, c: one_target(g * TARGET_GROUP + t, c), carry
        )

    lax.fori_loop(0, targets // TARGET_GROUP, one_group, 0)


def near_kernel(split, index_hbm, rows_ref, trans_ref, table, factor, acc_ref, index_scr, sems):
    index = (index_hbm, index_scr, sems)
    start_indices(index)
    put_rows(table, rows_ref, 0, rows_ref.shape[0], 0)
    put_all_factors(factor, trans_ref)
    zero = jnp.zeros((8, table.shape[1]), F32)

    def one_target(b, carry):
        @pl.when(index_scr[b * 256 + 127] > 0)
        def _():
            total = pair_sums(index_scr, b * 256, split, table, factor, (zero, zero))
            acc_ref[b, :8] = total[0]
            acc_ref[b, 8:] = total[1]

        return carry

    over_targets(index, acc_ref.shape[0], one_target)


def rest_kernel(dims, first_hbm, second_hbm, table_in, factor, *refs):
    slots, cap_l, cap_p, base, split, list_len, count = dims
    near = slots // 2
    near_own, near_recv = refs[:near], refs[near:slots]
    acc_ref, keep_ref, send_ref, table, index_scr, late_scr, sems, late_sem = refs[slots + 1 :]
    core = lax.axis_index("rhs")
    device = lax.axis_index("space")
    index = (second_hbm, index_scr, sems)
    start_indices(index)
    for k in range(near):
        for values, which in ((near_own[k], core), (near_recv[k], 1 - core)):
            slot = which * near + k
            sender = device - jnp.where(which == 0, k - near, k + 1)
            valid = (sender >= 0) & (sender < count)
            put_rows(table, values, 0, cap_l, base + slot * cap_l, valid)
            put_rows(table, values, cap_l, cap_p, base + slots * cap_l + slot * cap_p, valid)
    zero = jnp.zeros((8, table.shape[1]), F32)

    def one_target(b, carry):
        @pl.when(index_scr[b * 256 + 127] == 0)
        def _():
            span = pl.ds(pl.multiple_of(b * 256, 256), 256)
            copy = pltpu.make_async_copy(first_hbm.at[span], late_scr, late_sem)
            copy.start()
            copy.wait()
            total = pair_sums(late_scr, 0, split, table, factor, (zero, zero))
            acc_ref[b, :8] = total[0]
            acc_ref[b, 8:] = total[1]

        total = pair_sums(
            index_scr, b * 256, list_len - split, table, factor, (acc_ref[b, :8], acc_ref[b, 8:])
        )
        incoming = jnp.concatenate(total, axis=1)
        lower, upper = incoming[:4], incoming[4:]
        keep_ref[b] = jnp.where(core == 0, lower, upper).astype(BF16)
        send_ref[b] = jnp.where(core == 0, upper, lower).astype(BF16)
        return carry

    over_targets(index, keep_ref.shape[0], one_target)


def local_kernel(leaves, keep_ref, recv_ref, mat_ref, leaf_ref, parent_ref):
    core = lax.axis_index("rhs")
    parents = keep_ref.shape[0] - leaves
    rhs, width = keep_ref.shape[1:]
    for values, which in ((keep_ref, core), (recv_ref, 1 - core)):
        flat = values[...].reshape((leaves + parents) * rhs, width)
        local = jnp.dot(flat, mat_ref[...], preferred_element_type=F32)
        local = local.reshape(leaves + parents, rhs, width)
        leaf_ref[pl.ds(which * leaves, leaves)] = local[:leaves]
        parent_ref[pl.ds(which * parents, parents)] = local[leaves:]


def shards(
    positions, point_counts, charges, frequencies, octants, child_shift, to_wave, to_local,
    translation, send_leaf, send_parent, leaf_pairs, parent_pairs,
):
    other = 1 - lax.axis_index("rhs")
    count = lax.axis_size("space")
    leaves = positions.shape[0] // 2
    parents = leaves // 8
    rhs = charges.shape[1]
    width = to_wave.shape[0]
    slots = send_leaf.shape[1]
    near = slots // 2
    held = leaves + parents
    list_len = leaf_pairs.shape[2]
    split = list_len // 2
    cap_l, cap_p = send_leaf.shape[2], send_parent.shape[2]
    table_rows = 2 * held + slots * (cap_l + cap_p)

    arrived_charges = swap_cores(charges)
    fetched = [
        (jnp.transpose(leaf_pairs, (2, 1, 0)), (list_len, 2, leaves)),
        (parent_pairs, (parents, 2, list_len)),
        (jnp.transpose(positions, (1, 0, 2)), (3, leaves, positions.shape[2])),
        (charges, (leaves,) + charges.shape[1:]),
    ]
    whole = (send_leaf[0], send_parent[0], translation, point_counts, octants, frequencies)
    fetched += [(value, value.shape) for value in whole]
    leaf_half, parent_half, pos_half, own_half, leaf_ids, parent_ids, factors, *early = pl.pallas_call(
        fetch_kernel,
        out_shape=[jax.ShapeDtypeStruct(shape, value.dtype) for value, shape in fetched],
        in_specs=[HBM] * len(fetched),
        out_specs=[VMEM] * len(fetched),
        scratch_shapes=[pltpu.SemaphoreType.DMA((len(fetched),))],
        compiler_params=pltpu.CompilerParams(vmem_limit_bytes=12 << 20),
        name="fetch",
    )(*in_hbm(*(value for value, _ in fetched)))
    waves = pl.pallas_call(
        upward_kernel,
        out_shape=jax.ShapeDtypeStruct((held, 2 * rhs, width), BF16),
        in_specs=[SMEM] * 2 + [VMEM] * 4 + [HBM] * 2,
        out_specs=VMEM,
        scratch_shapes=[
            pltpu.VMEM((3, width // 2, positions.shape[2]), F32),
            pltpu.VMEM((leaves, 2 * rhs, width), BF16),
            pltpu.VMEM((8, parents, 2 * rhs, width), BF16),
            pltpu.VMEM(child_shift.shape, BF16),
            pltpu.VMEM(to_wave.shape, BF16),
            pltpu.SemaphoreType.DMA((2,)),
        ],
        compiler_params=pltpu.CompilerParams(vmem_limit_bytes=12 << 20),
        name="upward",
    )(
        *early, pos_half, own_half, arrived_charges, *in_hbm(child_shift, to_wave)
    )
    arrived_waves = swap_cores(waves)
    waves, leaf_half, parent_half = lax.optimization_barrier((waves, leaf_half, parent_half))
    index_shape = jax.ShapeDtypeStruct((2 * held, 128), jnp.int32)
    first, second = pl.pallas_call(
        functools.partial(plan_kernel, 2 * held, split),
        out_shape=[index_shape] * 2,
        in_specs=[VMEM] * 2,
        out_specs=[VMEM] * 2,
        compiler_params=pltpu.CompilerParams(vmem_limit_bytes=12 << 20),
        name="plan",
    )(leaf_half, parent_half)
    arrived_waves, first, second = lax.optimization_barrier((arrived_waves, first, second))
    first, second = first.reshape(-1), second.reshape(-1)
    rows, *sent = pl.pallas_call(
        pack_kernel,
        out_shape=[jax.ShapeDtypeStruct((2 * held, 2 * rhs, width), BF16)]
        + [jax.ShapeDtypeStruct((cap_l + cap_p, 2 * rhs, width), BF16)] * near,
        in_specs=[SMEM] * 2 + [VMEM] * 2,
        out_specs=[VMEM] * (1 + near),
        compiler_params=pltpu.CompilerParams(vmem_limit_bytes=12 << 20),
        name="pack",
    )(leaf_ids, parent_ids, waves, arrived_waves)
    def slot_permutation(k):
        pairs = []
        for core, offset in ((0, k - near), (1, k + 1)):
            pairs += [(2 * e + core, 2 * ((e + offset) % count) + core) for e in range(count)]
        return pairs

    near_own = [
        lax.ppermute(part, ("space", "rhs"), slot_permutation(k)) for k, part in enumerate(sent)
    ]
    index_scr = pltpu.SMEM((held * 256,), jnp.int32)
    index_sems = pltpu.SemaphoreType.DMA((held // TARGET_GROUP,))
    table_shape = jax.ShapeDtypeStruct((table_rows * 16, width // 2), F32)
    factor_shape = jax.ShapeDtypeStruct((translation.shape[0] * 16, width // 2), F32)
    acc_shape = jax.ShapeDtypeStruct((held, 16, width // 2), F32)
    table, factor, acc = pl.pallas_call(
        functools.partial(near_kernel, split),
        out_shape=[table_shape, factor_shape, acc_shape],
        in_specs=[ANY, VMEM, VMEM],
        out_specs=[VMEM] * 3,
        scratch_shapes=[index_scr, index_sems],
        cost_estimate=pl.CostEstimate(
            flops=20_000_000_000, bytes_accessed=60_000_000, transcendentals=0
        ),
        compiler_params=pltpu.CompilerParams(vmem_limit_bytes=20 << 20),
        name="near",
    )(first, rows, factors)
    *near_own, acc = lax.optimization_barrier((*near_own, acc))
    near_recv = [swap_cores(part) for part in near_own]
    _, keep, send, _ = pl.pallas_call(
        functools.partial(
            rest_kernel, (slots, cap_l, cap_p, 2 * held, split, list_len, count)
        ),
        out_shape=[acc_shape]
        + [jax.ShapeDtypeStruct((held, rhs, width), BF16)] * 2
        + [table_shape],
        in_specs=[ANY] * 2 + [VMEM] * (3 + slots),
        out_specs=[VMEM] * 4,
        scratch_shapes=[
            index_scr,
            pltpu.SMEM((256,), jnp.int32),
            index_sems,
            pltpu.SemaphoreType.DMA,
        ],
        input_output_aliases={2: 3, 4 + slots: 0},
        compiler_params=pltpu.CompilerParams(vmem_limit_bytes=20 << 20),
        name="rest",
    )(first, second, table, factor, *near_own, *near_recv, acc)
    arrived = swap_cores(send)
    return tuple(
        pl.pallas_call(
            functools.partial(local_kernel, leaves),
            out_shape=[
                jax.ShapeDtypeStruct((2 * leaves, rhs, width), F32),
                jax.ShapeDtypeStruct((2 * parents, rhs, width), F32),
            ],
            in_specs=[VMEM] * 3,
            out_specs=[VMEM] * 2,
            compiler_params=pltpu.CompilerParams(vmem_limit_bytes=12 << 20),
        name="local",
        )(keep, arrived, to_local)
    )


def solution(mesh):
    in_specs = (
        P("space", None, None), P("space"), P("space", "rhs", None), P(), P("space"), P(), P(), P(),
        P(), P("space", None, None), P("space", None, None), P("space", None, None),
        P("space", None, None),
    )
    out_specs = (P("space", "rhs", None), P("space", "rhs", None))
    return jax.shard_map(shards, mesh=mesh, in_specs=in_specs, out_specs=out_specs, check_vma=False)
```

```python
import functools
import math

import jax
import jax.numpy as jnp
from jax import lax
from jax.experimental import pallas as pl
from jax.experimental.pallas import tpu as pltpu
from jax.sharding import PartitionSpec as P

F32 = jnp.float32
BF16 = jnp.bfloat16
GROUP = 9
LEAF_UNROLL = 32
TARGET_GROUP = 16
SIN_POLY = (4.44286790342698, -7.307443431653506, 3.594788153158899, -0.7843741906863176)
COS_POLY = (
    1.4142134967586113,
    -6.978850998632011,
    5.7394613208713325,
    -1.883563790130787,
    0.31069962133630835,
)

VMEM = pl.BlockSpec(memory_space=pltpu.VMEM)
SMEM = pl.BlockSpec(memory_space=pltpu.SMEM)
ANY = pl.BlockSpec(memory_space=pl.ANY)
HBM = pl.BlockSpec(memory_space=pltpu.HBM)


def in_hbm(*values):
    return [pltpu.with_memory_space_constraint(value, pltpu.HBM) for value in values]


def swap_cores(value):
    return lax.ppermute(value, "rhs", [(0, 1), (1, 0)])


def horner(coefficients, x):
    total = coefficients[-1] * x + coefficients[-2]
    for coefficient in coefficients[-3::-1]:
        total = total * x + coefficient
    return total


def tree(values):
    values = list(values)
    while len(values) > 1:
        paired = [values[i] + values[i + 1] for i in range(0, len(values) - 1, 2)]
        values = paired + values[2 * len(paired) :]
    return values[0]


def sin_cos_turns(turns):
    r = turns - jnp.round(turns)
    r2 = r * r
    s = r * horner(SIN_POLY, r2)
    c = horner(COS_POLY, r2)
    return s * c, 1.0 - s * s


def upward_kernel(
    counts_ref, octants_ref, freq_ref, pos_ref, own_ref, recv_ref, shift_hbm, wave_mat_hbm,
    out_ref, freq_scr, mult_scr, child_scr, shift_ref, wave_mat_ref, sems,
):
    core = lax.axis_index("rhs")
    leaves, rhs_half, slots = own_ref.shape
    nodes = freq_ref.shape[1]
    base = core * leaves
    copies = [
        pltpu.make_async_copy(wave_mat_hbm, wave_mat_ref, sems.at[0]),
        pltpu.make_async_copy(shift_hbm, shift_ref, sems.at[1]),
    ]
    for copy in copies:
        copy.start()
    for d in range(3):
        row = freq_ref[d : d + 1, :] * (1.0 / (2.0 * math.pi))
        freq_scr[d] = jnp.broadcast_to(row, (slots, nodes)).T
    lane = lax.broadcasted_iota(jnp.int32, (2 * rhs_half, slots), 1)

    def one_leaf(b):
        own, recv = own_ref[b].astype(F32), recv_ref[base + b].astype(F32)
        lower = jnp.where(core == 0, own, recv)
        upper = jnp.where(core == 0, recv, own)
        charge = jnp.concatenate([lower, upper], axis=0)
        charge = jnp.where(lane < counts_ref[base + b], charge, 0.0).astype(BF16)
        xs = [jnp.broadcast_to(pos_ref[d, pl.ds(b, 1), :], (nodes, slots)) for d in range(3)]
        turns = freq_scr[0] * xs[0] + freq_scr[1] * xs[1] + freq_scr[2] * xs[2]
        sin, cos = sin_cos_turns(turns)
        basis = jnp.concatenate([cos.astype(BF16), sin.astype(BF16)], axis=0)
        multipole = lax.dot_general(
            charge, basis, (((1,), (1,)), ((), ())), preferred_element_type=F32
        ).astype(BF16)
        mult_scr[b] = multipole
        child_scr[octants_ref[base + b], b // 8] = multipole

    def step(g, carry):
        for k in range(LEAF_UNROLL):
            one_leaf(g * LEAF_UNROLL + k)
        return carry

    lax.fori_loop(0, leaves // LEAF_UNROLL, step, 0)
    for copy in copies:
        copy.wait()
    parents = leaves // 8
    rhs, width = mult_scr.shape[1:]
    wave_mat = wave_mat_ref[...]
    multipoles = mult_scr[...].reshape(leaves * rhs, width)
    waves = jnp.dot(multipoles, wave_mat, preferred_element_type=F32).astype(BF16)
    out_ref[:leaves] = waves.reshape(leaves, rhs, width)
    summed = None
    for octant in range(8):
        part = jnp.dot(
            child_scr[octant].reshape(parents * rhs, width),
            shift_ref[octant],
            preferred_element_type=F32,
        )
        summed = part if summed is None else summed + part
    parent_waves = jnp.dot(summed.astype(BF16), wave_mat, preferred_element_type=F32)
    out_ref[leaves:] = parent_waves.astype(BF16).reshape(parents, rhs, width)


def fetch_kernel(*refs):
    count = (len(refs) - 1) // 2
    sources, targets, sems = refs[:count], refs[count:-1], refs[-1]
    core = lax.axis_index("rhs")
    leaves, parents = targets[0].shape[2], targets[1].shape[0]
    half = pl.ds(pl.multiple_of(core * leaves, leaves), leaves)
    views = [
        sources[0].at[:, :, half],
        sources[1].at[pl.ds(core * parents, parents)],
        sources[2].at[:, half, :],
        sources[3].at[half],
        *sources[4:],
    ]
    copies = [
        pltpu.make_async_copy(view, target, sems.at[i])
        for i, (view, target) in enumerate(zip(views, targets))
    ]
    for copy in copies:
        copy.start()
    for copy in copies:
        copy.wait()


def plan_kernel(local_rows, split, leaf_ref, parent_ref, first_out, second_out):
    list_len, _, leaves = leaf_ref.shape
    parents = parent_ref.shape[0]
    targets = leaves + parents
    depth = -(-list_len // 8) * 8

    def packed(source, shift):
        return source + shift * (1 << 10)

    leaf_words = packed(leaf_ref[:, 0, :], leaf_ref[:, 1, :])
    parent_words = packed(parent_ref[:, 0, :], parent_ref[:, 1, :])
    parent_words = jnp.concatenate(
        [parent_words, jnp.zeros((parents, 256 - list_len), jnp.int32)], axis=1
    )
    parent_words = jnp.concatenate(
        [parent_words, jnp.zeros((128 - parents, 256), jnp.int32)], axis=0
    ).T[:depth]
    leaf_words = jnp.concatenate(
        [leaf_words, jnp.zeros((depth - list_len, leaves), jnp.int32)], axis=0
    )
    words = jnp.concatenate([leaf_words, parent_words], axis=1)
    row = lax.broadcasted_iota(jnp.int32, words.shape, 0)
    local = ((words & 1023) < local_rows) & (row < list_len)
    below = lax.broadcasted_iota(jnp.int32, (depth, depth), 0) >= lax.broadcasted_iota(
        jnp.int32, (depth, depth), 1
    )
    running = jnp.dot(
        jnp.where(below, 1.0, 0.0).astype(BF16),
        jnp.where(local, 1.0, 0.0).astype(BF16),
        preferred_element_type=F32,
    ).astype(jnp.int32)
    total = running[depth - 1 :]
    front = jnp.where(local, words + (row + 1 - running) * (1 << 20), 0)
    back = jnp.where(local, 0, words + (total - running) * (1 << 20))
    for k in range(8):
        bit = 1 << (20 + k)
        step = 1 << k
        moved = pltpu.roll(front, depth - step, 0)
        front = jnp.where((moved & bit) != 0, moved, jnp.where((front & bit) != 0, 0, front))
        moved = pltpu.roll(back, step, 0)
        back = jnp.where((moved & bit) != 0, moved, jnp.where((back & bit) != 0, 0, back))
    words = front + back
    sources = (words & 1023) * 16
    classes = (lax.shift_right_logical(words, 10) & 1023) * 16
    ready = (total >= split).astype(jnp.int32)
    lane = lax.broadcasted_iota(jnp.int32, ready.shape, 1)
    late = jnp.max(jnp.where(lane < targets, 1 - ready, 0), axis=1, keepdims=True)
    for h, values in enumerate((sources, classes)):
        head = jnp.where(row[:128] == 127, ready, values[:128])
        tail = jnp.where(row[:128] == 127, late, pltpu.roll(values, depth - split, 0)[:128])
        first_out[pl.ds(h, targets, stride=2), :] = head.T[:targets]
        second_out[pl.ds(h, targets, stride=2), :] = tail.T[:targets]


def pack_kernel(leaf_ids_ref, parent_ids_ref, own_ref, recv_ref, *refs):
    core = lax.axis_index("rhs")
    rows_ref, outs = refs[0], refs[1:]
    cap_l, cap_p = leaf_ids_ref.shape[1], parent_ids_ref.shape[1]
    parents = rows_ref.shape[0] // 18
    leaves = 8 * parents
    for values, which in ((own_ref, core), (recv_ref, 1 - core)):
        rows_ref[pl.ds(which * leaves, leaves)] = values[:leaves]
        rows_ref[pl.ds(2 * leaves + which * parents, parents)] = values[leaves:]
    for j, out in enumerate(outs):
        slot = core * len(outs) + j
        for k in range(cap_l):
            out[k] = rows_ref[leaf_ids_ref[slot, k]]
        for k in range(cap_p):
            out[cap_l + k] = rows_ref[2 * leaves + parent_ids_ref[slot, k]]


def put_rows(table, source, at, count, base, valid=None):
    half = table.shape[1]

    def body(k, carry):
        value = source[at + k].astype(F32)
        if valid is not None:
            value = jnp.where(valid, value, 0.0)
        row = pl.multiple_of((base + k) * 16, 16)
        table[pl.ds(row, 8), :] = value[:, :half]
        table[pl.ds(pl.multiple_of(row + 8, 8), 8), :] = value[:, half:]
        return carry

    lax.fori_loop(0, count, body, 0, unroll=8)


def put_all_factors(factor, trans_ref):
    half = factor.shape[1]

    def put_factors(first, values):
        for k in range(values.shape[0]):
            row = pl.multiple_of((first + k) * 16, 16)
            factor[pl.ds(row, 8), :] = jnp.broadcast_to(values[k : k + 1, :half], (8, half))
            factor[pl.ds(pl.multiple_of(row + 8, 8), 8), :] = jnp.broadcast_to(
                values[k : k + 1, half:], (8, half)
            )

    def factor_block(g, carry):
        first = pl.multiple_of(g * 8, 8)
        put_factors(first, trans_ref[pl.ds(first, 8), :])
        return carry

    full = trans_ref.shape[0] // 8 * 8
    lax.fori_loop(0, full // 8, factor_block, 0)
    if full < trans_ref.shape[0]:
        put_factors(full, trans_ref[full:, :])


def pair_sums(index_ref, first, count, table, factor, total):
    total_re, total_im = total
    reals, imags = [], []
    for k in range(count):
        if k % GROUP == 0:
            span = min(GROUP, count - k)
            sources = index_ref.at[pl.ds(first + k, span)]
            classes = index_ref.at[pl.ds(first + 128 + k, span)]
        s = pl.multiple_of(sources[k % GROUP], 8)
        o = pl.multiple_of(classes[k % GROUP], 8)
        wave, shift = table.at[pl.ds(s, 16)], factor.at[pl.ds(o, 16)]
        wave_re, wave_im, shift_re, shift_im = wave[:8], wave[8:], shift[:8], shift[8:]
        reals.append(shift_re * wave_re - shift_im * wave_im)
        imags.append(shift_re * wave_im + shift_im * wave_re)
        if len(reals) == 3 or k == count - 1:
            total_re, total_im = total_re + tree(reals), total_im + tree(imags)
            reals, imags = [], []
    return total_re, total_im


def index_copy(index_hbm, index_scr, sems, group):
    words = TARGET_GROUP * 256
    span = pl.ds(pl.multiple_of(group * words, 1024), words)
    return pltpu.make_async_copy(index_hbm.at[span], index_scr.at[span], sems.at[group])


def start_indices(index):
    for group in range(2):
        index_copy(*index, group).start()


def over_targets(index, targets, one_target):
    def one_group(g, carry):
        @pl.when(g + 2 < targets // TARGET_GROUP)
        def _():
            index_copy(*index, g + 2).start()

        @pl.when(g > 0)
        def _():
            index_copy(*index, g).wait()

        return lax.fori_loop(
            0, TARGET_GROUP, lambda t, c: one_target(g * TARGET_GROUP + t, c), carry
        )

    lax.fori_loop(0, targets // TARGET_GROUP, one_group, 0)


def near_kernel(split, index_hbm, rows_ref, trans_ref, table, factor, acc_ref, index_scr, sems):
    index = (index_hbm, index_scr, sems)
    start_indices(index)
    put_rows(table, rows_ref, 0, rows_ref.shape[0], 0)
    put_all_factors(factor, trans_ref)
    zero = jnp.zeros((8, table.shape[1]), F32)

    def one_target(b, carry):
        total = pair_sums(index_scr, b * 256, split, table, factor, (zero, zero))
        acc_ref[b, :8] = total[0]
        acc_ref[b, 8:] = total[1]
        return carry

    index_copy(*index, 0).wait()
    over_targets(index, acc_ref.shape[0], one_target)


def rest_kernel(dims, first_hbm, second_hbm, table_in, factor, *refs):
    slots, cap_l, cap_p, base, split, list_len, count = dims
    near = slots // 2
    near_own, near_recv = refs[:near], refs[near:slots]
    acc_ref, keep_ref, send_ref, table, index_scr, late_scr, sems, late_sem = refs[slots + 1 :]
    core = lax.axis_index("rhs")
    device = lax.axis_index("space")
    index = (second_hbm, index_scr, sems)
    start_indices(index)
    for k in range(near):
        for values, which in ((near_own[k], core), (near_recv[k], 1 - core)):
            slot = which * near + k
            sender = device - jnp.where(which == 0, k - near, k + 1)
            valid = (sender >= 0) & (sender < count)
            put_rows(table, values, 0, cap_l, base + slot * cap_l, valid)
            put_rows(table, values, cap_l, cap_p, base + slots * cap_l + slot * cap_p, valid)
    zero = jnp.zeros((8, table.shape[1]), F32)

    index_copy(*index, 0).wait()

    @pl.when(index_scr[127] > 0)
    def _():
        def redo(b, carry):
            span = pl.ds(pl.multiple_of(b * 256, 256), 256)
            copy = pltpu.make_async_copy(first_hbm.at[span], late_scr, late_sem)
            copy.start()
            copy.wait()

            @pl.when(late_scr[127] == 0)
            def _():
                total = pair_sums(late_scr, 0, split, table, factor, (zero, zero))
                acc_ref[b, :8] = total[0]
                acc_ref[b, 8:] = total[1]

            return carry

        lax.fori_loop(0, keep_ref.shape[0], redo, 0)

    def one_target(b, carry):
        total = pair_sums(
            index_scr, b * 256, list_len - split, table, factor, (acc_ref[b, :8], acc_ref[b, 8:])
        )
        incoming = jnp.concatenate(total, axis=1)
        lower, upper = incoming[:4], incoming[4:]
        keep_ref[b] = jnp.where(core == 0, lower, upper).astype(BF16)
        send_ref[b] = jnp.where(core == 0, upper, lower).astype(BF16)
        return carry

    over_targets(index, keep_ref.shape[0], one_target)


def local_kernel(leaves, keep_ref, recv_ref, mat_ref, leaf_ref, parent_ref):
    core = lax.axis_index("rhs")
    parents = keep_ref.shape[0] - leaves
    rhs, width = keep_ref.shape[1:]
    for values, which in ((keep_ref, core), (recv_ref, 1 - core)):
        flat = values[...].reshape((leaves + parents) * rhs, width)
        local = jnp.dot(flat, mat_ref[...], preferred_element_type=F32)
        local = local.reshape(leaves + parents, rhs, width)
        leaf_ref[pl.ds(which * leaves, leaves)] = local[:leaves]
        parent_ref[pl.ds(which * parents, parents)] = local[leaves:]


def shards(
    positions, point_counts, charges, frequencies, octants, child_shift, to_wave, to_local,
    translation, send_leaf, send_parent, leaf_pairs, parent_pairs,
):
    other = 1 - lax.axis_index("rhs")
    count = lax.axis_size("space")
    leaves = positions.shape[0] // 2
    parents = leaves // 8
    rhs = charges.shape[1]
    width = to_wave.shape[0]
    slots = send_leaf.shape[1]
    near = slots // 2
    held = leaves + parents
    list_len = leaf_pairs.shape[2]
    split = list_len // 2
    cap_l, cap_p = send_leaf.shape[2], send_parent.shape[2]
    table_rows = 2 * held + slots * (cap_l + cap_p)

    arrived_charges = swap_cores(charges)
    fetched = [
        (jnp.transpose(leaf_pairs, (2, 1, 0)), (list_len, 2, leaves)),
        (parent_pairs, (parents, 2, list_len)),
        (jnp.transpose(positions, (1, 0, 2)), (3, leaves, positions.shape[2])),
        (charges, (leaves,) + charges.shape[1:]),
    ]
    whole = (send_leaf[0], send_parent[0], translation, point_counts, octants, frequencies)
    fetched += [(value, value.shape) for value in whole]
    leaf_half, parent_half, pos_half, own_half, leaf_ids, parent_ids, factors, *early = pl.pallas_call(
        fetch_kernel,
        out_shape=[jax.ShapeDtypeStruct(shape, value.dtype) for value, shape in fetched],
        in_specs=[HBM] * len(fetched),
        out_specs=[VMEM] * len(fetched),
        scratch_shapes=[pltpu.SemaphoreType.DMA((len(fetched),))],
        compiler_params=pltpu.CompilerParams(vmem_limit_bytes=12 << 20),
        name="fetch",
    )(*in_hbm(*(value for value, _ in fetched)))
    waves = pl.pallas_call(
        upward_kernel,
        out_shape=jax.ShapeDtypeStruct((held, 2 * rhs, width), BF16),
        in_specs=[SMEM] * 2 + [VMEM] * 4 + [HBM] * 2,
        out_specs=VMEM,
        scratch_shapes=[
            pltpu.VMEM((3, width // 2, positions.shape[2]), F32),
            pltpu.VMEM((leaves, 2 * rhs, width), BF16),
            pltpu.VMEM((8, parents, 2 * rhs, width), BF16),
            pltpu.VMEM(child_shift.shape, BF16),
            pltpu.VMEM(to_wave.shape, BF16),
            pltpu.SemaphoreType.DMA((2,)),
        ],
        compiler_params=pltpu.CompilerParams(vmem_limit_bytes=12 << 20),
        name="upward",
    )(
        *early, pos_half, own_half, arrived_charges, *in_hbm(child_shift, to_wave)
    )
    arrived_waves = swap_cores(waves)
    waves, leaf_half, parent_half = lax.optimization_barrier((waves, leaf_half, parent_half))
    index_shape = jax.ShapeDtypeStruct((2 * held, 128), jnp.int32)
    first, second = pl.pallas_call(
        functools.partial(plan_kernel, 2 * held, split),
        out_shape=[index_shape] * 2,
        in_specs=[VMEM] * 2,
        out_specs=[VMEM] * 2,
        compiler_params=pltpu.CompilerParams(vmem_limit_bytes=12 << 20),
        name="plan",
    )(leaf_half, parent_half)
    arrived_waves, first, second = lax.optimization_barrier((arrived_waves, first, second))
    first, second = first.reshape(-1), second.reshape(-1)
    rows, *sent = pl.pallas_call(
        pack_kernel,
        out_shape=[jax.ShapeDtypeStruct((2 * held, 2 * rhs, width), BF16)]
        + [jax.ShapeDtypeStruct((cap_l + cap_p, 2 * rhs, width), BF16)] * near,
        in_specs=[SMEM] * 2 + [VMEM] * 2,
        out_specs=[VMEM] * (1 + near),
        compiler_params=pltpu.CompilerParams(vmem_limit_bytes=12 << 20),
        name="pack",
    )(leaf_ids, parent_ids, waves, arrived_waves)
    def slot_permutation(k):
        pairs = []
        for core, offset in ((0, k - near), (1, k + 1)):
            pairs += [(2 * e + core, 2 * ((e + offset) % count) + core) for e in range(count)]
        return pairs

    near_own = [
        lax.ppermute(part, ("space", "rhs"), slot_permutation(k)) for k, part in enumerate(sent)
    ]
    index_scr = pltpu.SMEM((held * 256,), jnp.int32)
    index_sems = pltpu.SemaphoreType.DMA((held // TARGET_GROUP,))
    table_shape = jax.ShapeDtypeStruct((table_rows * 16, width // 2), F32)
    factor_shape = jax.ShapeDtypeStruct((translation.shape[0] * 16, width // 2), F32)
    acc_shape = jax.ShapeDtypeStruct((held, 16, width // 2), F32)
    table, factor, acc = pl.pallas_call(
        functools.partial(near_kernel, split),
        out_shape=[table_shape, factor_shape, acc_shape],
        in_specs=[ANY, VMEM, VMEM],
        out_specs=[VMEM] * 3,
        scratch_shapes=[index_scr, index_sems],
        cost_estimate=pl.CostEstimate(
            flops=20_000_000_000, bytes_accessed=60_000_000, transcendentals=0
        ),
        compiler_params=pltpu.CompilerParams(vmem_limit_bytes=20 << 20),
        name="near",
    )(first, rows, factors)
    *near_own, acc = lax.optimization_barrier((*near_own, acc))
    near_recv = [swap_cores(part) for part in near_own]
    _, keep, send, _ = pl.pallas_call(
        functools.partial(
            rest_kernel, (slots, cap_l, cap_p, 2 * held, split, list_len, count)
        ),
        out_shape=[acc_shape]
        + [jax.ShapeDtypeStruct((held, rhs, width), BF16)] * 2
        + [table_shape],
        in_specs=[ANY] * 2 + [VMEM] * (3 + slots),
        out_specs=[VMEM] * 4,
        scratch_shapes=[
            index_scr,
            pltpu.SMEM((256,), jnp.int32),
            index_sems,
            pltpu.SemaphoreType.DMA,
        ],
        input_output_aliases={2: 3, 4 + slots: 0},
        compiler_params=pltpu.CompilerParams(vmem_limit_bytes=20 << 20),
        name="rest",
    )(first, second, table, factor, *near_own, *near_recv, acc)
    arrived = swap_cores(send)
    return tuple(
        pl.pallas_call(
            functools.partial(local_kernel, leaves),
            out_shape=[
                jax.ShapeDtypeStruct((2 * leaves, rhs, width), F32),
                jax.ShapeDtypeStruct((2 * parents, rhs, width), F32),
            ],
            in_specs=[VMEM] * 3,
            out_specs=[VMEM] * 2,
            compiler_params=pltpu.CompilerParams(vmem_limit_bytes=12 << 20),
        name="local",
        )(keep, arrived, to_local)
    )


def solution(mesh):
    in_specs = (
        P("space", None, None), P("space"), P("space", "rhs", None), P(), P("space"), P(), P(), P(),
        P(), P("space", None, None), P("space", None, None), P("space", None, None),
        P("space", None, None),
    )
    out_specs = (P("space", "rhs", None), P("space", "rhs", None))
    return jax.shard_map(shards, mesh=mesh, in_specs=in_specs, out_specs=out_specs, check_vma=False)
```

```python
import functools
import math

import jax
import jax.numpy as jnp
from jax import lax
from jax.experimental import pallas as pl
from jax.experimental.pallas import tpu as pltpu
from jax.sharding import PartitionSpec as P

F32 = jnp.float32
BF16 = jnp.bfloat16
GROUP = 9
LEAF_UNROLL = 32
TARGET_GROUP = 24
SIN_POLY = (4.44286790342698, -7.307443431653506, 3.594788153158899, -0.7843741906863176)
COS_POLY = (
    1.4142134967586113,
    -6.978850998632011,
    5.7394613208713325,
    -1.883563790130787,
    0.31069962133630835,
)

VMEM = pl.BlockSpec(memory_space=pltpu.VMEM)
SMEM = pl.BlockSpec(memory_space=pltpu.SMEM)
ANY = pl.BlockSpec(memory_space=pl.ANY)
HBM = pl.BlockSpec(memory_space=pltpu.HBM)


def in_hbm(*values):
    return [pltpu.with_memory_space_constraint(value, pltpu.HBM) for value in values]


def swap_cores(value):
    return lax.ppermute(value, "rhs", [(0, 1), (1, 0)])


def horner(coefficients, x):
    total = coefficients[-1] * x + coefficients[-2]
    for coefficient in coefficients[-3::-1]:
        total = total * x + coefficient
    return total


def tree(values):
    values = list(values)
    while len(values) > 1:
        paired = [values[i] + values[i + 1] for i in range(0, len(values) - 1, 2)]
        values = paired + values[2 * len(paired) :]
    return values[0]


def sin_cos_turns(turns):
    r = turns - jnp.round(turns)
    r2 = r * r
    s = r * horner(SIN_POLY, r2)
    c = horner(COS_POLY, r2)
    return s * c, 1.0 - s * s


def upward_kernel(
    counts_ref, octants_ref, freq_ref, pos_ref, own_ref, recv_ref, shift_hbm, wave_mat_hbm,
    out_ref, freq_scr, mult_scr, child_scr, shift_ref, wave_mat_ref, sems,
):
    core = lax.axis_index("rhs")
    leaves, rhs_half, slots = own_ref.shape
    nodes = freq_ref.shape[1]
    base = core * leaves
    copies = [
        pltpu.make_async_copy(wave_mat_hbm, wave_mat_ref, sems.at[0]),
        pltpu.make_async_copy(shift_hbm, shift_ref, sems.at[1]),
    ]
    for copy in copies:
        copy.start()
    for d in range(3):
        row = freq_ref[d : d + 1, :] * (1.0 / (2.0 * math.pi))
        freq_scr[d] = jnp.broadcast_to(row, (slots, nodes)).T
    lane = lax.broadcasted_iota(jnp.int32, (2 * rhs_half, slots), 1)

    def one_leaf(b):
        own, recv = own_ref[b].astype(F32), recv_ref[base + b].astype(F32)
        lower = jnp.where(core == 0, own, recv)
        upper = jnp.where(core == 0, recv, own)
        charge = jnp.concatenate([lower, upper], axis=0)
        charge = jnp.where(lane < counts_ref[base + b], charge, 0.0).astype(BF16)
        xs = [jnp.broadcast_to(pos_ref[d, pl.ds(b, 1), :], (nodes, slots)) for d in range(3)]
        turns = freq_scr[0] * xs[0] + freq_scr[1] * xs[1] + freq_scr[2] * xs[2]
        sin, cos = sin_cos_turns(turns)
        basis = jnp.concatenate([cos.astype(BF16), sin.astype(BF16)], axis=0)
        multipole = lax.dot_general(
            charge, basis, (((1,), (1,)), ((), ())), preferred_element_type=F32
        ).astype(BF16)
        mult_scr[b] = multipole
        child_scr[octants_ref[base + b], b // 8] = multipole

    def step(g, carry):
        for k in range(LEAF_UNROLL):
            one_leaf(g * LEAF_UNROLL + k)
        return carry

    lax.fori_loop(0, leaves // LEAF_UNROLL, step, 0)
    for copy in copies:
        copy.wait()
    parents = leaves // 8
    rhs, width = mult_scr.shape[1:]
    wave_mat = wave_mat_ref[...]
    multipoles = mult_scr[...].reshape(leaves * rhs, width)
    waves = jnp.dot(multipoles, wave_mat, preferred_element_type=F32).astype(BF16)
    out_ref[:leaves] = waves.reshape(leaves, rhs, width)
    summed = None
    for octant in range(8):
        part = jnp.dot(
            child_scr[octant].reshape(parents * rhs, width),
            shift_ref[octant],
            preferred_element_type=F32,
        )
        summed = part if summed is None else summed + part
    parent_waves = jnp.dot(summed.astype(BF16), wave_mat, preferred_element_type=F32)
    out_ref[leaves:] = parent_waves.astype(BF16).reshape(parents, rhs, width)


def fetch_kernel(*refs):
    count = (len(refs) - 1) // 2
    sources, targets, sems = refs[:count], refs[count:-1], refs[-1]
    core = lax.axis_index("rhs")
    leaves, parents = targets[0].shape[2], targets[1].shape[0]
    half = pl.ds(pl.multiple_of(core * leaves, leaves), leaves)
    views = [
        sources[0].at[:, :, half],
        sources[1].at[pl.ds(core * parents, parents)],
        sources[2].at[:, half, :],
        sources[3].at[half],
        *sources[4:],
    ]
    copies = [
        pltpu.make_async_copy(view, target, sems.at[i])
        for i, (view, target) in enumerate(zip(views, targets))
    ]
    for copy in copies:
        copy.start()
    for copy in copies:
        copy.wait()


def plan_kernel(local_rows, split, leaf_ref, parent_ref, first_out, second_out):
    list_len, _, leaves = leaf_ref.shape
    parents = parent_ref.shape[0]
    targets = leaves + parents
    depth = -(-list_len // 8) * 8

    def packed(source, shift):
        return source + shift * (1 << 10)

    leaf_words = packed(leaf_ref[:, 0, :], leaf_ref[:, 1, :])
    parent_words = packed(parent_ref[:, 0, :], parent_ref[:, 1, :])
    parent_words = jnp.concatenate(
        [parent_words, jnp.zeros((parents, 256 - list_len), jnp.int32)], axis=1
    )
    parent_words = jnp.concatenate(
        [parent_words, jnp.zeros((128 - parents, 256), jnp.int32)], axis=0
    ).T[:depth]
    leaf_words = jnp.concatenate(
        [leaf_words, jnp.zeros((depth - list_len, leaves), jnp.int32)], axis=0
    )
    words = jnp.concatenate([leaf_words, parent_words], axis=1)
    row = lax.broadcasted_iota(jnp.int32, words.shape, 0)
    local = ((words & 1023) < local_rows) & (row < list_len)
    below = lax.broadcasted_iota(jnp.int32, (depth, depth), 0) >= lax.broadcasted_iota(
        jnp.int32, (depth, depth), 1
    )
    running = jnp.dot(
        jnp.where(below, 1.0, 0.0).astype(BF16),
        jnp.where(local, 1.0, 0.0).astype(BF16),
        preferred_element_type=F32,
    ).astype(jnp.int32)
    total = running[depth - 1 :]
    front = jnp.where(local, words + (row + 1 - running) * (1 << 20), 0)
    back = jnp.where(local, 0, words + (total - running) * (1 << 20))
    for k in range(8):
        bit = 1 << (20 + k)
        step = 1 << k
        moved = pltpu.roll(front, depth - step, 0)
        front = jnp.where((moved & bit) != 0, moved, jnp.where((front & bit) != 0, 0, front))
        moved = pltpu.roll(back, step, 0)
        back = jnp.where((moved & bit) != 0, moved, jnp.where((back & bit) != 0, 0, back))
    words = front + back
    sources = (words & 1023) * 16
    classes = (lax.shift_right_logical(words, 10) & 1023) * 16
    ready = (total >= split).astype(jnp.int32)
    lane = lax.broadcasted_iota(jnp.int32, ready.shape, 1)
    late = jnp.max(jnp.where(lane < targets, 1 - ready, 0), axis=1, keepdims=True)
    for h, values in enumerate((sources, classes)):
        head = jnp.where(row[:128] == 127, ready, values[:128])
        tail = jnp.where(row[:128] == 127, late, pltpu.roll(values, depth - split, 0)[:128])
        first_out[pl.ds(h, targets, stride=2), :] = head.T[:targets]
        second_out[pl.ds(h, targets, stride=2), :] = tail.T[:targets]


def pack_kernel(leaf_ids_ref, parent_ids_ref, own_ref, recv_ref, *refs):
    core = lax.axis_index("rhs")
    rows_ref, outs = refs[0], refs[1:]
    cap_l, cap_p = leaf_ids_ref.shape[1], parent_ids_ref.shape[1]
    parents = rows_ref.shape[0] // 18
    leaves = 8 * parents
    for values, which in ((own_ref, core), (recv_ref, 1 - core)):
        rows_ref[pl.ds(which * leaves, leaves)] = values[:leaves]
        rows_ref[pl.ds(2 * leaves + which * parents, parents)] = values[leaves:]
    for j, out in enumerate(outs):
        slot = core * len(outs) + j
        for k in range(cap_l):
            out[k] = rows_ref[leaf_ids_ref[slot, k]]
        for k in range(cap_p):
            out[cap_l + k] = rows_ref[2 * leaves + parent_ids_ref[slot, k]]


def put_rows(table, source, at, count, base, valid=None):
    half = table.shape[1]

    def body(k, carry):
        value = source[at + k].astype(F32)
        if valid is not None:
            value = jnp.where(valid, value, 0.0)
        row = pl.multiple_of((base + k) * 16, 16)
        table[pl.ds(row, 8), :] = value[:, :half]
        table[pl.ds(pl.multiple_of(row + 8, 8), 8), :] = value[:, half:]
        return carry

    lax.fori_loop(0, count, body, 0, unroll=8)


def put_all_factors(factor, trans_ref):
    half = factor.shape[1]

    def put_factors(first, values):
        for k in range(values.shape[0]):
            row = pl.multiple_of((first + k) * 16, 16)
            factor[pl.ds(row, 8), :] = jnp.broadcast_to(values[k : k + 1, :half], (8, half))
            factor[pl.ds(pl.multiple_of(row + 8, 8), 8), :] = jnp.broadcast_to(
                values[k : k + 1, half:], (8, half)
            )

    def factor_block(g, carry):
        first = pl.multiple_of(g * 8, 8)
        put_factors(first, trans_ref[pl.ds(first, 8), :])
        return carry

    full = trans_ref.shape[0] // 8 * 8
    lax.fori_loop(0, full // 8, factor_block, 0)
    if full < trans_ref.shape[0]:
        put_factors(full, trans_ref[full:, :])


def pair_sums(index_ref, first, count, table, factor, total):
    total_re, total_im = total
    reals, imags = [], []
    for k in range(count):
        if k % GROUP == 0:
            span = min(GROUP, count - k)
            sources = index_ref.at[pl.ds(first + k, span)]
            classes = index_ref.at[pl.ds(first + 128 + k, span)]
        s = pl.multiple_of(sources[k % GROUP], 8)
        o = pl.multiple_of(classes[k % GROUP], 8)
        wave, shift = table.at[pl.ds(s, 16)], factor.at[pl.ds(o, 16)]
        wave_re, wave_im, shift_re, shift_im = wave[:8], wave[8:], shift[:8], shift[8:]
        reals.append(shift_re * wave_re - shift_im * wave_im)
        imags.append(shift_re * wave_im + shift_im * wave_re)
        if len(reals) == 1 or k == count - 1:
            total_re, total_im = total_re + tree(reals), total_im + tree(imags)
            reals, imags = [], []
    return total_re, total_im


def index_copy(index_hbm, index_scr, sems, group):
    words = TARGET_GROUP * 256
    span = pl.ds(pl.multiple_of(group * words, 1024), words)
    return pltpu.make_async_copy(index_hbm.at[span], index_scr.at[span], sems.at[group])


def start_indices(index):
    for group in range(2):
        index_copy(*index, group).start()


def over_targets(index, targets, one_target):
    def one_group(g, carry):
        @pl.when(g + 2 < targets // TARGET_GROUP)
        def _():
            index_copy(*index, g + 2).start()

        @pl.when(g > 0)
        def _():
            index_copy(*index, g).wait()

        return lax.fori_loop(
            0, TARGET_GROUP, lambda t, c: one_target(g * TARGET_GROUP + t, c), carry
        )

    lax.fori_loop(0, targets // TARGET_GROUP, one_group, 0)


def near_kernel(split, index_hbm, rows_ref, trans_ref, table, factor, acc_ref, index_scr, sems):
    index = (index_hbm, index_scr, sems)
    start_indices(index)
    put_rows(table, rows_ref, 0, rows_ref.shape[0], 0)
    put_all_factors(factor, trans_ref)
    zero = jnp.zeros((8, table.shape[1]), F32)

    def one_target(b, carry):
        total = pair_sums(index_scr, b * 256, split, table, factor, (zero, zero))
        acc_ref[b, :8] = total[0]
        acc_ref[b, 8:] = total[1]
        return carry

    index_copy(*index, 0).wait()
    over_targets(index, acc_ref.shape[0], one_target)


def rest_kernel(dims, first_hbm, second_hbm, table_in, factor, *refs):
    slots, cap_l, cap_p, base, split, list_len, count = dims
    near = slots // 2
    near_own, near_recv = refs[:near], refs[near:slots]
    acc_ref, keep_ref, send_ref, table, index_scr, late_scr, sems, late_sem = refs[slots + 1 :]
    core = lax.axis_index("rhs")
    device = lax.axis_index("space")
    index = (second_hbm, index_scr, sems)
    start_indices(index)
    for k in range(near):
        for values, which in ((near_own[k], core), (near_recv[k], 1 - core)):
            slot = which * near + k
            sender = device - jnp.where(which == 0, k - near, k + 1)
            valid = (sender >= 0) & (sender < count)
            put_rows(table, values, 0, cap_l, base + slot * cap_l, valid)
            put_rows(table, values, cap_l, cap_p, base + slots * cap_l + slot * cap_p, valid)
    zero = jnp.zeros((8, table.shape[1]), F32)

    index_copy(*index, 0).wait()

    @pl.when(index_scr[127] > 0)
    def _():
        def redo(b, carry):
            span = pl.ds(pl.multiple_of(b * 256, 256), 256)
            copy = pltpu.make_async_copy(first_hbm.at[span], late_scr, late_sem)
            copy.start()
            copy.wait()

            @pl.when(late_scr[127] == 0)
            def _():
                total = pair_sums(late_scr, 0, split, table, factor, (zero, zero))
                acc_ref[b, :8] = total[0]
                acc_ref[b, 8:] = total[1]

            return carry

        lax.fori_loop(0, keep_ref.shape[0], redo, 0)

    def one_target(b, carry):
        total = pair_sums(
            index_scr, b * 256, list_len - split, table, factor, (acc_ref[b, :8], acc_ref[b, 8:])
        )
        incoming = jnp.concatenate(total, axis=1)
        lower, upper = incoming[:4], incoming[4:]
        keep_ref[b] = jnp.where(core == 0, lower, upper).astype(BF16)
        send_ref[b] = jnp.where(core == 0, upper, lower).astype(BF16)
        return carry

    over_targets(index, keep_ref.shape[0], one_target)


def local_kernel(leaves, keep_ref, recv_ref, mat_ref, leaf_ref, parent_ref):
    core = lax.axis_index("rhs")
    parents = keep_ref.shape[0] - leaves
    rhs, width = keep_ref.shape[1:]
    for values, which in ((keep_ref, core), (recv_ref, 1 - core)):
        flat = values[...].reshape((leaves + parents) * rhs, width)
        local = jnp.dot(flat, mat_ref[...], preferred_element_type=F32)
        local = local.reshape(leaves + parents, rhs, width)
        leaf_ref[pl.ds(which * leaves, leaves)] = local[:leaves]
        parent_ref[pl.ds(which * parents, parents)] = local[leaves:]


def shards(
    positions, point_counts, charges, frequencies, octants, child_shift, to_wave, to_local,
    translation, send_leaf, send_parent, leaf_pairs, parent_pairs,
):
    other = 1 - lax.axis_index("rhs")
    count = lax.axis_size("space")
    leaves = positions.shape[0] // 2
    parents = leaves // 8
    rhs = charges.shape[1]
    width = to_wave.shape[0]
    slots = send_leaf.shape[1]
    near = slots // 2
    held = leaves + parents
    list_len = leaf_pairs.shape[2]
    split = list_len // 2
    cap_l, cap_p = send_leaf.shape[2], send_parent.shape[2]
    table_rows = 2 * held + slots * (cap_l + cap_p)

    arrived_charges = swap_cores(charges)
    fetched = [
        (jnp.transpose(leaf_pairs, (2, 1, 0)), (list_len, 2, leaves)),
        (parent_pairs, (parents, 2, list_len)),
        (jnp.transpose(positions, (1, 0, 2)), (3, leaves, positions.shape[2])),
        (charges, (leaves,) + charges.shape[1:]),
    ]
    whole = (send_leaf[0], send_parent[0], translation, point_counts, octants, frequencies)
    fetched += [(value, value.shape) for value in whole]
    leaf_half, parent_half, pos_half, own_half, leaf_ids, parent_ids, factors, *early = pl.pallas_call(
        fetch_kernel,
        out_shape=[jax.ShapeDtypeStruct(shape, value.dtype) for value, shape in fetched],
        in_specs=[HBM] * len(fetched),
        out_specs=[VMEM] * len(fetched),
        scratch_shapes=[pltpu.SemaphoreType.DMA((len(fetched),))],
        compiler_params=pltpu.CompilerParams(vmem_limit_bytes=12 << 20),
        name="fetch",
    )(*in_hbm(*(value for value, _ in fetched)))
    waves = pl.pallas_call(
        upward_kernel,
        out_shape=jax.ShapeDtypeStruct((held, 2 * rhs, width), BF16),
        in_specs=[SMEM] * 2 + [VMEM] * 4 + [HBM] * 2,
        out_specs=VMEM,
        scratch_shapes=[
            pltpu.VMEM((3, width // 2, positions.shape[2]), F32),
            pltpu.VMEM((leaves, 2 * rhs, width), BF16),
            pltpu.VMEM((8, parents, 2 * rhs, width), BF16),
            pltpu.VMEM(child_shift.shape, BF16),
            pltpu.VMEM(to_wave.shape, BF16),
            pltpu.SemaphoreType.DMA((2,)),
        ],
        compiler_params=pltpu.CompilerParams(vmem_limit_bytes=12 << 20),
        name="upward",
    )(
        *early, pos_half, own_half, arrived_charges, *in_hbm(child_shift, to_wave)
    )
    arrived_waves = swap_cores(waves)
    waves, leaf_half, parent_half = lax.optimization_barrier((waves, leaf_half, parent_half))
    index_shape = jax.ShapeDtypeStruct((2 * held, 128), jnp.int32)
    first, second = pl.pallas_call(
        functools.partial(plan_kernel, 2 * held, split),
        out_shape=[index_shape] * 2,
        in_specs=[VMEM] * 2,
        out_specs=[VMEM] * 2,
        compiler_params=pltpu.CompilerParams(vmem_limit_bytes=12 << 20),
        name="plan",
    )(leaf_half, parent_half)
    arrived_waves, first, second = lax.optimization_barrier((arrived_waves, first, second))
    first, second = first.reshape(-1), second.reshape(-1)
    rows, *sent = pl.pallas_call(
        pack_kernel,
        out_shape=[jax.ShapeDtypeStruct((2 * held, 2 * rhs, width), BF16)]
        + [jax.ShapeDtypeStruct((cap_l + cap_p, 2 * rhs, width), BF16)] * near,
        in_specs=[SMEM] * 2 + [VMEM] * 2,
        out_specs=[VMEM] * (1 + near),
        compiler_params=pltpu.CompilerParams(vmem_limit_bytes=12 << 20),
        name="pack",
    )(leaf_ids, parent_ids, waves, arrived_waves)
    def slot_permutation(k):
        pairs = []
        for core, offset in ((0, k - near), (1, k + 1)):
            pairs += [(2 * e + core, 2 * ((e + offset) % count) + core) for e in range(count)]
        return pairs

    near_own = [
        lax.ppermute(part, ("space", "rhs"), slot_permutation(k)) for k, part in enumerate(sent)
    ]
    index_scr = pltpu.SMEM((held * 256,), jnp.int32)
    index_sems = pltpu.SemaphoreType.DMA((held // TARGET_GROUP,))
    table_shape = jax.ShapeDtypeStruct((table_rows * 16, width // 2), F32)
    factor_shape = jax.ShapeDtypeStruct((translation.shape[0] * 16, width // 2), F32)
    acc_shape = jax.ShapeDtypeStruct((held, 16, width // 2), F32)
    table, factor, acc = pl.pallas_call(
        functools.partial(near_kernel, split),
        out_shape=[table_shape, factor_shape, acc_shape],
        in_specs=[ANY, VMEM, VMEM],
        out_specs=[VMEM] * 3,
        scratch_shapes=[index_scr, index_sems],
        cost_estimate=pl.CostEstimate(
            flops=20_000_000_000, bytes_accessed=60_000_000, transcendentals=0
        ),
        compiler_params=pltpu.CompilerParams(vmem_limit_bytes=20 << 20),
        name="near",
    )(first, rows, factors)
    *near_own, acc = lax.optimization_barrier((*near_own, acc))
    near_recv = [swap_cores(part) for part in near_own]
    _, keep, send, _ = pl.pallas_call(
        functools.partial(
            rest_kernel, (slots, cap_l, cap_p, 2 * held, split, list_len, count)
        ),
        out_shape=[acc_shape]
        + [jax.ShapeDtypeStruct((held, rhs, width), BF16)] * 2
        + [table_shape],
        in_specs=[ANY] * 2 + [VMEM] * (3 + slots),
        out_specs=[VMEM] * 4,
        scratch_shapes=[
            index_scr,
            pltpu.SMEM((256,), jnp.int32),
            index_sems,
            pltpu.SemaphoreType.DMA,
        ],
        input_output_aliases={2: 3, 4 + slots: 0},
        compiler_params=pltpu.CompilerParams(vmem_limit_bytes=20 << 20),
        name="rest",
    )(first, second, table, factor, *near_own, *near_recv, acc)
    arrived = swap_cores(send)
    return tuple(
        pl.pallas_call(
            functools.partial(local_kernel, leaves),
            out_shape=[
                jax.ShapeDtypeStruct((2 * leaves, rhs, width), F32),
                jax.ShapeDtypeStruct((2 * parents, rhs, width), F32),
            ],
            in_specs=[VMEM] * 3,
            out_specs=[VMEM] * 2,
            compiler_params=pltpu.CompilerParams(vmem_limit_bytes=12 << 20),
        name="local",
        )(keep, arrived, to_local)
    )


def solution(mesh):
    in_specs = (
        P("space", None, None), P("space"), P("space", "rhs", None), P(), P("space"), P(), P(), P(),
        P(), P("space", None, None), P("space", None, None), P("space", None, None),
        P("space", None, None),
    )
    out_specs = (P("space", "rhs", None), P("space", "rhs", None))
    return jax.shard_map(shards, mesh=mesh, in_specs=in_specs, out_specs=out_specs, check_vma=False)
```
